128 devices in a mesh: defocus: 8 (over x_lo, y), blk: 16 (over z, x_hi, core).
Axes of the slice: x: 4 (x_hi: 2, x_lo: 2; x = x_hi * 2 + x_lo), y: 4, z: 4, core: 2. Of those that a mesh axis runs over, the one named last changes fastest.
Arguments:
- images: bfloat16 [8, 16, 384, 384], P('defocus', 'blk'), may hold values from -6 to 6
- projections: bfloat16 [16, 384, 384], P('blk', 'defocus'), may hold values from -6 to 6
- ctf_row: int32 [8, 16], P('defocus', 'blk'), may hold values from 0 to 63
- defocus_term: float32 [64], replicated, may hold values from 100 to 400
- astig_term: float32 [64], replicated, may hold values from -40 to 40
- astig_cross: float32 [64], replicated, may hold values from -40 to 40
- phase_shift: float32 [64], replicated, may hold values from 0.1 to 1.5
Outputs:
- peak: float32 [8, 16, 384, 384], P('defocus', 'blk')
The draws below stay inside these ranges and needn't reach their ends.
All inputs are finite; a program needn't handle non-finite values.
Results may differ from the reference program's by a relative error of at most 0.0095.
Values may be sent and summed in bfloat16 or wider, within the bound.
No kernel may reach another device: no remote copies, remote signals or barrier semaphores. Data moves between devices by JAX's collectives and lax.ppermute only.
A program may use at most 64 MiB of HBM per device.

```python
import math
import jax
import jax.numpy as jnp
from jax import lax

PIXELS = 384
PARAM_ROWS = 64
DEFOCUS_GROUPS = 8
GROUP_TILES = 16
LIBRARY = 16


def set_ends(array, stream_key, smallest, top_value):
    longest = array.shape.index(max(array.shape))
    spots = []
    for shift in (0, 1):
        where = [jax.random.randint(jax.random.fold_in(stream_key, axis), (), 0, length) for axis, length in enumerate(array.shape)]
        where[longest] = (where[longest] + shift) % array.shape[longest]
        spots.append(tuple(where))
    return array.at[spots[0]].set(smallest).at[spots[1]].set(top_value)


def levels(key, shape, split, smallest, largest):
    factor_of = 1.0
    for axis_at, blocks in split:
        heights = jax.random.uniform(jax.random.fold_in(jax.random.fold_in(key, 6), axis_at), (blocks,), jnp.float32, smallest / len(split), largest / len(split))
        factor_of = factor_of * jnp.repeat(jnp.exp(heights), shape[axis_at] // blocks).reshape((-1,) + (1,) * (len(shape) - 1 - axis_at))
    return factor_of


def scatter_about(stream_key, extent, deviation, reach, shards=(), kind=jnp.bfloat16):
    values = jax.random.normal(stream_key, extent, jnp.float32) * deviation
    if len(shards) > 0:
        values = levels(stream_key, extent, shards, -0.22, 0.18) * values
    return jnp.clip(values, min=-reach, max=reach).astype(kind)


def setup_inputs(seed: int = 0) -> dict:
    streams_of = jax.random.split(jax.random.key(seed), 8)
    return {
        "images": scatter_about(streams_of[0], (DEFOCUS_GROUPS, GROUP_TILES, PIXELS, PIXELS), 1.0, 6.0, ((0, 8), (1, 16))),
        "projections": scatter_about(streams_of[1], (LIBRARY, PIXELS, PIXELS), 1.0, 6.0, ((0, 16), (1, 8))),
        "ctf_row": set_ends(jax.random.randint(streams_of[2], (DEFOCUS_GROUPS, GROUP_TILES), 0, PARAM_ROWS), jax.random.fold_in(streams_of[2], 1), 0, PARAM_ROWS - 1).astype(jnp.int32),
        "defocus_term": jnp.clip(jnp.exp(jax.random.uniform(streams_of[3], (PARAM_ROWS,), jnp.float32, math.log(100.0), math.log(400.0))), 100.0, 400.0),
        "astig_term": jnp.clip(jax.random.uniform(streams_of[4], (PARAM_ROWS,), jnp.float32, -40.0, 40.0), -40.0, 40.0),
        "astig_cross": jnp.clip(jax.random.uniform(streams_of[5], (PARAM_ROWS,), jnp.float32, -40.0, 40.0), -40.0, 40.0),
        "phase_shift": jnp.clip(jax.random.uniform(streams_of[6], (PARAM_ROWS,), jnp.float32, 0.1, 1.5), 0.1, 1.5),
    }


def make_tables(pixels):
    indices = jnp.arange(pixels, dtype=jnp.int32)
    phases = indices[:, None] * indices[None, :] % pixels
    angles = phases.astype(jnp.float32) * (2.0 * math.pi / pixels)
    return (jnp.cos(angles).astype(jnp.bfloat16), jnp.sin(angles).astype(jnp.bfloat16))

def batch_right(template_stack, lookup_table):
    return jnp.einsum('xgs,so->xgo', template_stack.astype(jnp.float32), lookup_table.astype(jnp.float32))

def batch_left(lookup_table, template_stack):
    return jnp.einsum('ua,tab->tub', lookup_table.astype(jnp.float32), template_stack.astype(jnp.float32))

def forward_sections(template_stack, cosine_table, sine_table):
    part_re = batch_right(template_stack, cosine_table).astype(jnp.bfloat16)
    part_im = (-batch_right(template_stack, sine_table)).astype(jnp.bfloat16)
    spectrum_re = batch_left(cosine_table, part_re) + batch_left(sine_table, part_im)
    spectrum_im = batch_left(cosine_table, part_im) - batch_left(sine_table, part_re)
    return (spectrum_re, spectrum_im)

def reference(images, projections, ctf_row, defocus_term, astig_term, astig_cross, phase_shift):
    pixels = images.shape[-1]
    groups = images.shape[0]
    group_tiles = images.shape[1]
    cosine_table, sine_table = make_tables(pixels)
    flat_images = images.reshape(groups * group_tiles, pixels, pixels)
    spectrum_re, spectrum_im = forward_sections(flat_images, cosine_table, sine_table)
    powers = (spectrum_re * spectrum_re + spectrum_im * spectrum_im).reshape(groups, group_tiles, pixels, pixels)
    mean_power = lax.optimization_barrier(jnp.mean(powers, axis=1))
    noise_group = mean_power + 0.05 * lax.optimization_barrier(jnp.mean(mean_power, axis=(1, 2), keepdims=True))
    noise_power = jnp.repeat(noise_group, group_tiles, axis=0)
    indices = jnp.arange(pixels, dtype=jnp.int32)
    signed = jnp.where(indices < pixels // 2, indices, indices - pixels)
    frequency = signed.astype(jnp.float32) / pixels
    row_freq = frequency[:, None]
    col_freq = frequency[None, :]
    radial = row_freq * row_freq + col_freq * col_freq
    stretch = row_freq * row_freq - col_freq * col_freq
    skewed = 2.0 * row_freq * col_freq
    row_ids = ctf_row.reshape(-1).astype(jnp.int32)
    chi_angle = defocus_term[row_ids][:, None, None] * radial + astig_term[row_ids][:, None, None] * stretch + astig_cross[row_ids][:, None, None] * skewed + phase_shift[row_ids][:, None, None]
    transfer_gain = -jnp.sin(chi_angle)
    factor = transfer_gain / noise_power
    ctf_weight = transfer_gain * factor
    template_re, template_im = forward_sections(projections, cosine_table, sine_table)
    template_re, template_im = lax.optimization_barrier((template_re.astype(jnp.bfloat16), template_im.astype(jnp.bfloat16)))

    def one_plane(running, planes):
        plane_re = planes[0].astype(jnp.float32)
        plane_im = planes[1].astype(jnp.float32)
        template_norm = lax.optimization_barrier(jnp.sum((plane_re * plane_re + plane_im * plane_im)[None] * ctf_weight, axis=(1, 2)))
        scaling = factor / jnp.sqrt(template_norm + 1e-06)[:, None, None]
        product_re = ((spectrum_re * plane_re + spectrum_im * plane_im) * scaling).astype(jnp.bfloat16)
        product_im = ((spectrum_im * plane_re - spectrum_re * plane_im) * scaling).astype(jnp.bfloat16)
        half_re = (batch_right(product_re, cosine_table) - batch_right(product_im, sine_table)).astype(jnp.bfloat16)
        half_im = (batch_right(product_re, sine_table) + batch_right(product_im, cosine_table)).astype(jnp.bfloat16)
        scores = batch_left(cosine_table, half_re) - batch_left(sine_table, half_im)
        return (jnp.maximum(running, scores), None)
    initial = jnp.full(flat_images.shape, -jnp.inf, jnp.float32)
    maxima, _ = lax.scan(one_plane, initial, (template_re, template_im))
    return maxima.reshape(groups, group_tiles, pixels, pixels)
```

```python
import math

import jax
import jax.numpy as jnp
import ml_dtypes
import numpy as np
from jax import lax
from jax.experimental import pallas as pl
from jax.experimental.pallas import tpu as pltpu
from jax.sharding import Mesh
from jax.sharding import PartitionSpec as P

DEF = ("xlo", "y")
BLK = ("z", "xhi", "core")
CHIPS = ("xlo", "y", "z", "xhi")
N = 384
HALF = N // 2
ROWS = 208
PART = ROWS // 2
F32 = jnp.float32
BF16 = jnp.bfloat16


def tables():
    j = np.arange(N)
    phase = (j[:, None] * j[None, :]) % N
    cos = np.cos(2.0 * np.pi * phase / N)
    sin = np.sin(2.0 * np.pi * phase / N)
    bf = ml_dtypes.bfloat16
    first = np.zeros((2 * ROWS, N))
    first[: HALF + 1] = cos[: HALF + 1]
    first[ROWS : ROWS + HALF + 1] = -sin[: HALF + 1]
    forward = np.block([[cos, -sin], [sin, cos]])
    inverse = np.block([[cos, sin], [-sin, cos]])
    weight = np.full(HALF + 1, 2.0)
    weight[0] = weight[HALF] = 1.0
    fold = np.zeros((2, ROWS, ROWS))
    fold[0, : HALF + 1, : HALF + 1] = cos[: HALF + 1, : HALF + 1].astype(bf).astype(float) * weight
    fold[1, : HALF + 1, : HALF + 1] = sin[: HALF + 1, : HALF + 1].astype(bf).astype(float) * weight
    unfold = np.zeros((HALF, 2 * ROWS))
    unfold[0, HALF] = 1.0
    for i in range(1, HALF):
        unfold[i, ROWS + HALF - i] = 1.0
    return [a.astype(bf) for a in (first, forward, inverse, fold, unfold)]


def dot(a, b):
    return jnp.dot(a, b, preferred_element_type=F32)


def half_spectrum(image, first, forward):
    part = dot(first, image).astype(BF16)
    both = jnp.concatenate([part[:ROWS], part[ROWS:]], axis=1)
    out = dot(both, forward)
    return out[:, :N], out[:, N:]


def tile_kernel(core_ref, own_ref, other_ref, first_ref, forward_ref, spec_ref, power_ref, total_ref):
    for t, ref in enumerate((own_ref, other_ref)):
        re, im = half_spectrum(ref[...], first_ref[...], forward_ref[...])
        spec_ref[t, 0] = re
        spec_ref[t, 1] = im
        square = re * re + im * im
        total_ref[...] = square if t == 0 else total_ref[...] + square
    start = pl.multiple_of(core_ref[0] * PART, 8)
    power_ref[...] = total_ref[pl.ds(start, PART), :].astype(BF16)


def sine(x):
    x = x - jnp.round(x)
    a = jnp.abs(x)
    a = jnp.minimum(a, 0.5 - a)
    s = a * a
    p = jnp.full_like(x, -15.0946425768229800)
    for c in (
        42.0586939448600400,
        -76.7058597530613900,
        81.6052492760750400,
        -41.3417022403997600,
        6.28318530717958648,
    ):
        p = p * s + c
    p = p * a
    return jnp.where(x < 0.0, -p, p)


def gain_kernel(row_ref, mark_ref, d_ref, a_ref, x_ref, p_ref, gain_ref, weight_ref):
    other = jnp.max(mark_ref[...].astype(F32)).astype(jnp.int32)
    u = lax.broadcasted_iota(jnp.int32, (ROWS, N), 0)
    v = lax.broadcasted_iota(jnp.int32, (ROWS, N), 1)
    row = jnp.where(u < HALF, u, u - N).astype(F32) * (1.0 / N)
    col = jnp.where(v < HALF, v, v - N).astype(F32) * (1.0 / N)
    radial = row * row + col * col
    stretch = row * row - col * col
    skew = 2.0 * row * col
    inner = (u > 0) & (u < HALF)
    scale = jnp.where(inner, 2.0, jnp.where(u <= HALF, 1.0, 0.0))
    turn = 1.0 / (2.0 * math.pi)
    for t, r in enumerate((row_ref[0, 0], other)):
        base = (d_ref[r] * turn) * radial + (a_ref[r] * turn) * stretch + p_ref[r] * turn
        cross = (x_ref[r] * turn) * skew
        plus = -sine(base + cross)
        minus = -sine(base - cross)
        mirror = jnp.where(inner & (v == HALF), minus, plus)
        gain_ref[t] = 0.5 * (plus + mirror)
        weight_ref[t] = (0.5 * scale) * (plus * plus + mirror * mirror)


def match_kernel(
    image_ref,
    spec_ref,
    low_ref,
    high_ref,
    gain_ref,
    weight_ref,
    first_ref,
    forward_ref,
    inverse_ref,
    fold_ref,
    best_ref,
    give_ref,
    spec_sc,
    weight_sc,
    best_sc,
):
    step = pl.program_id(0)

    @pl.when(step == 0)
    def _():
        power = jnp.concatenate([low_ref[...], high_ref[...]], axis=0).astype(F32) * (1.0 / 16.0)
        u = lax.broadcasted_iota(jnp.int32, (ROWS, N), 0)
        scale = jnp.where((u > 0) & (u < HALF), 2.0, jnp.where(u <= HALF, 1.0, 0.0))
        mean = jnp.sum(power * scale) * (1.0 / (N * N))
        inverse_noise = 1.0 / (jnp.where(u <= HALF, power, 1.0) + 0.05 * mean)
        for t in range(2):
            factor = gain_ref[t] * inverse_noise
            spec_sc[t, 0] = spec_ref[t, 0] * factor
            spec_sc[t, 1] = spec_ref[t, 1] * factor
            weight_sc[t] = weight_ref[t] * inverse_noise
        best_sc[...] = jnp.full_like(best_sc, -jnp.inf)

    image = image_ref[...].reshape(N, N)
    re, im = half_spectrum(image, first_ref[...], forward_ref[...])
    re = re.astype(BF16).astype(F32)
    im = im.astype(BF16).astype(F32)
    square = re * re + im * im
    for t in range(2):
        norm = jnp.sum(square * weight_sc[t])
        scale = lax.rsqrt(jnp.full((1, 2 * N), norm + 1e-06, F32))
        s_re, s_im = spec_sc[t, 0], spec_sc[t, 1]
        both = jnp.concatenate(
            [
                (s_re * re + s_im * im).astype(BF16),
                (s_im * re - s_re * im).astype(BF16),
            ],
            axis=1,
        )
        half = (dot(both, inverse_ref[...]) * scale).astype(BF16)
        even = dot(fold_ref[0], half[:, :N])
        odd = dot(fold_ref[1], half[:, N:])
        best_sc[t, 0] = jnp.maximum(best_sc[t, 0], even - odd)
        best_sc[t, 1] = jnp.maximum(best_sc[t, 1], even + odd)

    @pl.when(step == pl.num_programs(0) - 1)
    def _():
        best_ref[...] = best_sc[0]
        give_ref[...] = best_sc[1].astype(BF16)


def join_kernel(best_ref, got_ref, unfold_ref, out_ref):
    best = jnp.maximum(best_ref[...], got_ref[...].astype(F32))
    out_ref[:HALF] = best[0, :HALF]
    rest = best.reshape(2 * ROWS, N)
    total = None
    for _ in range(3):
        part = rest.astype(BF16)
        rest = rest - part.astype(F32)
        moved = dot(unfold_ref[...], part)
        total = moved if total is None else total + moved
    out_ref[HALF:] = total


def vmem(count):
    return [pl.BlockSpec(memory_space=pltpu.VMEM)] * count


def smem(count):
    return [pl.BlockSpec(memory_space=pltpu.SMEM)] * count


def cost(flops, size):
    return pl.CostEstimate(flops=flops, bytes_accessed=size, transcendentals=0)


def per_device(images, projections, ctf_row, defocus_term, astig_term, astig_cross, phase_shift):
    first, forward, inverse, fold, unfold = (jnp.asarray(a) for a in tables())
    chips = math.prod(lax.axis_size(a) for a in CHIPS)
    groups = math.prod(lax.axis_size(a) for a in DEF)
    planes = chips // groups
    core = lax.axis_index("core")
    swap = [(0, 1), (1, 0)]

    block = projections[0]
    library = lax.all_to_all(
        jnp.broadcast_to(block[None], (chips,) + block.shape), CHIPS, 0, 0, tiled=False
    )

    tile = images[0, 0]
    mark = jnp.broadcast_to(ctf_row.astype(BF16), (16, N))
    sent = jnp.concatenate([tile, mark], axis=0)
    received = lax.ppermute(sent, "core", swap)

    limit = pltpu.CompilerParams(vmem_limit_bytes=40 << 20)
    spec, power = pl.pallas_call(
        tile_kernel,
        out_shape=[
            jax.ShapeDtypeStruct((2, 2, ROWS, N), F32),
            jax.ShapeDtypeStruct((PART, N), BF16),
        ],
        grid=(1,),
        in_specs=smem(1)
        + [
            pl.BlockSpec((N, N), lambda i: (0, 0)),
            pl.BlockSpec((N, N), lambda i: (0, 0)),
            pl.BlockSpec((2 * ROWS, N), lambda i: (0, 0)),
            pl.BlockSpec((2 * N, 2 * N), lambda i: (0, 0)),
        ],
        out_specs=[
            pl.BlockSpec((2, 2, ROWS, N), lambda i: (0, 0, 0, 0)),
            pl.BlockSpec((PART, N), lambda i: (0, 0)),
        ],
        scratch_shapes=[pltpu.VMEM((ROWS, N), F32)],
        compiler_params=limit,
        cost_estimate=cost(2 * 2 * ROWS * N * N * 6, 4 << 20),
        name="tile",
    )(core[None].astype(jnp.int32), tile, received, first, forward)

    gain, weight = pl.pallas_call(
        gain_kernel,
        out_shape=[jax.ShapeDtypeStruct((2, ROWS, N), F32)] * 2,
        grid=(1,),
        in_specs=smem(1)
        + [pl.BlockSpec((16, N), lambda i: (N // 16, 0))]
        + smem(4),
        out_specs=[pl.BlockSpec((2, ROWS, N), lambda i: (0, 0, 0))] * 2,
        compiler_params=limit,
        cost_estimate=cost(2 * ROWS * N * 60, 2 << 20),
        name="gain",
    )(ctf_row, received, defocus_term, astig_term, astig_cross, phase_shift)

    deep = lax.axis_size("z")
    sums = power.astype(F32)
    for s in range(1, deep):
        moved = lax.ppermute(power, "z", [(i, (i + s) % deep) for i in range(deep)])
        sums = sums + moved.astype(F32)
    sums = sums.astype(BF16)
    moved = lax.ppermute(sums, "xhi", swap)
    mine = (sums.astype(F32) + moved.astype(F32)).astype(BF16)
    theirs = lax.ppermute(mine, "core", swap)
    low = jnp.where(core == 0, mine, theirs)
    high = jnp.where(core == 0, theirs, mine)

    library = library.reshape(groups, planes, N // groups, N)
    best, give = pl.pallas_call(
        match_kernel,
        out_shape=[
            jax.ShapeDtypeStruct((2, ROWS, N), F32),
            jax.ShapeDtypeStruct((2, ROWS, N), BF16),
        ],
        grid=(planes,),
        in_specs=[
            pl.BlockSpec((groups, None, N // groups, N), lambda i: (0, i, 0, 0)),
            pl.BlockSpec((2, 2, ROWS, N), lambda i: (0, 0, 0, 0)),
            pl.BlockSpec((PART, N), lambda i: (0, 0)),
            pl.BlockSpec((PART, N), lambda i: (0, 0)),
            pl.BlockSpec((2, ROWS, N), lambda i: (0, 0, 0)),
            pl.BlockSpec((2, ROWS, N), lambda i: (0, 0, 0)),
            pl.BlockSpec((2 * ROWS, N), lambda i: (0, 0)),
            pl.BlockSpec((2 * N, 2 * N), lambda i: (0, 0)),
            pl.BlockSpec((2 * N, 2 * N), lambda i: (0, 0)),
            pl.BlockSpec((2, ROWS, ROWS), lambda i: (0, 0, 0)),
        ],
        out_specs=[
            pl.BlockSpec((2, ROWS, N), lambda i: (0, 0, 0)),
            pl.BlockSpec((2, ROWS, N), lambda i: (0, 0, 0)),
        ],
        scratch_shapes=[
            pltpu.VMEM((2, 2, ROWS, N), F32),
            pltpu.VMEM((2, ROWS, N), F32),
            pltpu.VMEM((2, 2, ROWS, N), F32),
        ],
        compiler_params=limit,
        cost_estimate=cost(planes * 2 * ROWS * N * N * 16, 8 << 20),
        name="match",
    )(library, spec, low, high, gain, weight, first, forward, inverse, fold)

    got = lax.ppermute(give, "core", swap)
    peak = pl.pallas_call(
        join_kernel,
        out_shape=jax.ShapeDtypeStruct((N, N), F32),
        compiler_params=limit,
        cost_estimate=cost(3 * 2 * HALF * 2 * ROWS * N, 2 << 20),
        name="join",
    )(best, got, unfold)
    return peak[None, None]


def solution(mesh):
    fine = Mesh(mesh.devices.reshape(2, 4, 4, 2, 2), DEF + BLK)
    in_specs = (P(DEF, BLK, None, None), P(BLK, DEF, None), P(DEF, BLK), P(), P(), P(), P())
    out_specs = P(DEF, BLK, None, None)
    return jax.shard_map(
        per_device, mesh=fine, in_specs=in_specs, out_specs=out_specs, check_vma=False
    )
```

```python
import math

import jax
import jax.numpy as jnp
import ml_dtypes
import numpy as np
from jax import lax
from jax.experimental import pallas as pl
from jax.experimental.pallas import tpu as pltpu
from jax.sharding import Mesh
from jax.sharding import PartitionSpec as P

DEF = ("xlo", "y")
BLK = ("z", "xhi", "core")
CHIPS = ("xlo", "y", "z", "xhi")
ZX = ("z", "xhi")
N = 384
HALF = N // 2
THIRD = N // 3
BLOCKS = (80, 64, 64)
ROWS = sum(BLOCKS)
PART = ROWS // 2
ROOT = math.sqrt(3.0) / 2.0
F32 = jnp.float32
BF16 = jnp.bfloat16


def tables():
    j = np.arange(N)
    phase = (j[:, None] * j[None, :]) % N
    cos = np.cos(2.0 * np.pi * phase / N)
    sin = np.sin(2.0 * np.pi * phase / N)
    bf = ml_dtypes.bfloat16
    u = np.concatenate([3 * np.arange(b) + c for c, b in enumerate(BLOCKS)])
    keep = (u <= HALF)[:, None]
    u = np.minimum(u, HALF)
    v = np.concatenate([3 * np.arange(THIRD) + c for c in range(3)])
    first = np.concatenate([keep * cos[u], keep * -sin[u]])
    c, s = cos[:, v], sin[:, v]
    forward = np.block([[c, -s], [s, c]])
    r = np.arange(THIRD)
    b0, b1 = BLOCKS[0], BLOCKS[0] + BLOCKS[1]
    real = np.concatenate([(keep * cos[u])[:b0, r], (keep * -sin[u])[:b0, r]])
    c1, s1 = cos[u[b0:b1]][:, r], sin[u[b0:b1]][:, r]
    c2, s2 = cos[u[b1:]][:, r], sin[u[b1:]][:, r]
    pair = np.block([[c1, s1], [c2, -s2], [-s1, c1], [-s2, -c2]])
    ahead, back = [], []
    for k in range(3):
        ck = cos[r][:, 3 * r + k]
        sk = sin[r][:, 3 * r + k]
        ahead.append(np.block([[ck, -sk], [sk, ck]]))
        back.append(np.block([[ck.T, sk.T], [-sk.T, ck.T]]))
    ahead, back = np.stack(ahead), np.stack(back)
    weight = np.where((u == 0) | (u == HALF), 1.0, 2.0) * keep[:, 0]
    fold = np.zeros((2, ROWS, ROWS))
    fold[0, : HALF + 1] = cos[: HALF + 1][:, u].astype(bf).astype(float) * weight
    fold[1, : HALF + 1] = sin[: HALF + 1][:, u].astype(bf).astype(float) * weight
    unfold = np.zeros((HALF, 2 * ROWS))
    unfold[0, HALF] = 1.0
    for i in range(1, HALF):
        unfold[i, ROWS + HALF - i] = 1.0
    names = ("first", "forward", "real", "pair", "ahead", "back", "fold", "unfold")
    arrays = (first, forward, real, pair, ahead, back, fold, unfold)
    return {n: jnp.asarray(a.astype(bf)) for n, a in zip(names, arrays)}


def dot(a, b):
    return jnp.dot(a, b, preferred_element_type=F32)


def row_numbers():
    i = lax.broadcasted_iota(jnp.int32, (ROWS, N), 0)
    k = lax.broadcasted_iota(jnp.int32, (ROWS, N), 1)
    b0, b1 = BLOCKS[0], BLOCKS[0] + BLOCKS[1]
    u = jnp.where(i < b0, 3 * i, jnp.where(i < b1, 3 * (i - b0) + 1, 3 * (i - b1) + 2))
    v = jnp.where(
        k < THIRD, 3 * k, jnp.where(k < 2 * THIRD, 3 * (k - THIRD) + 1, 3 * (k - 2 * THIRD) + 2)
    )
    return u, v


def row_scale(u):
    return jnp.where((u > 0) & (u < HALF), 2.0, jnp.where(u <= HALF, 1.0, 0.0))


def copy_kernel(block_ref, out_ref, wide_sc, sems):
    count = wide_sc.shape[0]
    wide_sc[...] = jnp.broadcast_to(block_ref[...][None], wide_sc.shape)
    moves = [
        pltpu.make_async_copy(wide_sc, out_ref.at[pl.ds(i * count, count)], sems.at[i])
        for i in range(out_ref.shape[0] // count)
    ]
    for move in moves:
        move.start()
    for move in moves:
        move.wait()


def sine(x):
    x = x - jnp.round(x)
    a = jnp.abs(x)
    a = jnp.minimum(a, 0.5 - a)
    s = a * a
    p = jnp.full_like(x, -15.0946425768229800)
    for c in (
        42.0586939448600400,
        -76.7058597530613900,
        81.6052492760750400,
        -41.3417022403997600,
        6.28318530717958648,
    ):
        p = p * s + c
    p = p * a
    return jnp.where(x < 0.0, -p, p)


def tile_kernel(
    core_ref,
    row_ref,
    d_ref,
    a_ref,
    x_ref,
    p_ref,
    own_ref,
    other_ref,
    first_ref,
    forward_ref,
    spec_ref,
    weight_ref,
    power_ref,
    total_ref,
):
    mark = other_ref[N:, :].astype(F32)
    other = jnp.max(mark).astype(jnp.int32)
    u, v = row_numbers()
    row = jnp.where(u < HALF, u, u - N).astype(F32) * (1.0 / N)
    col = jnp.where(v < HALF, v, v - N).astype(F32) * (1.0 / N)
    radial = row * row + col * col
    stretch = row * row - col * col
    skew = 2.0 * row * col
    inner = (u > 0) & (u < HALF)
    scale = row_scale(u)
    turn = 1.0 / (2.0 * math.pi)
    for t, r in enumerate((row_ref[0, 0], other)):
        image = own_ref[...] if t == 0 else other_ref[:N, :]
        part = dot(first_ref[...], image).astype(BF16)
        both = jnp.concatenate([part[:ROWS], part[ROWS:]], axis=1)
        out = dot(both, forward_ref[...])
        re, im = out[:, :N], out[:, N:]
        square = re * re + im * im
        total_ref[...] = square if t == 0 else total_ref[...] + square
        base = (d_ref[r] * turn) * radial + (a_ref[r] * turn) * stretch + p_ref[r] * turn
        cross = (x_ref[r] * turn) * skew
        plus = -sine(base + cross)
        minus = -sine(base - cross)
        mirror = jnp.where(inner & (v == HALF), minus, plus)
        gain = 0.5 * (plus + mirror)
        spec_ref[t, 0] = re * gain
        spec_ref[t, 1] = im * gain
        weight_ref[t] = (0.5 * scale) * (plus * plus + mirror * mirror)
    start = pl.multiple_of(core_ref[0] * PART, 8)
    power_ref[...] = total_ref[pl.ds(start, PART), :].astype(BF16)


def library_kernel(image_ref, real_ref, pair_ref, ahead_ref, out_ref):
    image = image_ref[...].reshape(N, N).astype(F32)
    x0, x1, x2 = image[:THIRD], image[THIRD : 2 * THIRD], image[2 * THIRD :]
    plus, minus = x1 + x2, x1 - x2
    f0 = (x0 + plus).astype(BF16)
    f1 = jnp.concatenate(
        [(x0 - 0.5 * plus).astype(BF16), (-ROOT * minus).astype(BF16)], axis=0
    )
    low = dot(real_ref[...], f0)
    high = dot(pair_ref[...], f1)
    b0 = BLOCKS[0]
    b2 = BLOCKS[1] + BLOCKS[2]
    re = jnp.concatenate([low[:b0], high[:b2]], axis=0)
    im = jnp.concatenate([low[b0:], high[b2:]], axis=0)
    r0, r1, r2 = re[:, :THIRD], re[:, THIRD : 2 * THIRD], re[:, 2 * THIRD :]
    i0, i1, i2 = im[:, :THIRD], im[:, THIRD : 2 * THIRD], im[:, 2 * THIRD :]
    rp, rm = r1 + r2, ROOT * (r1 - r2)
    ip, im_ = i1 + i2, ROOT * (i1 - i2)
    rh, ih = r0 - 0.5 * rp, i0 - 0.5 * ip
    parts = ((r0 + rp, i0 + ip), (rh + im_, ih - rm), (rh - im_, ih + rm))
    for k, (a, b) in enumerate(parts):
        lhs = jnp.concatenate([a.astype(BF16), b.astype(BF16)], axis=1)
        out = dot(lhs, ahead_ref[k]).astype(BF16)
        out_ref[0, :, k * THIRD : (k + 1) * THIRD] = out[:, :THIRD]
        out_ref[1, :, k * THIRD : (k + 1) * THIRD] = out[:, THIRD:]


def match_kernel(
    lib_ref,
    spec_ref,
    weight_ref,
    low_ref,
    high_ref,
    back_ref,
    fold_ref,
    out_ref,
    spec_sc,
    weight_sc,
    best_sc,
):
    step = pl.program_id(0)

    @pl.when(step == 0)
    def _():
        power = jnp.concatenate([low_ref[...], high_ref[...]], axis=0).astype(F32) * (1.0 / 16.0)
        u, _ = row_numbers()
        mean = jnp.sum(power * row_scale(u)) * (1.0 / (N * N))
        inverse_noise = 1.0 / (jnp.where(u <= HALF, power, 1.0) + 0.05 * mean)
        spec_sc[0] = spec_ref[0] * inverse_noise
        spec_sc[1] = spec_ref[1] * inverse_noise
        weight_sc[...] = weight_ref[...] * inverse_noise
        best_sc[...] = jnp.full_like(best_sc, -jnp.inf)

    re = lib_ref[0].astype(F32)
    im = lib_ref[1].astype(F32)
    norm = jnp.sum((re * re + im * im) * weight_sc[...])
    scale = lax.rsqrt(jnp.full((1, THIRD), norm + 1e-06, F32))
    s_re, s_im = spec_sc[0], spec_sc[1]
    p_re = (s_re * re + s_im * im).astype(BF16)
    p_im = (s_im * re - s_re * im).astype(BF16)
    g = []
    for k in range(3):
        at = slice(k * THIRD, (k + 1) * THIRD)
        g.append(dot(jnp.concatenate([p_re[:, at], p_im[:, at]], axis=1), back_ref[k]))
    (r0, i0), (r1, i1), (r2, i2) = ((x[:, :THIRD], x[:, THIRD:]) for x in g)
    slant = scale * ROOT
    rp, rm = r1 + r2, slant * (r1 - r2)
    ip, im_ = i1 + i2, slant * (i1 - i2)
    rh, ih = scale * (r0 - 0.5 * rp), scale * (i0 - 0.5 * ip)
    h_re = [scale * (r0 + rp), rh - im_, rh + im_]
    h_im = [scale * (i0 + ip), ih + rm, ih - rm]
    h_re = jnp.concatenate([h.astype(BF16) for h in h_re], axis=1)
    h_im = jnp.concatenate([h.astype(BF16) for h in h_im], axis=1)
    even = dot(fold_ref[0], h_re)
    odd = dot(fold_ref[1], h_im)
    best_sc[0] = jnp.maximum(best_sc[0], even - odd)
    best_sc[1] = jnp.maximum(best_sc[1], even + odd)

    @pl.when(step == pl.num_programs(0) - 1)
    def _():
        out_ref[...] = best_sc[...].astype(out_ref.dtype)


def join_kernel(best_ref, got_ref, unfold_ref, out_ref):
    best = jnp.maximum(best_ref[...], got_ref[...].astype(F32))
    out_ref[:HALF] = best[0, :HALF]
    rest = best.reshape(2 * ROWS, N)
    total = None
    for _ in range(3):
        part = rest.astype(BF16)
        rest = rest - part.astype(F32)
        moved = dot(unfold_ref[...], part)
        total = moved if total is None else total + moved
    out_ref[HALF:] = total


def vmem(count):
    return [pl.BlockSpec(memory_space=pltpu.VMEM)] * count


def smem(count):
    return [pl.BlockSpec(memory_space=pltpu.SMEM)] * count


def cost(flops, size):
    return pl.CostEstimate(flops=flops, bytes_accessed=size, transcendentals=0)


def params(mib):
    return pltpu.CompilerParams(vmem_limit_bytes=mib << 20)


def per_device(images, projections, ctf_row, defocus_term, astig_term, astig_cross, phase_shift):
    tab = tables()
    chips = math.prod(lax.axis_size(a) for a in CHIPS)
    groups = math.prod(lax.axis_size(a) for a in DEF)
    planes = chips // groups
    core = lax.axis_index("core")
    swap = [(0, 1), (1, 0)]

    block = projections[0]
    copies = pl.pallas_call(
        copy_kernel,
        out_shape=jax.ShapeDtypeStruct((chips,) + block.shape, BF16),
        in_specs=vmem(1),
        out_specs=pl.BlockSpec(memory_space=pltpu.HBM),
        scratch_shapes=[
            pltpu.VMEM((groups,) + block.shape, BF16),
            pltpu.SemaphoreType.DMA((planes,)),
        ],
        compiler_params=params(4),
        cost_estimate=cost(0, 3 << 20),
        name="copies",
    )(block)
    library = lax.all_to_all(copies, CHIPS, 0, 0, tiled=False)

    tile = images[0, 0]
    mark = jnp.broadcast_to(ctf_row.astype(BF16), (16, N))
    received = lax.ppermute(jnp.concatenate([tile, mark], axis=0), "core", swap)

    spec, weight, power = pl.pallas_call(
        tile_kernel,
        out_shape=[
            jax.ShapeDtypeStruct((2, 2, ROWS, N), F32),
            jax.ShapeDtypeStruct((2, ROWS, N), F32),
            jax.ShapeDtypeStruct((PART, N), BF16),
        ],
        in_specs=smem(6) + vmem(4),
        out_specs=vmem(3),
        scratch_shapes=[pltpu.VMEM((ROWS, N), F32)],
        compiler_params=params(16),
        cost_estimate=cost(2 * 2 * ROWS * N * N * 6, 4 << 20),
        name="tile",
    )(
        core[None].astype(jnp.int32),
        ctf_row,
        defocus_term,
        astig_term,
        astig_cross,
        phase_shift,
        tile,
        received,
        tab["first"],
        tab["forward"],
    )

    deep, wide = (lax.axis_size(a) for a in ZX)
    sums = power.astype(F32)
    for dz in range(deep):
        for dx in range(wide):
            if dz or dx:
                perm = [
                    (z * wide + x, (z + dz) % deep * wide + (x + dx) % wide)
                    for z in range(deep)
                    for x in range(wide)
                ]
                sums = sums + lax.ppermute(power, ZX, perm).astype(F32)
    mine = sums.astype(BF16)
    theirs = lax.ppermute(mine, "core", swap)
    low = jnp.where(core == 0, mine, theirs)
    high = jnp.where(core == 0, theirs, mine)

    library = library.reshape(groups, planes, N // groups, N)
    spectra = pl.pallas_call(
        library_kernel,
        out_shape=jax.ShapeDtypeStruct((planes, 2, ROWS, N), BF16),
        grid=(planes,),
        in_specs=[pl.BlockSpec((groups, None, N // groups, N), lambda i: (0, i, 0, 0))] + vmem(3),
        out_specs=pl.BlockSpec((None, 2, ROWS, N), lambda i: (i, 0, 0, 0)),
        compiler_params=params(16),
        cost_estimate=cost(planes * 2 * ROWS * 768 * 256 * 2, 5 << 20),
        name="library",
    )(library, tab["real"], tab["pair"], tab["ahead"])

    def match(t, dtype, name):
        return pl.pallas_call(
            match_kernel,
            out_shape=jax.ShapeDtypeStruct((2, ROWS, N), dtype),
            grid=(planes,),
            in_specs=[
                pl.BlockSpec((None, 2, ROWS, N), lambda i: (i, 0, 0, 0)),
                pl.BlockSpec((None, 2, ROWS, N), lambda i: (t, 0, 0, 0)),
                pl.BlockSpec((None, ROWS, N), lambda i: (t, 0, 0)),
            ]
            + vmem(4),
            out_specs=vmem(1)[0],
            scratch_shapes=[
                pltpu.VMEM((2, ROWS, N), F32),
                pltpu.VMEM((ROWS, N), F32),
                pltpu.VMEM((2, ROWS, N), F32),
            ],
            compiler_params=params(16),
            cost_estimate=cost(planes * 2 * ROWS * 768 * 256 * 2, 4 << 20),
            name=name,
        )(spectra, spec, weight, low, high, tab["back"], tab["fold"])

    give = match(1, BF16, "other")
    got = lax.ppermute(give, "core", swap)
    best = match(0, F32, "own")
    peak = pl.pallas_call(
        join_kernel,
        out_shape=jax.ShapeDtypeStruct((N, N), F32),
        in_specs=vmem(3),
        out_specs=vmem(1)[0],
        compiler_params=params(16),
        cost_estimate=cost(3 * 2 * HALF * 2 * ROWS * N, 2 << 20),
        name="join",
    )(best, got, tab["unfold"])
    return peak[None, None]


def solution(mesh):
    fine = Mesh(mesh.devices.reshape(2, 4, 4, 2, 2), DEF + BLK)
    in_specs = (P(DEF, BLK, None, None), P(BLK, DEF, None), P(DEF, BLK), P(), P(), P(), P())
    out_specs = P(DEF, BLK, None, None)
    return jax.shard_map(
        per_device, mesh=fine, in_specs=in_specs, out_specs=out_specs, check_vma=False
    )
```

```python
import functools
import math

import jax
import jax.numpy as jnp
import ml_dtypes
import numpy as np
from jax import lax
from jax.experimental import pallas as pl
from jax.experimental.pallas import tpu as pltpu
from jax.sharding import Mesh
from jax.sharding import PartitionSpec as P

DEF = ("xlo", "y")
BLK = ("z", "xhi", "core")
N = 384
HALF = N // 2
THIRD = N // 3
BLOCKS = (64, 64, 72)
ROWS = sum(BLOCKS)
ROOT = math.sqrt(3.0) / 2.0
F32 = jnp.float32
BF16 = jnp.bfloat16


def tables():
    j = np.arange(N)
    phase = (j[:, None] * j[None, :]) % N
    cos = np.cos(2.0 * np.pi * phase / N)
    sin = np.sin(2.0 * np.pi * phase / N)
    bf = ml_dtypes.bfloat16
    u = np.concatenate([3 * np.arange(b) + c for c, b in zip((1, 2, 0), BLOCKS)])
    keep = (u <= HALF)[:, None]
    u = np.minimum(u, HALF)
    r = np.arange(THIRD)
    b1, b2 = BLOCKS[0], BLOCKS[0] + BLOCKS[1]
    real = np.concatenate([(keep * cos[u])[b2:, r], (keep * -sin[u])[b2:, r]])
    c1, s1 = cos[u[:b1]][:, r], sin[u[:b1]][:, r]
    c2, s2 = cos[u[b1:b2]][:, r], sin[u[b1:b2]][:, r]
    pair = np.block([[c1, s1], [c2, -s2], [-s1, c1], [-s2, -c2]])
    ahead, back = [], []
    for k in range(3):
        ck = cos[r][:, 3 * r + k]
        sk = sin[r][:, 3 * r + k]
        ahead.append(np.block([[ck, -sk], [sk, ck]]))
        back.append(np.block([[ck.T, sk.T], [-sk.T, ck.T]]))
    ahead, back = np.stack(ahead), np.stack(back)
    weight = np.where((u == 0) | (u == HALF), 1.0, 2.0) * keep[:, 0]
    fold = np.zeros((2, ROWS, ROWS))
    fold[0, : HALF + 1] = cos[: HALF + 1][:, u].astype(bf).astype(float) * weight
    fold[1, : HALF + 1] = sin[: HALF + 1][:, u].astype(bf).astype(float) * weight
    unfold = np.zeros((HALF, 2 * ROWS))
    unfold[0, HALF] = 1.0
    for i in range(1, HALF):
        unfold[i, ROWS + HALF - i] = 1.0
    names = ("real", "pair", "ahead", "back", "fold", "unfold")
    arrays = (real, pair, ahead, back, fold, unfold)
    return {n: jnp.asarray(a.astype(bf)) for n, a in zip(names, arrays)}


def dot(a, b):
    return jnp.dot(a, b, preferred_element_type=F32)


def row_numbers():
    i = lax.broadcasted_iota(jnp.int32, (ROWS, N), 0)
    k = lax.broadcasted_iota(jnp.int32, (ROWS, N), 1)
    b1, b2 = BLOCKS[0], BLOCKS[0] + BLOCKS[1]
    u = jnp.where(i < b1, 3 * i + 1, jnp.where(i < b2, 3 * (i - b1) + 2, 3 * (i - b2)))
    v = jnp.where(
        k < THIRD, 3 * k, jnp.where(k < 2 * THIRD, 3 * (k - THIRD) + 1, 3 * (k - 2 * THIRD) + 2)
    )
    return u, v


def row_scale(u):
    return jnp.where((u > 0) & (u < HALF), 2.0, jnp.where(u <= HALF, 1.0, 0.0))


def spread(block_ref, out_ref, sems):
    moves = [
        pltpu.make_async_copy(block_ref, out_ref.at[i], sems.at[i]) for i in range(out_ref.shape[0])
    ]
    for move in moves:
        move.start()
    for move in moves:
        move.wait()


def copy_kernel(block_ref, out_ref, sems):
    spread(block_ref, out_ref, sems)


def sine(x):
    x = x - jnp.round(x)
    a = jnp.abs(x)
    a = jnp.minimum(a, 0.5 - a)
    s = a * a
    p = jnp.full_like(x, -15.0946425768229800)
    for c in (
        42.0586939448600400,
        -76.7058597530613900,
        81.6052492760750400,
        -41.3417022403997600,
        6.28318530717958648,
    ):
        p = p * s + c
    p = p * a
    return jnp.where(x < 0.0, -p, p)


def half_spectrum(image, real, pair, ahead):
    image = image.astype(F32)
    x0, x1, x2 = image[:THIRD], image[THIRD : 2 * THIRD], image[2 * THIRD :]
    plus, minus = x1 + x2, x1 - x2
    f0 = (x0 + plus).astype(BF16)
    f1 = jnp.concatenate([(x0 - 0.5 * plus).astype(BF16), (-ROOT * minus).astype(BF16)], axis=0)
    low = dot(real, f0)
    high = dot(pair, f1)
    b, c = BLOCKS[0] + BLOCKS[1], BLOCKS[2]
    re = jnp.concatenate([high[:b], low[:c]], axis=0)
    im = jnp.concatenate([high[b:], low[c:]], axis=0)
    r0, r1, r2 = re[:, :THIRD], re[:, THIRD : 2 * THIRD], re[:, 2 * THIRD :]
    i0, i1, i2 = im[:, :THIRD], im[:, THIRD : 2 * THIRD], im[:, 2 * THIRD :]
    rp, rm = r1 + r2, ROOT * (r1 - r2)
    ip, im_ = i1 + i2, ROOT * (i1 - i2)
    rh, ih = r0 - 0.5 * rp, i0 - 0.5 * ip
    parts = ((r0 + rp, i0 + ip), (rh + im_, ih - rm), (rh - im_, ih + rm))
    result = []
    for k, (a, b) in enumerate(parts):
        out = dot(jnp.concatenate([a.astype(BF16), b.astype(BF16)], axis=1), ahead[k])
        result.append((out[:, :THIRD], out[:, THIRD:]))
    return result


def store_spectrum(ref, parts):
    for k, (re, im) in enumerate(parts):
        at = slice(k * THIRD, (k + 1) * THIRD)
        ref[0, :, at] = re.astype(ref.dtype)
        ref[1, :, at] = im.astype(ref.dtype)


def own_kernel(image_ref, real_ref, pair_ref, ahead_ref, spec_ref):
    parts = half_spectrum(image_ref[...], real_ref[...], pair_ref[...], ahead_ref)
    store_spectrum(spec_ref, parts)


def other_kernel(image_ref, own_ref, real_ref, pair_ref, ahead_ref, spec_ref, power_ref):
    parts = half_spectrum(image_ref[...], real_ref[...], pair_ref[...], ahead_ref)
    store_spectrum(spec_ref, parts)
    for k, (re, im) in enumerate(parts):
        at = slice(k * THIRD, (k + 1) * THIRD)
        a, b = own_ref[0, :, at], own_ref[1, :, at]
        power_ref[:, at] = ((a * a + b * b) + (re * re + im * im)).astype(BF16)


def library_kernel(image_ref, real_ref, pair_ref, ahead_ref, spec_ref, out_ref, sems):
    image = image_ref[...].reshape(N, N)
    store_spectrum(spec_ref, half_spectrum(image, real_ref[...], pair_ref[...], ahead_ref))
    spread(spec_ref, out_ref, sems)


def whiten_kernel(
    row_ref,
    mate_ref,
    d_ref,
    a_ref,
    x_ref,
    p_ref,
    own_ref,
    other_ref,
    mine_ref,
    theirs_ref,
    spec_ref,
    weight_ref,
):
    u, v = row_numbers()
    scale = row_scale(u)
    power = (mine_ref[...].astype(F32) + theirs_ref[...].astype(F32)) * (1.0 / 16.0)
    mean = jnp.sum(power * scale) * (1.0 / (N * N))
    inverse_noise = 1.0 / (jnp.where(u <= HALF, power, 1.0) + 0.05 * mean)
    row = jnp.where(u < HALF, u, u - N).astype(F32) * (1.0 / N)
    col = jnp.where(v < HALF, v, v - N).astype(F32) * (1.0 / N)
    radial = row * row + col * col
    stretch = row * row - col * col
    skew = 2.0 * row * col
    inner = (u > 0) & (u < HALF)
    turn = 1.0 / (2.0 * math.pi)
    for t, r in enumerate((row_ref[0, 0], mate_ref[0, 0])):
        base = (d_ref[r] * turn) * radial + (a_ref[r] * turn) * stretch + p_ref[r] * turn
        cross = (x_ref[r] * turn) * skew
        plus = -sine(base + cross)
        minus = -sine(base - cross)
        mirror = jnp.where(inner & (v == HALF), minus, plus)
        gain = (0.5 * (plus + mirror)) * inverse_noise
        source = own_ref if t == 0 else other_ref
        spec_ref[t, 0] = source[0] * gain
        spec_ref[t, 1] = source[1] * gain
        weight_ref[t] = (0.5 * scale) * (plus * plus + mirror * mirror) * inverse_noise


def match_step(re, im, square, t, spec_ref, weight_ref, back_ref, fold_ref):
    norm = jnp.sum(square * weight_ref[t])
    scale = lax.rsqrt(jnp.full((1, THIRD), norm + 1e-06, F32))
    s_re, s_im = spec_ref[t, 0], spec_ref[t, 1]
    p_re = (s_re * re + s_im * im).astype(BF16)
    p_im = (s_im * re - s_re * im).astype(BF16)
    g = []
    for k in range(3):
        at = slice(k * THIRD, (k + 1) * THIRD)
        g.append(dot(jnp.concatenate([p_re[:, at], p_im[:, at]], axis=1), back_ref[k]))
    (r0, i0), (r1, i1), (r2, i2) = ((x[:, :THIRD], x[:, THIRD:]) for x in g)
    slant = scale * ROOT
    rp, rm = r1 + r2, slant * (r1 - r2)
    ip, im_ = i1 + i2, slant * (i1 - i2)
    rh, ih = scale * (r0 - 0.5 * rp), scale * (i0 - 0.5 * ip)
    h_re = [scale * (r0 + rp), rh - im_, rh + im_]
    h_im = [scale * (i0 + ip), ih + rm, ih - rm]
    h_re = jnp.concatenate([h.astype(BF16) for h in h_re], axis=1)
    h_im = jnp.concatenate([h.astype(BF16) for h in h_im], axis=1)
    even = dot(fold_ref[0], h_re)
    odd = dot(fold_ref[1], h_im)
    return even - odd, even + odd


def near_kernel(lib_ref, spec_ref, weight_ref, back_ref, fold_ref, out_ref):
    step = pl.program_id(0)

    @pl.when(step == 0)
    def _():
        out_ref[...] = jnp.full_like(out_ref, -jnp.inf)

    re = lib_ref[step, 0].astype(F32)
    im = lib_ref[step, 1].astype(F32)
    square = re * re + im * im
    for t in range(2):
        minus, plus = match_step(re, im, square, t, spec_ref, weight_ref, back_ref, fold_ref)
        out_ref[t, 0] = jnp.maximum(out_ref[t, 0], minus)
        out_ref[t, 1] = jnp.maximum(out_ref[t, 1], plus)


def far_kernel(t, lib_ref, spec_ref, weight_ref, back_ref, fold_ref, start_ref, out_ref, best_sc):
    step = pl.program_id(0)

    @pl.when(step == 0)
    def _():
        best_sc[...] = start_ref[t]

    re = lib_ref[step, 0].astype(F32)
    im = lib_ref[step, 1].astype(F32)
    square = re * re + im * im
    minus, plus = match_step(re, im, square, t, spec_ref, weight_ref, back_ref, fold_ref)
    best_sc[0] = jnp.maximum(best_sc[0], minus)
    best_sc[1] = jnp.maximum(best_sc[1], plus)

    @pl.when(step == pl.num_programs(0) - 1)
    def _():
        out_ref[...] = best_sc[...].astype(out_ref.dtype)


def join_kernel(best_ref, got_ref, unfold_ref, out_ref):
    best = jnp.maximum(best_ref[...], got_ref[...].astype(F32))
    out_ref[:HALF] = best[0, :HALF]
    rest = best.reshape(2 * ROWS, N)
    total = None
    for _ in range(3):
        part = rest.astype(BF16)
        rest = rest - part.astype(F32)
        moved = dot(unfold_ref[...], part)
        total = moved if total is None else total + moved
    out_ref[HALF:] = total


def vmem(count):
    return [pl.BlockSpec(memory_space=pltpu.VMEM)] * count


def smem(count):
    return [pl.BlockSpec(memory_space=pltpu.SMEM)] * count


def cost(flops, size):
    return pl.CostEstimate(flops=flops, bytes_accessed=size, transcendentals=0)


def params(mib):
    return pltpu.CompilerParams(vmem_limit_bytes=mib << 20)


def per_device(images, projections, ctf_row, defocus_term, astig_term, astig_cross, phase_shift):
    tab = tables()
    transform = (tab["real"], tab["pair"], tab["ahead"])
    groups = math.prod(lax.axis_size(a) for a in DEF)
    deep, wide = lax.axis_size("z"), lax.axis_size("xhi")
    core = lax.axis_index("core")
    swap = [(0, 1), (1, 0)]
    spectrum = pltpu.VMEM((2, ROWS, N), F32)
    work = 2 * ROWS * 768 * 256 * 2

    block = projections[0]
    image = lax.all_to_all(
        jnp.broadcast_to(block[None], (groups,) + block.shape), DEF, 0, 0, tiled=False
    )

    tile = images[0, 0]
    received = lax.ppermute(tile, "core", swap)
    own = pl.pallas_call(
        own_kernel,
        out_shape=spectrum,
        in_specs=vmem(4),
        out_specs=vmem(1)[0],
        compiler_params=params(16),
        cost_estimate=cost(work, 2 << 20),
        name="own_tile",
    )(tile, *transform)
    other, power = pl.pallas_call(
        other_kernel,
        out_shape=[spectrum, pltpu.VMEM((ROWS, N), BF16)],
        in_specs=vmem(5),
        out_specs=vmem(2),
        compiler_params=params(16),
        cost_estimate=cost(work, 2 << 20),
        name="other_tile",
    )(received, own, *transform)

    image, power = lax.optimization_barrier((image, power))

    sums = jnp.where(core == 0, power.astype(F32), 0.0)
    for dz in range(deep):
        perm = [
            ((z * wide + x) * 2 + c, ((z + dz) % deep * wide + (x ^ c)) * 2 + c)
            for z in range(deep)
            for x in range(wide)
            for c in range(2)
            if dz or c
        ]
        sums = sums + lax.ppermute(power, BLK, perm).astype(F32)
    mine = sums.astype(BF16)
    theirs = lax.ppermute(mine, "core", swap)
    mate = lax.ppermute(ctf_row, "core", swap)
    spec, weight = pl.pallas_call(
        whiten_kernel,
        out_shape=[pltpu.VMEM((2, 2, ROWS, N), F32), pltpu.VMEM((2, ROWS, N), F32)],
        in_specs=smem(6) + vmem(4),
        out_specs=vmem(2),
        compiler_params=params(16),
        cost_estimate=cost(2 * ROWS * N * 60, 4 << 20),
        name="whiten",
    )(ctf_row, mate, defocus_term, astig_term, astig_cross, phase_shift, own, other, mine, theirs)

    wide_shape = (deep, 2, ROWS, N)
    near, near_copies = pl.pallas_call(
        library_kernel,
        out_shape=[pltpu.VMEM((2, ROWS, N), BF16), pltpu.HBM(wide_shape, BF16)],
        in_specs=vmem(4),
        out_specs=[vmem(1)[0], pl.BlockSpec(memory_space=pltpu.HBM)],
        scratch_shapes=[pltpu.SemaphoreType.DMA((deep,))],
        compiler_params=params(16),
        cost_estimate=cost(work, 4 << 20),
        name="library",
    )(image, *transform)
    far, _ = lax.optimization_barrier((lax.ppermute(near, "xhi", swap), mine))
    near_all = lax.all_to_all(near_copies, "z", 0, 0, tiled=False)
    far_copies = pl.pallas_call(
        copy_kernel,
        out_shape=pltpu.HBM(wide_shape, BF16),
        in_specs=vmem(1),
        out_specs=pl.BlockSpec(memory_space=pltpu.HBM),
        scratch_shapes=[pltpu.SemaphoreType.DMA((deep,))],
        compiler_params=params(4),
        cost_estimate=cost(0, 3 << 20),
        name="copies",
    )(far)
    far_all = lax.all_to_all(far_copies, "z", 0, 0, tiled=False)

    near_best = pl.pallas_call(
        near_kernel,
        out_shape=pltpu.VMEM((2, 2, ROWS, N), F32),
        grid=(deep,),
        in_specs=vmem(5),
        out_specs=vmem(1)[0],
        compiler_params=params(16),
        cost_estimate=cost(2 * deep * 2 * work, 8 << 20),
        name="near",
    )(near_all, spec, weight, tab["back"], tab["fold"])
    far_all, near_best = lax.optimization_barrier((far_all, near_best))

    def match(t, dtype, name):
        return pl.pallas_call(
            functools.partial(far_kernel, t),
            out_shape=pltpu.VMEM((2, ROWS, N), dtype),
            grid=(deep,),
            in_specs=vmem(6),
            out_specs=vmem(1)[0],
            scratch_shapes=[pltpu.VMEM((2, ROWS, N), F32)],
            compiler_params=params(16),
            cost_estimate=cost(deep * 2 * work, 4 << 20),
            name=name,
        )(far_all, spec, weight, tab["back"], tab["fold"], near_best)

    got = lax.ppermute(match(1, BF16, "far_other"), "core", swap)
    best = match(0, F32, "far_own")
    peak = pl.pallas_call(
        join_kernel,
        out_shape=jax.ShapeDtypeStruct((N, N), F32),
        in_specs=vmem(3),
        out_specs=vmem(1)[0],
        compiler_params=params(16),
        cost_estimate=cost(3 * 2 * HALF * 2 * ROWS * N, 2 << 20),
        name="join",
    )(best, got, tab["unfold"])
    return peak[None, None]


def solution(mesh):
    fine = Mesh(mesh.devices.reshape(2, 4, 4, 2, 2), DEF + BLK)
    in_specs = (P(DEF, BLK, None, None), P(BLK, DEF, None), P(DEF, BLK), P(), P(), P(), P())
    out_specs = P(DEF, BLK, None, None)
    return jax.shard_map(
        per_device, mesh=fine, in_specs=in_specs, out_specs=out_specs, check_vma=False
    )
```

```python
import math

import jax
import jax.numpy as jnp
import ml_dtypes
import numpy as np
from jax import lax
from jax.experimental import pallas as pl
from jax.experimental.pallas import tpu as pltpu
from jax.sharding import Mesh
from jax.sharding import PartitionSpec as P

DEF = ("xlo", "y")
BLK = ("z", "xhi", "core")
N = 384
HALF = N // 2
THIRD = N // 3
BLOCKS = (64, 64, 72)
ROWS = sum(BLOCKS)
FOLD = 208
ROOT = math.sqrt(3.0) / 2.0
F32 = jnp.float32
BF16 = jnp.bfloat16


def tables():
    j = np.arange(N)
    phase = (j[:, None] * j[None, :]) % N
    cos = np.cos(2.0 * np.pi * phase / N)
    sin = np.sin(2.0 * np.pi * phase / N)
    bf = ml_dtypes.bfloat16
    u = np.concatenate([3 * np.arange(b) + c for c, b in zip((1, 2, 0), BLOCKS)])
    keep = (u <= HALF)[:, None]
    u = np.minimum(u, HALF)
    r = np.arange(THIRD)
    b1, b2 = BLOCKS[0], BLOCKS[0] + BLOCKS[1]
    real = np.concatenate([(keep * cos[u])[b2:, r], (keep * -sin[u])[b2:, r]])
    c1, s1 = cos[u[:b1]][:, r], sin[u[:b1]][:, r]
    c2, s2 = cos[u[b1:b2]][:, r], sin[u[b1:b2]][:, r]
    pair = np.block([[c1, s1], [c2, -s2], [-s1, c1], [-s2, -c2]])
    ahead, back = [], []
    for k in range(3):
        ck = cos[r][:, 3 * r + k]
        sk = sin[r][:, 3 * r + k]
        ahead.append(np.block([[ck, -sk], [sk, ck]]))
        back.append(np.block([[ck.T, sk.T], [-sk.T, ck.T]]))
    ahead, back = np.stack(ahead), np.stack(back)
    weight = np.where((u == 0) | (u == HALF), 1.0, 2.0) * keep[:, 0]
    fold = np.zeros((2, ROWS, ROWS))
    fold[0, : HALF + 1] = cos[: HALF + 1][:, u].astype(bf).astype(float) * weight
    fold[1, : HALF + 1] = sin[: HALF + 1][:, u].astype(bf).astype(float) * weight
    unfold = np.zeros((HALF, 2 * ROWS))
    unfold[0, HALF] = 1.0
    for i in range(1, HALF):
        unfold[i, ROWS + HALF - i] = 1.0
    ahead_all = np.concatenate([ahead.reshape(-1, 2 * THIRD), pair, np.pad(real, ((0, 0), (0, THIRD)))])
    pad = ((0, 0), (0, FOLD - ROWS), (0, 2 * THIRD - ROWS))
    back_all = np.concatenate([back.reshape(-1, 2 * THIRD), np.pad(fold, pad).reshape(-1, 2 * THIRD)])
    return [jnp.asarray(a.astype(bf)) for a in (ahead_all, back_all, unfold)]


def dot(a, b):
    return jnp.dot(a, b, preferred_element_type=F32)


def row_numbers():
    i = lax.broadcasted_iota(jnp.int32, (ROWS, N), 0)
    k = lax.broadcasted_iota(jnp.int32, (ROWS, N), 1)
    b1, b2 = BLOCKS[0], BLOCKS[0] + BLOCKS[1]
    u = jnp.where(i < b1, 3 * i + 1, jnp.where(i < b2, 3 * (i - b1) + 2, 3 * (i - b2)))
    v = jnp.where(
        k < THIRD, 3 * k, jnp.where(k < 2 * THIRD, 3 * (k - THIRD) + 1, 3 * (k - 2 * THIRD) + 2)
    )
    return u, v


def row_scale(u):
    return jnp.where((u > 0) & (u < HALF), 2.0, jnp.where(u <= HALF, 1.0, 0.0))


def spread(block_ref, out_ref, sems):
    moves = [
        pltpu.make_async_copy(block_ref, out_ref.at[i], sems.at[i]) for i in range(out_ref.shape[0])
    ]
    for move in moves:
        move.start()
    for move in moves:
        move.wait()


def sine(x):
    x = x - jnp.round(x)
    a = jnp.abs(x)
    a = jnp.minimum(a, 0.5 - a)
    s = a * a
    p = jnp.full_like(x, -15.0946425768229800)
    for c in (
        42.0586939448600400,
        -76.7058597530613900,
        81.6052492760750400,
        -41.3417022403997600,
        6.28318530717958648,
    ):
        p = p * s + c
    p = p * a
    return jnp.where(x < 0.0, -p, p)


def half_spectrum(image, tab):
    wide = 2 * THIRD
    pair, real = tab[3 * wide : 4 * wide, :], tab[4 * wide :, :THIRD]
    image = image.astype(F32)
    x0, x1, x2 = image[:THIRD], image[THIRD : 2 * THIRD], image[2 * THIRD :]
    plus, minus = x1 + x2, x1 - x2
    f0 = (x0 + plus).astype(BF16)
    f1 = jnp.concatenate([(x0 - 0.5 * plus).astype(BF16), (-ROOT * minus).astype(BF16)], axis=0)
    low = dot(real, f0)
    high = dot(pair, f1)
    b, c = BLOCKS[0] + BLOCKS[1], BLOCKS[2]
    re = jnp.concatenate([high[:b], low[:c]], axis=0)
    im = jnp.concatenate([high[b:], low[c:]], axis=0)
    r0, r1, r2 = re[:, :THIRD], re[:, THIRD : 2 * THIRD], re[:, 2 * THIRD :]
    i0, i1, i2 = im[:, :THIRD], im[:, THIRD : 2 * THIRD], im[:, 2 * THIRD :]
    rp, rm = r1 + r2, ROOT * (r1 - r2)
    ip, im_ = i1 + i2, ROOT * (i1 - i2)
    rh, ih = r0 - 0.5 * rp, i0 - 0.5 * ip
    parts = ((r0 + rp, i0 + ip), (rh + im_, ih - rm), (rh - im_, ih + rm))
    result = []
    for k, (a, b) in enumerate(parts):
        lhs = jnp.concatenate([a.astype(BF16), b.astype(BF16)], axis=1)
        out = dot(lhs, tab[k * wide : (k + 1) * wide, :])
        result.append((out[:, :THIRD], out[:, THIRD:]))
    return result


def store_spectrum(ref, parts):
    for k, (re, im) in enumerate(parts):
        at = slice(k * THIRD, (k + 1) * THIRD)
        ref[0, :, at] = re.astype(ref.dtype)
        ref[1, :, at] = im.astype(ref.dtype)


def own_kernel(image_ref, tab_ref, spec_ref, power_ref):
    parts = half_spectrum(image_ref[...].reshape(N, N), tab_ref)
    store_spectrum(spec_ref, parts)
    for k, (re, im) in enumerate(parts):
        power_ref[:, k * THIRD : (k + 1) * THIRD] = (re * re + im * im).astype(BF16)


def other_kernel(image_ref, tab_ref, mate_ref, spec_ref):
    store_spectrum(spec_ref, half_spectrum(image_ref[...], tab_ref))


def library_kernel(image_ref, tab_ref, out_ref, spec_sc, sems):
    store_spectrum(spec_sc, half_spectrum(image_ref[...].reshape(N, N), tab_ref))
    spread(spec_sc, out_ref, sems)


def whiten_kernel(
    row_ref,
    mate_ref,
    d_ref,
    a_ref,
    x_ref,
    p_ref,
    own_ref,
    other_ref,
    mine_ref,
    theirs_ref,
    spec_ref,
    weight_ref,
):
    u, v = row_numbers()
    scale = row_scale(u)
    power = (mine_ref[...].astype(F32) + theirs_ref[...].astype(F32)) * (1.0 / 16.0)
    mean = jnp.sum(power * scale) * (1.0 / (N * N))
    inverse_noise = 1.0 / (jnp.where(u <= HALF, power, 1.0) + 0.05 * mean)
    row = jnp.where(u < HALF, u, u - N).astype(F32) * (1.0 / N)
    col = jnp.where(v < HALF, v, v - N).astype(F32) * (1.0 / N)
    radial = row * row + col * col
    stretch = row * row - col * col
    skew = 2.0 * row * col
    inner = (u > 0) & (u < HALF)
    turn = 1.0 / (2.0 * math.pi)
    for t, r in enumerate((row_ref[0, 0], mate_ref[0, 0])):
        base = (d_ref[r] * turn) * radial + (a_ref[r] * turn) * stretch + p_ref[r] * turn
        cross = (x_ref[r] * turn) * skew
        plus = -sine(base + cross)
        minus = -sine(base - cross)
        mirror = jnp.where(inner & (v == HALF), minus, plus)
        gain = (0.5 * (plus + mirror)) * inverse_noise
        source = own_ref if t == 0 else other_ref
        spec_ref[t, 0] = source[0] * gain
        spec_ref[t, 1] = source[1] * gain
        weight_ref[t] = (0.5 * scale) * (plus * plus + mirror * mirror) * inverse_noise


def match_step(re, im, square, t, spec_ref, weight_ref, tab):
    wide = 2 * THIRD
    norm = jnp.sum(square * weight_ref[t])
    scale = lax.rsqrt(jnp.full((1, THIRD), norm + 1e-06, F32))
    s_re, s_im = spec_ref[t, 0], spec_ref[t, 1]
    p_re = (s_re * re + s_im * im).astype(BF16)
    p_im = (s_im * re - s_re * im).astype(BF16)
    g = []
    for k in range(3):
        at = slice(k * THIRD, (k + 1) * THIRD)
        lhs = jnp.concatenate([p_re[:, at], p_im[:, at]], axis=1)
        g.append(dot(lhs, tab[k * wide : (k + 1) * wide, :]))
    (r0, i0), (r1, i1), (r2, i2) = ((x[:, :THIRD], x[:, THIRD:]) for x in g)
    slant = scale * ROOT
    rp, rm = r1 + r2, slant * (r1 - r2)
    ip, im_ = i1 + i2, slant * (i1 - i2)
    rh, ih = scale * (r0 - 0.5 * rp), scale * (i0 - 0.5 * ip)
    h_re = [scale * (r0 + rp), rh - im_, rh + im_]
    h_im = [scale * (i0 + ip), ih + rm, ih - rm]
    h_re = jnp.concatenate([h.astype(BF16) for h in h_re], axis=1)
    h_im = jnp.concatenate([h.astype(BF16) for h in h_im], axis=1)
    first = 3 * wide
    even = dot(tab[first : first + ROWS, :ROWS], h_re)
    odd = dot(tab[first + FOLD : first + FOLD + ROWS, :ROWS], h_im)
    return even - odd, even + odd


def near_kernel(lib_ref, spec_ref, weight_ref, tab_ref, out_ref):
    step = pl.program_id(0)

    @pl.when(step == 0)
    def _():
        out_ref[...] = jnp.full_like(out_ref, -jnp.inf)

    re = lib_ref[0].astype(F32)
    im = lib_ref[1].astype(F32)
    square = re * re + im * im
    for t in range(2):
        minus, plus = match_step(re, im, square, t, spec_ref, weight_ref, tab_ref)
        out_ref[t, 0] = jnp.maximum(out_ref[t, 0], minus)
        out_ref[t, 1] = jnp.maximum(out_ref[t, 1], plus)


def far_kernel(lib_ref, spec_ref, weight_ref, tab_ref, start_ref, out_ref, best_sc):
    step = pl.program_id(0)

    @pl.when(step == 0)
    def _():
        best_sc[...] = start_ref[0]

    re = lib_ref[0].astype(F32)
    im = lib_ref[1].astype(F32)
    square = re * re + im * im
    minus, plus = match_step(re, im, square, 0, spec_ref, weight_ref, tab_ref)
    best_sc[0] = jnp.maximum(best_sc[0], minus)
    best_sc[1] = jnp.maximum(best_sc[1], plus)

    @pl.when(step == pl.num_programs(0) - 1)
    def _():
        out_ref[...] = best_sc[...].astype(out_ref.dtype)


def join_kernel(best_ref, got_ref, unfold_ref, out_ref):
    best = jnp.maximum(best_ref[...], got_ref[...].astype(F32))
    out_ref[:HALF] = best[0, :HALF]
    rest = best.reshape(2 * ROWS, N)
    total = None
    for _ in range(3):
        part = rest.astype(BF16)
        rest = rest - part.astype(F32)
        moved = dot(unfold_ref[...], part)
        total = moved if total is None else total + moved
    out_ref[HALF:] = total


def full(*shape):
    return pl.BlockSpec(shape, lambda i: (0,) * len(shape))


def smem(count):
    return [pl.BlockSpec(memory_space=pltpu.SMEM)] * count


def cost(flops, size):
    return pl.CostEstimate(flops=flops, bytes_accessed=size, transcendentals=0)


def params(mib):
    return pltpu.CompilerParams(vmem_limit_bytes=mib << 20)


def per_device(images, projections, ctf_row, defocus_term, astig_term, astig_cross, phase_shift):
    ahead, back, unfold = tables()
    groups = math.prod(lax.axis_size(a) for a in DEF)
    deep, wide = lax.axis_size("z"), lax.axis_size("xhi")
    core = lax.axis_index("core")
    swap = [(0, 1), (1, 0)]
    plane = (2, ROWS, N)
    work = 2 * ROWS * 768 * 256 * 2
    near_spec = pl.BlockSpec(memory_space=pltpu.HBM)

    tile = images[0, 0]
    received = lax.ppermute(tile, "xhi", swap)
    mate = lax.ppermute(ctf_row, "xhi", swap)
    block = projections[0]
    copies = pl.pallas_call(
        spread,
        out_shape=pltpu.HBM((groups,) + block.shape, BF16),
        in_specs=[near_spec],
        out_specs=near_spec,
        scratch_shapes=[pltpu.SemaphoreType.DMA((groups,))],
        cost_estimate=cost(0, 1 << 20),
        name="copies",
    )(block)
    image = lax.all_to_all(copies, DEF, 0, 0, tiled=False)

    own, power = pl.pallas_call(
        own_kernel,
        out_shape=[jax.ShapeDtypeStruct(plane, F32), jax.ShapeDtypeStruct((ROWS, N), BF16)],
        grid=(1,),
        in_specs=[full(N, N), full(*ahead.shape)],
        out_specs=[full(*plane), full(ROWS, N)],
        compiler_params=params(16),
        cost_estimate=cost(work, 2 << 20),
        name="own_tile",
    )(tile, ahead)
    other = pl.pallas_call(
        other_kernel,
        out_shape=jax.ShapeDtypeStruct(plane, F32),
        grid=(1,),
        in_specs=[full(N, N), full(*ahead.shape)] + smem(1),
        out_specs=full(*plane),
        compiler_params=params(16),
        cost_estimate=cost(work, 2 << 20),
        name="other_tile",
    )(received, ahead, mate)

    beside = lax.ppermute(power, "core", swap)
    pair = (power.astype(F32) + beside.astype(F32)).astype(BF16)
    sums = jnp.where(core == 0, pair.astype(F32), 0.0)
    for dz in range(deep):
        perm = [
            ((z * wide + x) * 2 + c, ((z + dz) % deep * wide + (x ^ c)) * 2 + c)
            for z in range(deep)
            for x in range(wide)
            for c in range(2)
            if dz or c
        ]
        sums = sums + lax.ppermute(pair, BLK, perm).astype(F32)
    mine = sums.astype(BF16)

    image, _ = lax.optimization_barrier((image, pair))
    near_copies = pl.pallas_call(
        library_kernel,
        out_shape=pltpu.HBM((deep,) + plane, BF16),
        grid=(1,),
        in_specs=[full(groups, N // groups, N), full(*ahead.shape)],
        out_specs=near_spec,
        scratch_shapes=[pltpu.VMEM(plane, BF16), pltpu.SemaphoreType.DMA((deep,))],
        compiler_params=params(16),
        cost_estimate=cost(work, 4 << 20),
        name="library",
    )(image, ahead)
    near_copies, mine, other = lax.optimization_barrier((near_copies, mine, other))
    near_all = lax.all_to_all(near_copies, "z", 0, 0, tiled=False)

    theirs = lax.ppermute(mine, "core", swap)
    spec, weight = pl.pallas_call(
        whiten_kernel,
        out_shape=[jax.ShapeDtypeStruct((2,) + plane, F32), jax.ShapeDtypeStruct(plane, F32)],
        grid=(1,),
        in_specs=smem(6) + [full(*plane)] * 2 + [full(ROWS, N)] * 2,
        out_specs=[full(2, *plane), full(*plane)],
        compiler_params=params(20),
        cost_estimate=cost(2 * ROWS * N * 60, 4 << 20),
        name="whiten",
    )(ctf_row, mate, defocus_term, astig_term, astig_cross, phase_shift, own, other, mine, theirs)

    near_all, spec, weight = lax.optimization_barrier((near_all, spec, weight))
    far_all = lax.ppermute(near_all, "core", swap)
    lib_spec = pl.BlockSpec((None,) + plane, lambda i: (i, 0, 0, 0))
    near_best = pl.pallas_call(
        near_kernel,
        out_shape=jax.ShapeDtypeStruct((2,) + plane, F32),
        grid=(deep,),
        in_specs=[lib_spec, full(2, *plane), full(*plane), full(*back.shape)],
        out_specs=full(2, *plane),
        compiler_params=params(20),
        cost_estimate=cost(2 * deep * 2 * work, 8 << 20),
        name="near",
    )(near_all, spec, weight, back)
    far_all, near_best = lax.optimization_barrier((far_all, near_best))

    def match(t, dtype, name):
        return pl.pallas_call(
            far_kernel,
            out_shape=jax.ShapeDtypeStruct(plane, dtype),
            grid=(deep,),
            in_specs=[
                lib_spec,
                pl.BlockSpec((1,) + plane, lambda i: (t, 0, 0, 0)),
                pl.BlockSpec((1, ROWS, N), lambda i: (t, 0, 0)),
                full(*back.shape),
                pl.BlockSpec((1,) + plane, lambda i: (t, 0, 0, 0)),
            ],
            out_specs=full(*plane),
            scratch_shapes=[pltpu.VMEM(plane, F32)],
            compiler_params=params(20),
            cost_estimate=cost(deep * 2 * work, 4 << 20),
            name=name,
        )(far_all, spec, weight, back, near_best)

    got = lax.ppermute(match(1, BF16, "far_other"), "xhi", swap)
    best = match(0, F32, "far_own")
    peak = pl.pallas_call(
        join_kernel,
        out_shape=jax.ShapeDtypeStruct((N, N), F32),
        grid=(1,),
        in_specs=[full(*plane), full(*plane), full(*unfold.shape)],
        out_specs=full(N, N),
        compiler_params=params(16),
        cost_estimate=cost(3 * 2 * HALF * 2 * ROWS * N, 2 << 20),
        name="join",
    )(best, got, unfold)
    return peak[None, None]


def solution(mesh):
    fine = Mesh(mesh.devices.reshape(2, 4, 4, 2, 2), DEF + BLK)
    in_specs = (P(DEF, BLK, None, None), P(BLK, DEF, None), P(DEF, BLK), P(), P(), P(), P())
    out_specs = P(DEF, BLK, None, None)
    return jax.shard_map(
        per_device, mesh=fine, in_specs=in_specs, out_specs=out_specs, check_vma=False
    )
```

```python
import math

import jax
import jax.numpy as jnp
import ml_dtypes
import numpy as np
from jax import lax
from jax.experimental import pallas as pl
from jax.experimental.pallas import tpu as pltpu
from jax.sharding import Mesh
from jax.sharding import PartitionSpec as P

DEF = ("xlo", "y")
BLK = ("z", "xhi", "core")
LIB = ("xlo", "y", "z")
N = 384
HALF = N // 2
THIRD = N // 3
BLOCKS = (64, 64, 72)
ROWS = sum(BLOCKS)
MARK = 16
FOLD = 208
ROOT = math.sqrt(3.0) / 2.0
F32 = jnp.float32
BF16 = jnp.bfloat16


def tables():
    j = np.arange(N)
    phase = (j[:, None] * j[None, :]) % N
    cos = np.cos(2.0 * np.pi * phase / N)
    sin = np.sin(2.0 * np.pi * phase / N)
    bf = ml_dtypes.bfloat16
    u = np.concatenate([3 * np.arange(b) + c for c, b in zip((1, 2, 0), BLOCKS)])
    keep = (u <= HALF)[:, None]
    u = np.minimum(u, HALF)
    r = np.arange(THIRD)
    b1, b2 = BLOCKS[0], BLOCKS[0] + BLOCKS[1]
    real = np.concatenate([(keep * cos[u])[b2:, r], (keep * -sin[u])[b2:, r]])
    c1, s1 = cos[u[:b1]][:, r], sin[u[:b1]][:, r]
    c2, s2 = cos[u[b1:b2]][:, r], sin[u[b1:b2]][:, r]
    pair = np.block([[c1, s1], [c2, -s2], [-s1, c1], [-s2, -c2]])
    ahead, back = [], []
    for k in range(3):
        ck = cos[r][:, 3 * r + k]
        sk = sin[r][:, 3 * r + k]
        ahead.append(np.block([[ck, -sk], [sk, ck]]))
        back.append(np.block([[ck.T, sk.T], [-sk.T, ck.T]]))
    ahead, back = np.stack(ahead), np.stack(back)
    weight = np.where((u == 0) | (u == HALF), 1.0, 2.0) * keep[:, 0]
    fold = np.zeros((2, ROWS, ROWS))
    fold[0, : HALF + 1] = cos[: HALF + 1][:, u].astype(bf).astype(float) * weight
    fold[1, : HALF + 1] = sin[: HALF + 1][:, u].astype(bf).astype(float) * weight
    unfold = np.zeros((HALF, 2 * ROWS))
    unfold[0, HALF] = 1.0
    for i in range(1, HALF):
        unfold[i, ROWS + HALF - i] = 1.0
    ahead_all = np.concatenate([ahead.reshape(-1, 2 * THIRD), pair, np.pad(real, ((0, 0), (0, THIRD)))])
    pad = ((0, 0), (0, FOLD - ROWS), (0, 2 * THIRD - ROWS))
    back_all = np.concatenate([back.reshape(-1, 2 * THIRD), np.pad(fold, pad).reshape(-1, 2 * THIRD)])
    return [jnp.asarray(a.astype(bf)) for a in (ahead_all, back_all, unfold)]


def dot(a, b):
    return jnp.dot(a, b, preferred_element_type=F32)


def row_numbers():
    i = lax.broadcasted_iota(jnp.int32, (ROWS, N), 0)
    k = lax.broadcasted_iota(jnp.int32, (ROWS, N), 1)
    b1, b2 = BLOCKS[0], BLOCKS[0] + BLOCKS[1]
    u = jnp.where(i < b1, 3 * i + 1, jnp.where(i < b2, 3 * (i - b1) + 2, 3 * (i - b2)))
    v = jnp.where(
        k < THIRD, 3 * k, jnp.where(k < 2 * THIRD, 3 * (k - THIRD) + 1, 3 * (k - 2 * THIRD) + 2)
    )
    return u, v


def row_scale(u):
    return jnp.where((u > 0) & (u < HALF), 2.0, jnp.where(u <= HALF, 1.0, 0.0))


def spread(block_ref, out_ref, sems):
    moves = [
        pltpu.make_async_copy(block_ref, out_ref.at[i], sems.at[i]) for i in range(out_ref.shape[0])
    ]
    for move in moves:
        move.start()
    for move in moves:
        move.wait()


def sine(x):
    x = x - jnp.round(x)
    a = jnp.abs(x)
    a = jnp.minimum(a, 0.5 - a)
    s = a * a
    p = jnp.full_like(x, -15.0946425768229800)
    for c in (
        42.0586939448600400,
        -76.7058597530613900,
        81.6052492760750400,
        -41.3417022403997600,
        6.28318530717958648,
    ):
        p = p * s + c
    p = p * a
    return jnp.where(x < 0.0, -p, p)


def half_spectrum(image, tab):
    wide = 2 * THIRD
    pair, real = tab[3 * wide : 4 * wide, :], tab[4 * wide :, :THIRD]
    image = image.astype(F32)
    x0, x1, x2 = image[:THIRD], image[THIRD : 2 * THIRD], image[2 * THIRD :]
    plus, minus = x1 + x2, x1 - x2
    f0 = (x0 + plus).astype(BF16)
    f1 = jnp.concatenate([(x0 - 0.5 * plus).astype(BF16), (-ROOT * minus).astype(BF16)], axis=0)
    low = dot(real, f0)
    high = dot(pair, f1)
    b, c = BLOCKS[0] + BLOCKS[1], BLOCKS[2]
    re = jnp.concatenate([high[:b], low[:c]], axis=0)
    im = jnp.concatenate([high[b:], low[c:]], axis=0)
    r0, r1, r2 = re[:, :THIRD], re[:, THIRD : 2 * THIRD], re[:, 2 * THIRD :]
    i0, i1, i2 = im[:, :THIRD], im[:, THIRD : 2 * THIRD], im[:, 2 * THIRD :]
    rp, rm = r1 + r2, ROOT * (r1 - r2)
    ip, im_ = i1 + i2, ROOT * (i1 - i2)
    rh, ih = r0 - 0.5 * rp, i0 - 0.5 * ip
    parts = ((r0 + rp, i0 + ip), (rh + im_, ih - rm), (rh - im_, ih + rm))
    result = []
    for k, (a, b) in enumerate(parts):
        lhs = jnp.concatenate([a.astype(BF16), b.astype(BF16)], axis=1)
        out = dot(lhs, tab[k * wide : (k + 1) * wide, :])
        result.append((out[:, :THIRD], out[:, THIRD:]))
    return result


def store_spectrum(ref, parts):
    for k, (re, im) in enumerate(parts):
        at = slice(k * THIRD, (k + 1) * THIRD)
        ref[0, :, at] = re.astype(ref.dtype)
        ref[1, :, at] = im.astype(ref.dtype)


def own_kernel(row_ref, image_ref, tab_ref, spec_ref, power_ref, sent_ref):
    sent_ref[:N] = image_ref[...]
    sent_ref[N:] = jnp.full((MARK, N), row_ref[0, 0], jnp.int32).astype(F32).astype(BF16)
    parts = half_spectrum(image_ref[...].reshape(N, N), tab_ref)
    store_spectrum(spec_ref, parts)
    for k, (re, im) in enumerate(parts):
        power_ref[:, k * THIRD : (k + 1) * THIRD] = (re * re + im * im).astype(BF16)


def other_kernel(image_ref, tab_ref, spec_ref):
    store_spectrum(spec_ref, half_spectrum(image_ref[:N], tab_ref))


def library_kernel(image_ref, tab_ref, out_ref):
    store_spectrum(out_ref, half_spectrum(image_ref[...].reshape(N, N), tab_ref))


def gain_kernel(
    row_ref,
    d_ref,
    a_ref,
    x_ref,
    p_ref,
    mark_ref,
    own_ref,
    other_ref,
    spec_ref,
    weight_ref,
):
    u, v = row_numbers()
    scale = row_scale(u)
    row = jnp.where(u < HALF, u, u - N).astype(F32) * (1.0 / N)
    col = jnp.where(v < HALF, v, v - N).astype(F32) * (1.0 / N)
    radial = row * row + col * col
    stretch = row * row - col * col
    skew = 2.0 * row * col
    inner = (u > 0) & (u < HALF)
    turn = 1.0 / (2.0 * math.pi)
    mate = jnp.max(mark_ref[...].astype(F32)).astype(jnp.int32)
    for t, r in enumerate((row_ref[0, 0], mate)):
        base = (d_ref[r] * turn) * radial + (a_ref[r] * turn) * stretch + p_ref[r] * turn
        cross = (x_ref[r] * turn) * skew
        plus = -sine(base + cross)
        minus = -sine(base - cross)
        mirror = jnp.where(inner & (v == HALF), minus, plus)
        gain = 0.5 * (plus + mirror)
        source = own_ref if t == 0 else other_ref
        spec_ref[t, 0] = source[0] * gain
        spec_ref[t, 1] = source[1] * gain
        weight_ref[t] = (0.5 * scale) * (plus * plus + mirror * mirror)


def whiten_kernel(spec_ref, weight_ref, mine_ref, theirs_ref, spec_out, weight_out):
    u, _ = row_numbers()
    power = (mine_ref[...].astype(F32) + theirs_ref[...].astype(F32)) * (1.0 / 16.0)
    mean = jnp.sum(power * row_scale(u)) * (1.0 / (N * N))
    inverse_noise = 1.0 / (jnp.where(u <= HALF, power, 1.0) + 0.05 * mean)
    for t in range(2):
        spec_out[t, 0] = spec_ref[t, 0] * inverse_noise
        spec_out[t, 1] = spec_ref[t, 1] * inverse_noise
        weight_out[t] = weight_ref[t] * inverse_noise


def match_step(re, im, spec_ref, weight_ref, tab):
    wide = 2 * THIRD
    norm = jnp.sum((re * re + im * im) * weight_ref[...])
    scale = lax.rsqrt(jnp.full((1, THIRD), norm + 1e-06, F32))
    s_re, s_im = spec_ref[0], spec_ref[1]
    p_re = (s_re * re + s_im * im).astype(BF16)
    p_im = (s_im * re - s_re * im).astype(BF16)
    g = []
    for k in range(3):
        at = slice(k * THIRD, (k + 1) * THIRD)
        lhs = jnp.concatenate([p_re[:, at], p_im[:, at]], axis=1)
        g.append(dot(lhs, tab[k * wide : (k + 1) * wide, :]))
    (r0, i0), (r1, i1), (r2, i2) = ((x[:, :THIRD], x[:, THIRD:]) for x in g)
    slant = scale * ROOT
    rp, rm = r1 + r2, slant * (r1 - r2)
    ip, im_ = i1 + i2, slant * (i1 - i2)
    rh, ih = scale * (r0 - 0.5 * rp), scale * (i0 - 0.5 * ip)
    h_re = [scale * (r0 + rp), rh - im_, rh + im_]
    h_im = [scale * (i0 + ip), ih + rm, ih - rm]
    h_re = jnp.concatenate([h.astype(BF16) for h in h_re], axis=1)
    h_im = jnp.concatenate([h.astype(BF16) for h in h_im], axis=1)
    first = 3 * wide
    even = dot(tab[first : first + ROWS, :ROWS], h_re)
    odd = dot(tab[first + FOLD : first + FOLD + ROWS, :ROWS], h_im)
    return even - odd, even + odd


def match_kernel(near_ref, far_ref, spec_ref, weight_ref, tab_ref, out_ref, best_sc):
    step = pl.program_id(0)

    @pl.when(step == 0)
    def _():
        best_sc[...] = jnp.full_like(best_sc, -jnp.inf)

    pairs = [
        match_step(ref[0].astype(F32), ref[1].astype(F32), spec_ref, weight_ref, tab_ref)
        for ref in (near_ref, far_ref)
    ]
    for side in range(2):
        best_sc[side] = jnp.maximum(best_sc[side], jnp.maximum(pairs[0][side], pairs[1][side]))

    @pl.when(step == pl.num_programs(0) - 1)
    def _():
        out_ref[...] = best_sc[...].astype(out_ref.dtype)


def join_kernel(best_ref, got_ref, unfold_ref, out_ref):
    best = jnp.maximum(best_ref[...], got_ref[...].astype(F32))
    out_ref[:HALF] = best[0, :HALF]
    rest = best.reshape(2 * ROWS, N)
    total = None
    for _ in range(3):
        part = rest.astype(BF16)
        rest = rest - part.astype(F32)
        moved = dot(unfold_ref[...], part)
        total = moved if total is None else total + moved
    out_ref[HALF:] = total


def full(*shape):
    return pl.BlockSpec(shape, lambda i: (0,) * len(shape))


def smem(count):
    return [pl.BlockSpec(memory_space=pltpu.SMEM)] * count


def cost(flops, size):
    return pl.CostEstimate(flops=flops, bytes_accessed=size, transcendentals=0)


def params(mib):
    return pltpu.CompilerParams(vmem_limit_bytes=mib << 20)


def per_device(images, projections, ctf_row, defocus_term, astig_term, astig_cross, phase_shift):
    ahead, back, unfold = tables()
    groups = math.prod(lax.axis_size(a) for a in DEF)
    places = math.prod(lax.axis_size(a) for a in LIB)
    deep, wide = lax.axis_size("z"), lax.axis_size("xhi")
    core = lax.axis_index("core")
    swap = [(0, 1), (1, 0)]
    plane = (2, ROWS, N)
    work = 2 * ROWS * 768 * 256 * 2

    tile = images[0, 0]
    block = projections[0]
    copies = pl.pallas_call(
        spread,
        out_shape=pltpu.HBM((places,) + block.shape, BF16),
        grid=(1,),
        in_specs=[full(*block.shape)],
        out_specs=pl.BlockSpec(memory_space=pltpu.HBM),
        scratch_shapes=[pltpu.SemaphoreType.DMA((places,))],
        cost_estimate=cost(0, 1 << 20),
        name="copies",
    )(block)
    images_all = lax.all_to_all(copies, LIB, 0, 0, tiled=False)

    own, power, sent = pl.pallas_call(
        own_kernel,
        out_shape=[
            jax.ShapeDtypeStruct(plane, F32),
            jax.ShapeDtypeStruct((ROWS, N), BF16),
            jax.ShapeDtypeStruct((N + MARK, N), BF16),
        ],
        grid=(1,),
        in_specs=smem(1) + [full(N, N), full(*ahead.shape)],
        out_specs=[full(*plane), full(ROWS, N), full(N + MARK, N)],
        compiler_params=params(16),
        cost_estimate=cost(work, 2 << 20),
        name="own_tile",
    )(ctf_row, tile, ahead)
    received = lax.ppermute(sent, "xhi", swap)
    other = pl.pallas_call(
        other_kernel,
        out_shape=jax.ShapeDtypeStruct(plane, F32),
        grid=(1,),
        in_specs=[full(N + MARK, N), full(*ahead.shape)],
        out_specs=full(*plane),
        compiler_params=params(16),
        cost_estimate=cost(work, 2 << 20),
        name="other_tile",
    )(received, ahead)

    beside = lax.ppermute(power, "core", swap)
    pair = (power.astype(F32) + beside.astype(F32)).astype(BF16)
    sums = jnp.where(core == 0, pair.astype(F32), 0.0)
    for dz in range(deep):
        perm = [
            ((z * wide + x) * 2 + c, ((z + dz) % deep * wide + (x ^ c)) * 2 + c)
            for z in range(deep)
            for x in range(wide)
            for c in range(2)
            if dz or c
        ]
        sums = sums + lax.ppermute(pair, BLK, perm).astype(F32)
    mine = sums.astype(BF16)

    spec, weight = pl.pallas_call(
        gain_kernel,
        out_shape=[jax.ShapeDtypeStruct((2,) + plane, F32), jax.ShapeDtypeStruct(plane, F32)],
        grid=(1,),
        in_specs=smem(5)
        + [pl.BlockSpec((MARK, N), lambda i: (N // MARK, 0))]
        + [full(*plane)] * 2,
        out_specs=[full(2, *plane), full(*plane)],
        compiler_params=params(20),
        cost_estimate=cost(2 * ROWS * N * 60, 4 << 20),
        name="gain",
    )(ctf_row, defocus_term, astig_term, astig_cross, phase_shift, received, own, other)

    images_all, mine, spec = lax.optimization_barrier((images_all, mine, spec))

    near_all = pl.pallas_call(
        library_kernel,
        out_shape=jax.ShapeDtypeStruct((deep,) + plane, BF16),
        grid=(deep,),
        in_specs=[
            pl.BlockSpec((groups, None, N // groups, N), lambda i: (0, i, 0, 0)),
            full(*ahead.shape),
        ],
        out_specs=pl.BlockSpec((None,) + plane, lambda i: (i, 0, 0, 0)),
        compiler_params=params(16),
        cost_estimate=cost(deep * work, 4 << 20),
        name="library",
    )(images_all.reshape(groups, deep, N // groups, N), ahead)
    far_all = lax.ppermute(near_all, "core", swap)
    theirs = lax.ppermute(mine, "core", swap)

    white, white_weight = pl.pallas_call(
        whiten_kernel,
        out_shape=[jax.ShapeDtypeStruct((2,) + plane, F32), jax.ShapeDtypeStruct(plane, F32)],
        grid=(1,),
        in_specs=[full(2, *plane), full(*plane), full(ROWS, N), full(ROWS, N)],
        out_specs=[full(2, *plane), full(*plane)],
        compiler_params=params(20),
        cost_estimate=cost(2 * ROWS * N * 4, 4 << 20),
        name="whiten",
    )(spec, weight, mine, theirs)

    def match(t, dtype, name):
        lib_spec = pl.BlockSpec((None,) + plane, lambda i: (i, 0, 0, 0))
        return pl.pallas_call(
            match_kernel,
            out_shape=jax.ShapeDtypeStruct(plane, dtype),
            grid=(deep,),
            in_specs=[
                lib_spec,
                lib_spec,
                pl.BlockSpec((None,) + plane, lambda i: (t, 0, 0, 0)),
                pl.BlockSpec((None, ROWS, N), lambda i: (t, 0, 0)),
                full(*back.shape),
            ],
            out_specs=full(*plane),
            scratch_shapes=[pltpu.VMEM(plane, F32)],
            compiler_params=params(20),
            cost_estimate=cost(2 * deep * 2 * work, 6 << 20),
            name=name,
        )(near_all, far_all, white, white_weight, back)

    got = lax.ppermute(match(1, BF16, "match_other"), "xhi", swap)
    best = match(0, F32, "match_own")
    peak = pl.pallas_call(
        join_kernel,
        out_shape=jax.ShapeDtypeStruct((N, N), F32),
        grid=(1,),
        in_specs=[full(*plane), full(*plane), full(*unfold.shape)],
        out_specs=full(N, N),
        compiler_params=params(16),
        cost_estimate=cost(3 * 2 * HALF * 2 * ROWS * N, 2 << 20),
        name="join",
    )(best, got, unfold)
    return peak[None, None]


def solution(mesh):
    fine = Mesh(mesh.devices.reshape(2, 4, 4, 2, 2), DEF + BLK)
    in_specs = (P(DEF, BLK, None, None), P(BLK, DEF, None), P(DEF, BLK), P(), P(), P(), P())
    out_specs = P(DEF, BLK, None, None)
    return jax.shard_map(
        per_device, mesh=fine, in_specs=in_specs, out_specs=out_specs, check_vma=False
    )
```

```python
import math

import jax
import jax.numpy as jnp
import ml_dtypes
import numpy as np
from jax import lax
from jax.experimental import pallas as pl
from jax.experimental.pallas import tpu as pltpu
from jax.sharding import Mesh
from jax.sharding import PartitionSpec as P

DEF = ("xlo", "y")
BLK = ("z", "xhi", "core")
LIB = ("xlo", "y", "z")
N = 384
HALF = N // 2
THIRD = N // 3
BLOCKS = (64, 64, 72)
ROWS = sum(BLOCKS)
SPLIT = 96
PART = ROWS - SPLIT
FOLD = 208
ROOT = math.sqrt(3.0) / 2.0
F32 = jnp.float32
BF16 = jnp.bfloat16


def tables():
    j = np.arange(N)
    phase = (j[:, None] * j[None, :]) % N
    cos = np.cos(2.0 * np.pi * phase / N)
    sin = np.sin(2.0 * np.pi * phase / N)
    bf = ml_dtypes.bfloat16
    u = np.concatenate([3 * np.arange(b) + c for c, b in zip((1, 2, 0), BLOCKS)])
    keep = (u <= HALF)[:, None]
    u = np.minimum(u, HALF)
    r = np.arange(THIRD)
    b1, b2 = BLOCKS[0], BLOCKS[0] + BLOCKS[1]
    real = np.concatenate([(keep * cos[u])[b2:, r], (keep * -sin[u])[b2:, r]])
    c1, s1 = cos[u[:b1]][:, r], sin[u[:b1]][:, r]
    c2, s2 = cos[u[b1:b2]][:, r], sin[u[b1:b2]][:, r]
    pair = np.block([[c1, s1], [c2, -s2], [-s1, c1], [-s2, -c2]])
    ahead, back = [], []
    for k in range(3):
        ck = cos[r][:, 3 * r + k]
        sk = sin[r][:, 3 * r + k]
        ahead.append(np.block([[ck, -sk], [sk, ck]]))
        back.append(np.block([[ck.T, sk.T], [-sk.T, ck.T]]))
    ahead, back = np.stack(ahead), np.stack(back)
    weight = np.where((u == 0) | (u == HALF), 1.0, 2.0) * keep[:, 0]
    fold = np.zeros((2, ROWS, ROWS))
    fold[0, : HALF + 1] = cos[: HALF + 1][:, u].astype(bf).astype(float) * weight
    fold[1, : HALF + 1] = sin[: HALF + 1][:, u].astype(bf).astype(float) * weight
    unfold = np.zeros((HALF, 2 * ROWS))
    unfold[0, HALF] = 1.0
    for i in range(1, HALF):
        unfold[i, ROWS + HALF - i] = 1.0
    ahead_all = np.concatenate([ahead.reshape(-1, 2 * THIRD), pair, np.pad(real, ((0, 0), (0, THIRD)))])
    pad = ((0, 0), (0, FOLD - ROWS), (0, 2 * THIRD - ROWS))
    back_all = np.concatenate([back.reshape(-1, 2 * THIRD), np.pad(fold, pad).reshape(-1, 2 * THIRD)])
    return [jnp.asarray(a.astype(bf)) for a in (ahead_all, back_all, unfold)]


def dot(a, b):
    return jnp.dot(a, b, preferred_element_type=F32)


def row_numbers():
    i = lax.broadcasted_iota(jnp.int32, (ROWS, N), 0)
    k = lax.broadcasted_iota(jnp.int32, (ROWS, N), 1)
    b1, b2 = BLOCKS[0], BLOCKS[0] + BLOCKS[1]
    u = jnp.where(i < b1, 3 * i + 1, jnp.where(i < b2, 3 * (i - b1) + 2, 3 * (i - b2)))
    v = jnp.where(
        k < THIRD, 3 * k, jnp.where(k < 2 * THIRD, 3 * (k - THIRD) + 1, 3 * (k - 2 * THIRD) + 2)
    )
    return u, v


def row_scale(u):
    return jnp.where((u > 0) & (u < HALF), 2.0, jnp.where(u <= HALF, 1.0, 0.0))


def copy_kernel(block_ref, out_ref, wide_sc, sems):
    count = wide_sc.shape[0]
    wide_sc[...] = jnp.broadcast_to(block_ref[...][None], wide_sc.shape)
    moves = [
        pltpu.make_async_copy(wide_sc, out_ref.at[pl.ds(i * count, count)], sems.at[i])
        for i in range(out_ref.shape[0] // count)
    ]
    for move in moves:
        move.start()
    for move in moves:
        move.wait()


def sine(x):
    x = x - jnp.round(x)
    a = jnp.abs(x)
    a = jnp.minimum(a, 0.5 - a)
    s = a * a
    p = jnp.full_like(x, -15.0946425768229800)
    for c in (
        42.0586939448600400,
        -76.7058597530613900,
        81.6052492760750400,
        -41.3417022403997600,
        6.28318530717958648,
    ):
        p = p * s + c
    p = p * a
    return jnp.where(x < 0.0, -p, p)


def half_spectrum(image, tab):
    wide = 2 * THIRD
    pair, real = tab[3 * wide : 4 * wide, :], tab[4 * wide :, :THIRD]
    image = image.astype(F32)
    x0, x1, x2 = image[:THIRD], image[THIRD : 2 * THIRD], image[2 * THIRD :]
    plus, minus = x1 + x2, x1 - x2
    f0 = (x0 + plus).astype(BF16)
    f1 = jnp.concatenate([(x0 - 0.5 * plus).astype(BF16), (-ROOT * minus).astype(BF16)], axis=0)
    low = dot(real, f0)
    high = dot(pair, f1)
    b, c = BLOCKS[0] + BLOCKS[1], BLOCKS[2]
    re = jnp.concatenate([high[:b], low[:c]], axis=0)
    im = jnp.concatenate([high[b:], low[c:]], axis=0)
    r0, r1, r2 = re[:, :THIRD], re[:, THIRD : 2 * THIRD], re[:, 2 * THIRD :]
    i0, i1, i2 = im[:, :THIRD], im[:, THIRD : 2 * THIRD], im[:, 2 * THIRD :]
    rp, rm = r1 + r2, ROOT * (r1 - r2)
    ip, im_ = i1 + i2, ROOT * (i1 - i2)
    rh, ih = r0 - 0.5 * rp, i0 - 0.5 * ip
    parts = ((r0 + rp, i0 + ip), (rh + im_, ih - rm), (rh - im_, ih + rm))
    result = []
    for k, (a, b) in enumerate(parts):
        lhs = jnp.concatenate([a.astype(BF16), b.astype(BF16)], axis=1)
        out = dot(lhs, tab[k * wide : (k + 1) * wide, :])
        result.append((out[:, :THIRD], out[:, THIRD:]))
    return result


def store_spectrum(ref, parts):
    for k, (re, im) in enumerate(parts):
        at = slice(k * THIRD, (k + 1) * THIRD)
        ref[0, :, at] = re.astype(ref.dtype)
        ref[1, :, at] = im.astype(ref.dtype)


def ctf_factors(row, table):
    lane = lax.broadcasted_iota(jnp.int32, table.shape, 1).astype(F32)
    chosen = jnp.sum(jnp.where(lane == row, table, 0.0), axis=1, keepdims=True)
    chosen = chosen * (1.0 / (2.0 * math.pi))
    u, v = row_numbers()
    row = jnp.where(u < HALF, u, u - N).astype(F32) * (1.0 / N)
    col = jnp.where(v < HALF, v, v - N).astype(F32) * (1.0 / N)
    r2, c2 = row * row, col * col
    base = chosen[0:1] * (r2 + c2) + chosen[1:2] * (r2 - c2) + chosen[3:4]
    cross = chosen[2:3] * (2.0 * row * col)
    plus = -sine(base + cross)
    at = slice(0, THIRD)
    inner = (u[:, at] > 0) & (u[:, at] < HALF) & (v[:, at] == HALF)
    mirror = jnp.where(inner, -sine(base[:, at] - cross[:, at]), plus[:, at])
    gain = jnp.concatenate([0.5 * (plus[:, at] + mirror), plus[:, THIRD:]], axis=1)
    square = plus * plus
    square = jnp.concatenate(
        [0.5 * (square[:, at] + mirror * mirror), square[:, THIRD:]], axis=1
    )
    return gain, row_scale(u) * square


def tile_kernel(core_ref, mate_ref, own_ref, other_ref, tab_ref, spec_ref, keep_ref, send_ref, power_sc):
    parts = half_spectrum(own_ref[...], tab_ref)
    store_spectrum(spec_ref.at[0], parts)
    for k, (re, im) in enumerate(parts):
        power_sc[:, k * THIRD : (k + 1) * THIRD] = re * re + im * im
    low, high = power_sc[:PART], power_sc[SPLIT:]
    first = core_ref[...] == 0
    keep_ref[...] = jnp.where(first, low, high).astype(BF16)
    send_ref[...] = jnp.where(first, high, low).astype(BF16)
    store_spectrum(spec_ref.at[1], half_spectrum(other_ref[...], tab_ref))


def gain_kernel(row_ref, mate_ref, table_ref, tile_ref, spec_ref, weight_ref):
    for t, ref in enumerate((row_ref, mate_ref)):
        gain, weight_ref[t] = ctf_factors(ref[...].astype(F32), table_ref[...])
        spec_ref[t, 0] = tile_ref[t, 0] * gain
        spec_ref[t, 1] = tile_ref[t, 1] * gain


def library_kernel(image_ref, tab_ref, out_ref):
    store_spectrum(out_ref, half_spectrum(image_ref[...].reshape(N, N), tab_ref))


def match_step(re, im, spec_ref, weight_ref, tab):
    wide = 2 * THIRD
    norm = jnp.sum((re * re + im * im) * weight_ref[...])
    scale = lax.rsqrt(jnp.full((1, THIRD), norm + 1e-06, F32))
    s_re, s_im = spec_ref[0], spec_ref[1]
    p_re = (s_re * re + s_im * im).astype(BF16)
    p_im = (s_im * re - s_re * im).astype(BF16)
    g = []
    for k in range(3):
        at = slice(k * THIRD, (k + 1) * THIRD)
        lhs = jnp.concatenate([p_re[:, at], p_im[:, at]], axis=1)
        g.append(dot(lhs, tab[k * wide : (k + 1) * wide, :]))
    (r0, i0), (r1, i1), (r2, i2) = ((x[:, :THIRD], x[:, THIRD:]) for x in g)
    slant = scale * ROOT
    rp, rm = r1 + r2, slant * (r1 - r2)
    ip, im_ = i1 + i2, slant * (i1 - i2)
    rh, ih = scale * (r0 - 0.5 * rp), scale * (i0 - 0.5 * ip)
    h_re = [scale * (r0 + rp), rh - im_, rh + im_]
    h_im = [scale * (i0 + ip), ih + rm, ih - rm]
    h_re = jnp.concatenate([h.astype(BF16) for h in h_re], axis=1)
    h_im = jnp.concatenate([h.astype(BF16) for h in h_im], axis=1)
    first = 3 * wide
    even = dot(tab[first : first + ROWS, :ROWS], h_re)
    odd = dot(tab[first + FOLD : first + FOLD + ROWS, :ROWS], h_im)
    return even - odd, even + odd


def match_kernel(
    core_ref,
    near_ref,
    far_ref,
    spec_ref,
    weight_ref,
    mine_ref,
    theirs_ref,
    tab_ref,
    unfold_ref,
    out_ref,
    spec_sc,
    weight_sc,
    best_sc,
):
    step = pl.program_id(0)

    @pl.when(step == 0)
    def _():
        u, _ = row_numbers()
        mine, theirs = mine_ref[...].astype(F32), theirs_ref[...].astype(F32)
        first = core_ref[...] == 0
        low, high = jnp.where(first, mine, theirs), jnp.where(first, theirs, mine)
        power = jnp.concatenate([low[:SPLIT], high], axis=0) * (1.0 / 16.0)
        mean = jnp.sum(power * row_scale(u)) * (1.0 / (N * N))
        inverse_noise = 1.0 / (jnp.where(u <= HALF, power, 1.0) + 0.05 * mean)
        spec_sc[0] = spec_ref[0] * inverse_noise
        spec_sc[1] = spec_ref[1] * inverse_noise
        weight_sc[...] = weight_ref[...] * inverse_noise
        best_sc[...] = jnp.full_like(best_sc, -jnp.inf)

    pairs = [
        match_step(ref[0].astype(F32), ref[1].astype(F32), spec_sc, weight_sc, tab_ref)
        for ref in (near_ref, far_ref)
    ]
    for side in range(2):
        best_sc[side] = jnp.maximum(best_sc[side], jnp.maximum(pairs[0][side], pairs[1][side]))

    @pl.when(step == pl.num_programs(0) - 1)
    def _():
        out_ref[:HALF] = best_sc[0, :HALF].astype(out_ref.dtype)
        rest = best_sc[...].reshape(2 * ROWS, N)
        total = None
        for _ in range(3 if out_ref.dtype == F32 else 1):
            part = rest.astype(BF16)
            rest = rest - part.astype(F32)
            moved = dot(unfold_ref[...], part)
            total = moved if total is None else total + moved
        out_ref[HALF:] = total.astype(out_ref.dtype)


def join_kernel(best_ref, got_ref, out_ref):
    out_ref[...] = jnp.maximum(best_ref[...], got_ref[...].astype(F32))


def full(*shape):
    return pl.BlockSpec(shape, lambda i: (0,) * len(shape))


def cost(flops, size):
    return pl.CostEstimate(flops=flops, bytes_accessed=size, transcendentals=0)


def params(mib):
    return pltpu.CompilerParams(vmem_limit_bytes=mib << 20)


def per_device(images, projections, ctf_row, defocus_term, astig_term, astig_cross, phase_shift):
    ahead, back, unfold = tables()
    groups = math.prod(lax.axis_size(a) for a in DEF)
    places = math.prod(lax.axis_size(a) for a in LIB)
    deep, wide = lax.axis_size("z"), lax.axis_size("xhi")
    core = lax.axis_index("core").astype(jnp.int32).reshape(1, 1)
    swap = [(0, 1), (1, 0)]
    plane = (2, ROWS, N)
    work = 2 * ROWS * 768 * 256 * 2

    tile = images[0, 0]
    received = lax.ppermute(tile, "xhi", swap)
    mate = lax.ppermute(ctf_row, "xhi", swap)
    block = projections[0]
    copies = pl.pallas_call(
        copy_kernel,
        out_shape=pltpu.HBM((places,) + block.shape, BF16),
        grid=(1,),
        in_specs=[full(*block.shape)],
        out_specs=pl.BlockSpec(memory_space=pltpu.HBM),
        scratch_shapes=[
            pltpu.VMEM((groups,) + block.shape, BF16),
            pltpu.SemaphoreType.DMA((places // groups,)),
        ],
        cost_estimate=cost(0, 1 << 20),
        name="copies",
    )(block)
    images_all = lax.all_to_all(copies, LIB, 0, 0, tiled=False)

    tiles, keep, send = pl.pallas_call(
        tile_kernel,
        out_shape=[
            jax.ShapeDtypeStruct((2,) + plane, F32),
            jax.ShapeDtypeStruct((PART, N), BF16),
            jax.ShapeDtypeStruct((PART, N), BF16),
        ],
        grid=(1,),
        in_specs=[full(1, 1), full(1, 1), full(N, N), full(N, N), full(*ahead.shape)],
        out_specs=[full(2, *plane), full(PART, N), full(PART, N)],
        scratch_shapes=[pltpu.VMEM((ROWS, N), F32)],
        compiler_params=params(16),
        cost_estimate=cost(200 * work, 3 << 20),
        name="tile",
    )(core, mate, tile, received, ahead)

    pair = (keep.astype(F32) + lax.ppermute(send, "core", swap).astype(F32)).astype(BF16)
    sums = pair.astype(F32)
    for dz in range(1, deep):
        moved = lax.ppermute(pair, "z", [(z, (z + dz) % deep) for z in range(deep)])
        sums = sums + moved.astype(F32)
    sums = sums.astype(BF16)

    table = jnp.stack([defocus_term, astig_term, astig_cross, phase_shift])
    table = jnp.pad(table, ((0, 4), (0, 128 - table.shape[1])))
    spec, weight = pl.pallas_call(
        gain_kernel,
        out_shape=[
            jax.ShapeDtypeStruct((2,) + plane, F32),
            jax.ShapeDtypeStruct((2, ROWS, N), F32),
        ],
        grid=(1,),
        in_specs=[full(1, 1), full(1, 1), full(*table.shape), full(2, *plane)],
        out_specs=[full(2, *plane), full(2, ROWS, N)],
        compiler_params=params(20),
        cost_estimate=cost(2 * ROWS * N * 60, 4 << 20),
        name="gain",
    )(ctf_row, mate, table, tiles)

    images_all, sums, spec = lax.optimization_barrier((images_all, sums, spec))
    across = lax.ppermute(sums, "xhi", swap)
    mine = (sums.astype(F32) + across.astype(F32)).astype(BF16)
    theirs = lax.ppermute(mine, "core", swap)

    near_all = pl.pallas_call(
        library_kernel,
        out_shape=jax.ShapeDtypeStruct((deep,) + plane, BF16),
        grid=(deep,),
        in_specs=[
            pl.BlockSpec((groups, None, N // groups, N), lambda i: (0, i, 0, 0)),
            full(*ahead.shape),
        ],
        out_specs=pl.BlockSpec((None,) + plane, lambda i: (i, 0, 0, 0)),
        compiler_params=params(16),
        cost_estimate=cost(100 * deep * work, 4 << 20),
        name="library",
    )(images_all.reshape(groups, deep, N // groups, N), ahead)
    far_all = lax.ppermute(near_all, "core", swap)
    def match(t, dtype, name):
        lib_spec = pl.BlockSpec((None,) + plane, lambda i: (i, 0, 0, 0))
        return pl.pallas_call(
            match_kernel,
            out_shape=jax.ShapeDtypeStruct((N, N), dtype),
            grid=(deep,),
            in_specs=[
                full(1, 1),
                lib_spec,
                lib_spec,
                pl.BlockSpec((None,) + plane, lambda i: (t, 0, 0, 0)),
                pl.BlockSpec((None, ROWS, N), lambda i: (t, 0, 0)),
                full(PART, N),
                full(PART, N),
                full(*back.shape),
                full(*unfold.shape),
            ],
            out_specs=full(N, N),
            scratch_shapes=[
                pltpu.VMEM(plane, F32),
                pltpu.VMEM((ROWS, N), F32),
                pltpu.VMEM(plane, F32),
            ],
            compiler_params=params(20),
            cost_estimate=cost(2 * deep * 2 * work, 6 << 20),
            name=name,
        )(core, near_all, far_all, spec, weight, mine, theirs, back, unfold)

    got = lax.ppermute(match(1, BF16, "match_other"), "xhi", swap)
    best = match(0, F32, "match_own")
    peak = pl.pallas_call(
        join_kernel,
        out_shape=jax.ShapeDtypeStruct((N, N), F32),
        grid=(1,),
        in_specs=[full(N, N), full(N, N)],
        out_specs=full(N, N),
        cost_estimate=cost(N * N, 1 << 20),
        name="join",
    )(best, got)
    return peak[None, None]


def solution(mesh):
    fine = Mesh(mesh.devices.reshape(2, 4, 4, 2, 2), DEF + BLK)
    in_specs = (P(DEF, BLK, None, None), P(BLK, DEF, None), P(DEF, BLK), P(), P(), P(), P())
    out_specs = P(DEF, BLK, None, None)
    return jax.shard_map(
        per_device, mesh=fine, in_specs=in_specs, out_specs=out_specs, check_vma=False
    )
```

```python
import math

import jax
import jax.numpy as jnp
import ml_dtypes
import numpy as np
from jax import lax
from jax.experimental import pallas as pl
from jax.experimental.pallas import tpu as pltpu
from jax.sharding import Mesh
from jax.sharding import PartitionSpec as P

DEF = ("xlo", "y")
BLK = ("z", "xhi", "core")
LIB = ("xlo", "y", "z")
N = 384
HALF = N // 2
THIRD = N // 3
BLOCKS = (64, 64, 72)
ROWS = sum(BLOCKS)
SPLIT = 96
PART = ROWS - SPLIT
FOLD = 208
ROOT = math.sqrt(3.0) / 2.0
F32 = jnp.float32
BF16 = jnp.bfloat16


def tables():
    j = np.arange(N)
    phase = (j[:, None] * j[None, :]) % N
    cos = np.cos(2.0 * np.pi * phase / N)
    sin = np.sin(2.0 * np.pi * phase / N)
    bf = ml_dtypes.bfloat16
    u = np.concatenate([3 * np.arange(b) + c for c, b in zip((1, 2, 0), BLOCKS)])
    keep = (u <= HALF)[:, None]
    u = np.minimum(u, HALF)
    r = np.arange(THIRD)
    b1, b2 = BLOCKS[0], BLOCKS[0] + BLOCKS[1]
    real = np.concatenate([(keep * cos[u])[b2:, r], (keep * -sin[u])[b2:, r]])
    c1, s1 = cos[u[:b1]][:, r], sin[u[:b1]][:, r]
    c2, s2 = cos[u[b1:b2]][:, r], sin[u[b1:b2]][:, r]
    pair = np.block([[c1, s1], [c2, -s2], [-s1, c1], [-s2, -c2]])
    ahead, back = [], []
    for k in range(3):
        ck = cos[r][:, 3 * r + k]
        sk = sin[r][:, 3 * r + k]
        ahead.append(np.block([[ck, -sk], [sk, ck]]))
        back.append(np.block([[ck.T, sk.T], [-sk.T, ck.T]]))
    ahead, back = np.stack(ahead), np.stack(back)
    weight = np.where((u == 0) | (u == HALF), 1.0, 2.0) * keep[:, 0]
    fold = np.zeros((2, ROWS, ROWS))
    fold[0, : HALF + 1] = cos[: HALF + 1][:, u].astype(bf).astype(float) * weight
    fold[1, : HALF + 1] = sin[: HALF + 1][:, u].astype(bf).astype(float) * weight
    unfold = np.zeros((HALF, 2 * ROWS))
    unfold[0, HALF] = 1.0
    for i in range(1, HALF):
        unfold[i, ROWS + HALF - i] = 1.0
    ahead_all = np.concatenate([ahead.reshape(-1, 2 * THIRD), pair, np.pad(real, ((0, 0), (0, THIRD)))])
    pad = ((0, 0), (0, FOLD - ROWS), (0, 2 * THIRD - ROWS))
    back_all = np.concatenate([back.reshape(-1, 2 * THIRD), np.pad(fold, pad).reshape(-1, 2 * THIRD)])
    return [jnp.asarray(a.astype(bf)) for a in (ahead_all, back_all, unfold)]


def dot(a, b):
    return jnp.dot(a, b, preferred_element_type=F32)


def row_numbers():
    i = lax.broadcasted_iota(jnp.int32, (ROWS, N), 0)
    k = lax.broadcasted_iota(jnp.int32, (ROWS, N), 1)
    b1, b2 = BLOCKS[0], BLOCKS[0] + BLOCKS[1]
    u = jnp.where(i < b1, 3 * i + 1, jnp.where(i < b2, 3 * (i - b1) + 2, 3 * (i - b2)))
    v = jnp.where(
        k < THIRD, 3 * k, jnp.where(k < 2 * THIRD, 3 * (k - THIRD) + 1, 3 * (k - 2 * THIRD) + 2)
    )
    return u, v


def row_scale(u):
    return jnp.where((u > 0) & (u < HALF), 2.0, jnp.where(u <= HALF, 1.0, 0.0))


def copy_kernel(block_ref, out_ref, wide_sc, sems):
    count = wide_sc.shape[0]
    wide_sc[...] = jnp.broadcast_to(block_ref[...][None], wide_sc.shape)
    moves = [
        pltpu.make_async_copy(wide_sc, out_ref.at[pl.ds(i * count, count)], sems.at[i])
        for i in range(out_ref.shape[0] // count)
    ]
    for move in moves:
        move.start()
    for move in moves:
        move.wait()


def sine(x):
    x = x - jnp.round(x)
    a = jnp.abs(x)
    a = jnp.minimum(a, 0.5 - a)
    s = a * a
    p = jnp.full_like(x, -15.0946425768229800)
    for c in (
        42.0586939448600400,
        -76.7058597530613900,
        81.6052492760750400,
        -41.3417022403997600,
        6.28318530717958648,
    ):
        p = p * s + c
    p = p * a
    return jnp.where(x < 0.0, -p, p)


def half_spectrum(image, tab):
    wide = 2 * THIRD
    pair, real = tab[3 * wide : 4 * wide, :], tab[4 * wide :, :THIRD]
    image = image.astype(F32)
    x0, x1, x2 = image[:THIRD], image[THIRD : 2 * THIRD], image[2 * THIRD :]
    plus, minus = x1 + x2, x1 - x2
    f0 = (x0 + plus).astype(BF16)
    f1 = jnp.concatenate([(x0 - 0.5 * plus).astype(BF16), (-ROOT * minus).astype(BF16)], axis=0)
    low = dot(real, f0)
    high = dot(pair, f1)
    b, c = BLOCKS[0] + BLOCKS[1], BLOCKS[2]
    re = jnp.concatenate([high[:b], low[:c]], axis=0)
    im = jnp.concatenate([high[b:], low[c:]], axis=0)
    r0, r1, r2 = re[:, :THIRD], re[:, THIRD : 2 * THIRD], re[:, 2 * THIRD :]
    i0, i1, i2 = im[:, :THIRD], im[:, THIRD : 2 * THIRD], im[:, 2 * THIRD :]
    rp, rm = r1 + r2, ROOT * (r1 - r2)
    ip, im_ = i1 + i2, ROOT * (i1 - i2)
    rh, ih = r0 - 0.5 * rp, i0 - 0.5 * ip
    parts = ((r0 + rp, i0 + ip), (rh + im_, ih - rm), (rh - im_, ih + rm))
    result = []
    for k, (a, b) in enumerate(parts):
        lhs = jnp.concatenate([a.astype(BF16), b.astype(BF16)], axis=1)
        out = dot(lhs, tab[k * wide : (k + 1) * wide, :])
        result.append((out[:, :THIRD], out[:, THIRD:]))
    return result


def store_spectrum(ref, parts):
    for k, (re, im) in enumerate(parts):
        at = slice(k * THIRD, (k + 1) * THIRD)
        ref[0, :, at] = re.astype(ref.dtype)
        ref[1, :, at] = im.astype(ref.dtype)


def ctf_factors(row, table):
    lane = lax.broadcasted_iota(jnp.int32, table.shape, 1).astype(F32)
    chosen = jnp.sum(jnp.where(lane == row, table, 0.0), axis=1, keepdims=True)
    chosen = chosen * (1.0 / (2.0 * math.pi))
    u, v = row_numbers()
    row = jnp.where(u < HALF, u, u - N).astype(F32) * (1.0 / N)
    col = jnp.where(v < HALF, v, v - N).astype(F32) * (1.0 / N)
    r2, c2 = row * row, col * col
    base = chosen[0:1] * (r2 + c2) + chosen[1:2] * (r2 - c2) + chosen[3:4]
    cross = chosen[2:3] * (2.0 * row * col)
    plus = -sine(base + cross)
    at = slice(0, THIRD)
    inner = (u[:, at] > 0) & (u[:, at] < HALF) & (v[:, at] == HALF)
    mirror = jnp.where(inner, -sine(base[:, at] - cross[:, at]), plus[:, at])
    gain = jnp.concatenate([0.5 * (plus[:, at] + mirror), plus[:, THIRD:]], axis=1)
    square = plus * plus
    square = jnp.concatenate(
        [0.5 * (square[:, at] + mirror * mirror), square[:, THIRD:]], axis=1
    )
    return gain, row_scale(u) * square


def tile_kernel(
    core_ref, mate_ref, own_ref, other_ref, tab_ref, spec_ref, keep_ref, send_ref, power_sc
):
    for t, ref in enumerate((own_ref, other_ref)):
        parts = half_spectrum(ref[...], tab_ref)
        store_spectrum(spec_ref.at[t], parts)
        for k, (re, im) in enumerate(parts):
            at = slice(k * THIRD, (k + 1) * THIRD)
            square = re * re + im * im
            power_sc[:, at] = square if t == 0 else power_sc[:, at] + square
    low, high = power_sc[:PART], power_sc[SPLIT:]
    first = core_ref[...] == 0
    keep_ref[...] = jnp.where(first, low, high).astype(BF16)
    send_ref[...] = jnp.where(first, high, low).astype(BF16)


def gain_kernel(row_ref, mate_ref, table_ref, tile_ref, tab_ref, spec_ref, weight_ref):
    for t, ref in enumerate((row_ref, mate_ref)):
        gain, weight_ref[t] = ctf_factors(ref[...].astype(F32), table_ref[...])
        spec_ref[t, 0] = tile_ref[t, 0] * gain
        spec_ref[t, 1] = tile_ref[t, 1] * gain


def library_kernel(image_ref, tab_ref, out_ref):
    store_spectrum(out_ref, half_spectrum(image_ref[...].reshape(N, N), tab_ref))


def match_step(re, im, spec_ref, weight_ref, tab):
    wide = 2 * THIRD
    norm = jnp.sum((re * re + im * im) * weight_ref[...])
    scale = lax.rsqrt(jnp.full((1, THIRD), norm + 1e-06, F32))
    s_re, s_im = spec_ref[0], spec_ref[1]
    p_re = (s_re * re + s_im * im).astype(BF16)
    p_im = (s_im * re - s_re * im).astype(BF16)
    g = []
    for k in range(3):
        at = slice(k * THIRD, (k + 1) * THIRD)
        lhs = jnp.concatenate([p_re[:, at], p_im[:, at]], axis=1)
        g.append(dot(lhs, tab[k * wide : (k + 1) * wide, :]))
    (r0, i0), (r1, i1), (r2, i2) = ((x[:, :THIRD], x[:, THIRD:]) for x in g)
    slant = scale * ROOT
    rp, rm = r1 + r2, slant * (r1 - r2)
    ip, im_ = i1 + i2, slant * (i1 - i2)
    rh, ih = scale * (r0 - 0.5 * rp), scale * (i0 - 0.5 * ip)
    h_re = [scale * (r0 + rp), rh - im_, rh + im_]
    h_im = [scale * (i0 + ip), ih + rm, ih - rm]
    h_re = jnp.concatenate([h.astype(BF16) for h in h_re], axis=1)
    h_im = jnp.concatenate([h.astype(BF16) for h in h_im], axis=1)
    first = 3 * wide
    even = dot(tab[first : first + ROWS, :ROWS], h_re)
    odd = dot(tab[first + FOLD : first + FOLD + ROWS, :ROWS], h_im)
    return even - odd, even + odd


def whiten_kernel(core_ref, spec_ref, weight_ref, mine_ref, theirs_ref, spec_out, weight_out):
    mine, theirs = mine_ref[...].astype(F32), theirs_ref[...].astype(F32)
    first = core_ref[...] == 0
    low, high = jnp.where(first, mine, theirs), jnp.where(first, theirs, mine)
    power = jnp.concatenate([low[:SPLIT], high], axis=0) * (1.0 / 16.0)
    u, _ = row_numbers()
    mean = jnp.sum(power * row_scale(u)) * (1.0 / (N * N))
    inverse_noise = 1.0 / (jnp.where(u <= HALF, power, 1.0) + 0.05 * mean)
    for t in range(2):
        spec_out[t, 0] = spec_ref[t, 0] * inverse_noise
        spec_out[t, 1] = spec_ref[t, 1] * inverse_noise
        weight_out[t] = weight_ref[t] * inverse_noise


def near_kernel(lib_ref, spec_ref, weight_ref, tab_ref, out_ref):
    step = pl.program_id(0)

    @pl.when(step == 0)
    def _():
        out_ref[...] = jnp.full_like(out_ref, -jnp.inf)

    re, im = lib_ref[0].astype(F32), lib_ref[1].astype(F32)
    for t in range(2):
        sides = match_step(re, im, spec_ref.at[t], weight_ref.at[t], tab_ref)
        for k in range(2):
            out_ref[t, k] = jnp.maximum(out_ref[t, k], sides[k])


def far_kernel(lib_ref, spec_ref, weight_ref, tab_ref, start_ref, unfold_ref, out_ref, best_sc):
    step = pl.program_id(0)

    @pl.when(step == 0)
    def _():
        best_sc[...] = start_ref[...]

    pairs = [
        match_step(lib_ref[i, 0].astype(F32), lib_ref[i, 1].astype(F32), spec_ref, weight_ref, tab_ref)
        for i in range(2)
    ]
    for side in range(2):
        best_sc[side] = jnp.maximum(best_sc[side], jnp.maximum(pairs[0][side], pairs[1][side]))

    @pl.when(step == pl.num_programs(0) - 1)
    def _():
        out_ref[:HALF] = best_sc[0, :HALF].astype(out_ref.dtype)
        rest = best_sc[...].reshape(2 * ROWS, N)
        total = None
        for _ in range(3 if out_ref.dtype == F32 else 1):
            part = rest.astype(BF16)
            rest = rest - part.astype(F32)
            moved = dot(unfold_ref[...], part)
            total = moved if total is None else total + moved
        out_ref[HALF:] = total.astype(out_ref.dtype)


def full(*shape):
    return pl.BlockSpec(shape, lambda i: (0,) * len(shape))


def cost(flops, size):
    return pl.CostEstimate(flops=flops, bytes_accessed=size, transcendentals=0)


def params(mib):
    return pltpu.CompilerParams(vmem_limit_bytes=mib << 20)


def per_device(images, projections, ctf_row, defocus_term, astig_term, astig_cross, phase_shift):
    ahead, back, unfold = tables()
    groups = math.prod(lax.axis_size(a) for a in DEF)
    places = math.prod(lax.axis_size(a) for a in LIB)
    deep, wide = lax.axis_size("z"), lax.axis_size("xhi")
    core = lax.axis_index("core").astype(jnp.int32).reshape(1, 1)
    swap = [(0, 1), (1, 0)]
    plane = (2, ROWS, N)
    work = 2 * ROWS * 768 * 256 * 2

    tile = images[0, 0]
    received = lax.ppermute(tile, "xhi", swap)
    mate = lax.ppermute(ctf_row, "xhi", swap)
    block = projections[0]
    copies = pl.pallas_call(
        copy_kernel,
        out_shape=pltpu.HBM((places,) + block.shape, BF16),
        grid=(1,),
        in_specs=[full(*block.shape)],
        out_specs=pl.BlockSpec(memory_space=pltpu.HBM),
        scratch_shapes=[
            pltpu.VMEM((groups,) + block.shape, BF16),
            pltpu.SemaphoreType.DMA((places // groups,)),
        ],
        cost_estimate=cost(0, 1 << 20),
        name="copies",
    )(block)
    images_all = lax.all_to_all(copies, LIB, 0, 0, tiled=False)

    tiles, keep, send = pl.pallas_call(
        tile_kernel,
        out_shape=[
            jax.ShapeDtypeStruct((2,) + plane, F32),
            jax.ShapeDtypeStruct((PART, N), BF16),
            jax.ShapeDtypeStruct((PART, N), BF16),
        ],
        grid=(1,),
        in_specs=[full(1, 1), full(1, 1), full(N, N), full(N, N), full(*ahead.shape)],
        out_specs=[full(2, *plane), full(PART, N), full(PART, N)],
        scratch_shapes=[pltpu.VMEM((ROWS, N), F32)],
        compiler_params=params(12),
        cost_estimate=cost(200 * work, 3 << 20),
        name="tile",
    )(core, mate, tile, received, ahead)

    pair = (keep.astype(F32) + lax.ppermute(send, "core", swap).astype(F32)).astype(BF16)
    sums = pair.astype(F32)
    for dz in range(1, deep):
        moved = lax.ppermute(pair, "z", [(z, (z + dz) % deep) for z in range(deep)])
        sums = sums + moved.astype(F32)
    mine = sums.astype(BF16)

    table = jnp.stack([defocus_term, astig_term, astig_cross, phase_shift])
    table = jnp.pad(table, ((0, 4), (0, 128 - table.shape[1])))
    spec, weight = pl.pallas_call(
        gain_kernel,
        out_shape=[
            jax.ShapeDtypeStruct((2,) + plane, F32),
            jax.ShapeDtypeStruct((2, ROWS, N), F32),
        ],
        grid=(1,),
        in_specs=[full(1, 1), full(1, 1), full(*table.shape), full(2, *plane), full(*ahead.shape)],
        out_specs=[full(2, *plane), full(2, ROWS, N)],
        compiler_params=params(12),
        cost_estimate=cost(2 * ROWS * N * 60, 4 << 20),
        name="gain",
    )(ctf_row, mate, table, tiles, ahead)

    images_all, mine, spec = lax.optimization_barrier((images_all, mine, spec))
    theirs = lax.ppermute(mine, "core", swap)
    white, white_weight = pl.pallas_call(
        whiten_kernel,
        out_shape=[
            jax.ShapeDtypeStruct((2,) + plane, F32),
            jax.ShapeDtypeStruct((2, ROWS, N), F32),
        ],
        grid=(1,),
        in_specs=[full(1, 1), full(2, *plane), full(2, ROWS, N), full(PART, N), full(PART, N)],
        out_specs=[full(2, *plane), full(2, ROWS, N)],
        compiler_params=params(12),
        cost_estimate=cost(2 * ROWS * N * 4, 4 << 20),
        name="whiten",
    )(core, spec, weight, mine, theirs)

    near_all = pl.pallas_call(
        library_kernel,
        out_shape=jax.ShapeDtypeStruct((deep,) + plane, BF16),
        grid=(deep,),
        in_specs=[
            pl.BlockSpec((groups, None, N // groups, N), lambda i: (0, i, 0, 0)),
            full(*ahead.shape),
        ],
        out_specs=pl.BlockSpec((None,) + plane, lambda i: (i, 0, 0, 0)),
        compiler_params=params(12),
        cost_estimate=cost(deep * work, 4 << 20),
        name="library",
    )(images_all.reshape(groups, deep, N // groups, N), ahead)
    far_all = lax.ppermute(near_all, "core", swap)
    near_best = pl.pallas_call(
        near_kernel,
        out_shape=jax.ShapeDtypeStruct((2,) + plane, F32),
        grid=(deep,),
        in_specs=[
            pl.BlockSpec((None,) + plane, lambda i: (i, 0, 0, 0)),
            full(2, *plane),
            full(2, ROWS, N),
            full(*back.shape),
        ],
        out_specs=full(2, *plane),
        compiler_params=params(12),
        cost_estimate=cost(2 * deep * 2 * work, 8 << 20),
        name="near",
    )(near_all, white, white_weight, back)
    far_all, near_best = lax.optimization_barrier((far_all, near_best))

    def match(t, dtype, name):
        return pl.pallas_call(
            far_kernel,
            out_shape=jax.ShapeDtypeStruct((N, N), dtype),
            grid=(deep // 2,),
            in_specs=[
                pl.BlockSpec((2,) + plane, lambda i: (i, 0, 0, 0)),
                pl.BlockSpec((None,) + plane, lambda i: (t, 0, 0, 0)),
                pl.BlockSpec((None, ROWS, N), lambda i: (t, 0, 0)),
                full(*back.shape),
                pl.BlockSpec((None,) + plane, lambda i: (t, 0, 0, 0)),
                full(*unfold.shape),
            ],
            out_specs=full(N, N),
            scratch_shapes=[pltpu.VMEM(plane, F32)],
            compiler_params=params(12),
            cost_estimate=cost(deep * 2 * work, 5 << 20),
            name=name,
        )(far_all, white, white_weight, back, near_best, unfold)

    got = lax.ppermute(match(1, BF16, "far_other"), "xhi", swap)
    best = match(0, F32, "far_own")
    return jnp.maximum(best, got.astype(F32))[None, None]


def solution(mesh):
    fine = Mesh(mesh.devices.reshape(2, 4, 4, 2, 2), DEF + BLK)
    in_specs = (P(DEF, BLK, None, None), P(BLK, DEF, None), P(DEF, BLK), P(), P(), P(), P())
    out_specs = P(DEF, BLK, None, None)
    return jax.shard_map(
        per_device, mesh=fine, in_specs=in_specs, out_specs=out_specs, check_vma=False
    )
```

```python
import math

import jax
import jax.numpy as jnp
import ml_dtypes
import numpy as np
from jax import lax
from jax.experimental import pallas as pl
from jax.experimental.pallas import tpu as pltpu
from jax.sharding import Mesh
from jax.sharding import PartitionSpec as P

DEF = ("xlo", "y")
BLK = ("z", "xhi", "core")
LIB = ("xlo", "y", "z")
N = 384
HALF = N // 2
THIRD = N // 3
BLOCKS = (64, 64, 72)
ROWS = sum(BLOCKS)
SPLIT = 96
PART = ROWS - SPLIT
FOLD = 208
ROOT = math.sqrt(3.0) / 2.0
F32 = jnp.float32
BF16 = jnp.bfloat16


def tables():
    j = np.arange(N)
    phase = (j[:, None] * j[None, :]) % N
    cos = np.cos(2.0 * np.pi * phase / N)
    sin = np.sin(2.0 * np.pi * phase / N)
    bf = ml_dtypes.bfloat16
    u = np.concatenate([3 * np.arange(b) + c for c, b in zip((1, 2, 0), BLOCKS)])
    keep = (u <= HALF)[:, None]
    u = np.minimum(u, HALF)
    r = np.arange(THIRD)
    b1, b2 = BLOCKS[0], BLOCKS[0] + BLOCKS[1]
    real = np.concatenate([(keep * cos[u])[b2:, r], (keep * -sin[u])[b2:, r]])
    c1, s1 = cos[u[:b1]][:, r], sin[u[:b1]][:, r]
    c2, s2 = cos[u[b1:b2]][:, r], sin[u[b1:b2]][:, r]
    pair = np.block([[c1, s1], [c2, -s2], [-s1, c1], [-s2, -c2]])
    ahead, back = [], []
    for k in range(3):
        ck = cos[r][:, 3 * r + k]
        sk = sin[r][:, 3 * r + k]
        ahead.append(np.block([[ck, -sk], [sk, ck]]))
        back.append(np.block([[ck.T, sk.T], [-sk.T, ck.T]]))
    ahead, back = np.stack(ahead), np.stack(back)
    weight = np.where((u == 0) | (u == HALF), 1.0, 2.0) * keep[:, 0]
    fold = np.zeros((2, ROWS, ROWS))
    fold[0, : HALF + 1] = cos[: HALF + 1][:, u].astype(bf).astype(float) * weight
    fold[1, : HALF + 1] = sin[: HALF + 1][:, u].astype(bf).astype(float) * weight
    unfold = np.zeros((HALF, 2 * ROWS))
    unfold[0, HALF] = 1.0
    for i in range(1, HALF):
        unfold[i, ROWS + HALF - i] = 1.0
    ahead_all = np.concatenate([ahead.reshape(-1, 2 * THIRD), pair, np.pad(real, ((0, 0), (0, THIRD)))])
    pad = ((0, 0), (0, FOLD - ROWS), (0, 2 * THIRD - ROWS))
    back_all = np.concatenate([back.reshape(-1, 2 * THIRD), np.pad(fold, pad).reshape(-1, 2 * THIRD)])
    return [jnp.asarray(a.astype(bf)) for a in (ahead_all, back_all, unfold)]


def dot(a, b):
    return jnp.dot(a, b, preferred_element_type=F32)


def row_numbers():
    i = lax.broadcasted_iota(jnp.int32, (ROWS, N), 0)
    k = lax.broadcasted_iota(jnp.int32, (ROWS, N), 1)
    b1, b2 = BLOCKS[0], BLOCKS[0] + BLOCKS[1]
    u = jnp.where(i < b1, 3 * i + 1, jnp.where(i < b2, 3 * (i - b1) + 2, 3 * (i - b2)))
    v = jnp.where(
        k < THIRD, 3 * k, jnp.where(k < 2 * THIRD, 3 * (k - THIRD) + 1, 3 * (k - 2 * THIRD) + 2)
    )
    return u, v


def row_scale(u):
    return jnp.where((u > 0) & (u < HALF), 2.0, jnp.where(u <= HALF, 1.0, 0.0))


def copy_kernel(block_ref, out_ref, wide_sc, sems):
    count = wide_sc.shape[0]
    wide_sc[...] = jnp.broadcast_to(block_ref[...][None], wide_sc.shape)
    moves = [
        pltpu.make_async_copy(wide_sc, out_ref.at[pl.ds(i * count, count)], sems.at[i])
        for i in range(out_ref.shape[0] // count)
    ]
    for move in moves:
        move.start()
    for move in moves:
        move.wait()


def sine(x):
    x = x - jnp.round(x)
    a = jnp.abs(x)
    a = jnp.minimum(a, 0.5 - a)
    s = a * a
    p = jnp.full_like(x, -15.0946425768229800)
    for c in (
        42.0586939448600400,
        -76.7058597530613900,
        81.6052492760750400,
        -41.3417022403997600,
        6.28318530717958648,
    ):
        p = p * s + c
    p = p * a
    return jnp.where(x < 0.0, -p, p)


def half_spectrum(image, tab):
    wide = 2 * THIRD
    pair, real = tab[3 * wide : 4 * wide, :], tab[4 * wide :, :THIRD]
    image = image.astype(F32)
    x0, x1, x2 = image[:THIRD], image[THIRD : 2 * THIRD], image[2 * THIRD :]
    plus, minus = x1 + x2, x1 - x2
    f0 = (x0 + plus).astype(BF16)
    f1 = jnp.concatenate([(x0 - 0.5 * plus).astype(BF16), (-ROOT * minus).astype(BF16)], axis=0)
    low = dot(real, f0)
    high = dot(pair, f1)
    b, c = BLOCKS[0] + BLOCKS[1], BLOCKS[2]
    re = jnp.concatenate([high[:b], low[:c]], axis=0)
    im = jnp.concatenate([high[b:], low[c:]], axis=0)
    r0, r1, r2 = re[:, :THIRD], re[:, THIRD : 2 * THIRD], re[:, 2 * THIRD :]
    i0, i1, i2 = im[:, :THIRD], im[:, THIRD : 2 * THIRD], im[:, 2 * THIRD :]
    rp, rm = r1 + r2, ROOT * (r1 - r2)
    ip, im_ = i1 + i2, ROOT * (i1 - i2)
    rh, ih = r0 - 0.5 * rp, i0 - 0.5 * ip
    parts = ((r0 + rp, i0 + ip), (rh + im_, ih - rm), (rh - im_, ih + rm))
    result = []
    for k, (a, b) in enumerate(parts):
        lhs = jnp.concatenate([a.astype(BF16), b.astype(BF16)], axis=1)
        out = dot(lhs, tab[k * wide : (k + 1) * wide, :])
        result.append((out[:, :THIRD], out[:, THIRD:]))
    return result


def store_spectrum(ref, parts):
    for k, (re, im) in enumerate(parts):
        at = slice(k * THIRD, (k + 1) * THIRD)
        ref[0, :, at] = re.astype(ref.dtype)
        ref[1, :, at] = im.astype(ref.dtype)


def ctf_factors(row, table):
    lane = lax.broadcasted_iota(jnp.int32, table.shape, 1).astype(F32)
    chosen = jnp.sum(jnp.where(lane == row, table, 0.0), axis=1, keepdims=True)
    chosen = chosen * (1.0 / (2.0 * math.pi))
    u, v = row_numbers()
    row = jnp.where(u < HALF, u, u - N).astype(F32) * (1.0 / N)
    col = jnp.where(v < HALF, v, v - N).astype(F32) * (1.0 / N)
    r2, c2 = row * row, col * col
    base = chosen[0:1] * (r2 + c2) + chosen[1:2] * (r2 - c2) + chosen[3:4]
    cross = chosen[2:3] * (2.0 * row * col)
    plus = -sine(base + cross)
    at = slice(0, THIRD)
    inner = (u[:, at] > 0) & (u[:, at] < HALF) & (v[:, at] == HALF)
    mirror = jnp.where(inner, -sine(base[:, at] - cross[:, at]), plus[:, at])
    gain = jnp.concatenate([0.5 * (plus[:, at] + mirror), plus[:, THIRD:]], axis=1)
    square = plus * plus
    square = jnp.concatenate(
        [0.5 * (square[:, at] + mirror * mirror), square[:, THIRD:]], axis=1
    )
    return gain, row_scale(u) * square


def tile_kernel(
    core_ref, mate_ref, own_ref, other_ref, tab_ref, spec_ref, keep_ref, send_ref, power_sc
):
    for t, ref in enumerate((own_ref, other_ref)):
        parts = half_spectrum(ref[...], tab_ref)
        store_spectrum(spec_ref.at[t], parts)
        for k, (re, im) in enumerate(parts):
            at = slice(k * THIRD, (k + 1) * THIRD)
            square = re * re + im * im
            power_sc[:, at] = square if t == 0 else power_sc[:, at] + square
    low, high = power_sc[:PART], power_sc[SPLIT:]
    first = core_ref[...] == 0
    keep_ref[...] = jnp.where(first, low, high).astype(BF16)
    send_ref[...] = jnp.where(first, high, low).astype(BF16)


def gain_kernel(row_ref, mate_ref, table_ref, tile_ref, tab_ref, spec_ref, weight_ref):
    for t, ref in enumerate((row_ref, mate_ref)):
        gain, weight_ref[t] = ctf_factors(ref[...].astype(F32), table_ref[...])
        spec_ref[t, 0] = tile_ref[t, 0] * gain
        spec_ref[t, 1] = tile_ref[t, 1] * gain


def library_kernel(image_ref, tab_ref, out_ref):
    store_spectrum(out_ref, half_spectrum(image_ref[...].reshape(N, N), tab_ref))


def match_step(re, im, spec_ref, weight_ref, tab):
    wide = 2 * THIRD
    norm = jnp.sum((re * re + im * im) * weight_ref[...])
    scale = lax.rsqrt(jnp.full((1, THIRD), norm + 1e-06, F32))
    s_re, s_im = spec_ref[0], spec_ref[1]
    p_re = (s_re * re + s_im * im).astype(BF16)
    p_im = (s_im * re - s_re * im).astype(BF16)
    g = []
    for k in range(3):
        at = slice(k * THIRD, (k + 1) * THIRD)
        lhs = jnp.concatenate([p_re[:, at], p_im[:, at]], axis=1)
        g.append(dot(lhs, tab[k * wide : (k + 1) * wide, :]))
    (r0, i0), (r1, i1), (r2, i2) = ((x[:, :THIRD], x[:, THIRD:]) for x in g)
    slant = scale * ROOT
    rp, rm = r1 + r2, slant * (r1 - r2)
    ip, im_ = i1 + i2, slant * (i1 - i2)
    rh, ih = scale * (r0 - 0.5 * rp), scale * (i0 - 0.5 * ip)
    h_re = [scale * (r0 + rp), rh - im_, rh + im_]
    h_im = [scale * (i0 + ip), ih + rm, ih - rm]
    h_re = jnp.concatenate([h.astype(BF16) for h in h_re], axis=1)
    h_im = jnp.concatenate([h.astype(BF16) for h in h_im], axis=1)
    first = 3 * wide
    even = dot(tab[first : first + ROWS, :ROWS], h_re)
    odd = dot(tab[first + FOLD : first + FOLD + ROWS, :ROWS], h_im)
    return even - odd, even + odd


def whiten_kernel(core_ref, spec_ref, weight_ref, mine_ref, theirs_ref, spec_out, weight_out):
    mine, theirs = mine_ref[...].astype(F32), theirs_ref[...].astype(F32)
    first = core_ref[...] == 0
    low, high = jnp.where(first, mine, theirs), jnp.where(first, theirs, mine)
    power = jnp.concatenate([low[:SPLIT], high], axis=0) * (1.0 / 16.0)
    u, _ = row_numbers()
    mean = jnp.sum(power * row_scale(u)) * (1.0 / (N * N))
    inverse_noise = 1.0 / (jnp.where(u <= HALF, power, 1.0) + 0.05 * mean)
    for t in range(2):
        spec_out[t, 0] = spec_ref[t, 0] * inverse_noise
        spec_out[t, 1] = spec_ref[t, 1] * inverse_noise
        weight_out[t] = weight_ref[t] * inverse_noise


def match_kernel(near_ref, far_ref, spec_ref, weight_ref, tab_ref, unfold_ref, out_ref, best_sc):
    step = pl.program_id(0)

    @pl.when(step == 0)
    def _():
        best_sc[...] = jnp.full_like(best_sc, -jnp.inf)

    pairs = [
        match_step(ref[0].astype(F32), ref[1].astype(F32), spec_ref, weight_ref, tab_ref)
        for ref in (near_ref, far_ref)
    ]
    for side in range(2):
        best_sc[side] = jnp.maximum(best_sc[side], jnp.maximum(pairs[0][side], pairs[1][side]))

    @pl.when(step == pl.num_programs(0) - 1)
    def _():
        out_ref[:HALF] = best_sc[0, :HALF].astype(out_ref.dtype)
        rest = best_sc[...].reshape(2 * ROWS, N)
        total = None
        for _ in range(3 if out_ref.dtype == F32 else 1):
            part = rest.astype(BF16)
            rest = rest - part.astype(F32)
            moved = dot(unfold_ref[...], part)
            total = moved if total is None else total + moved
        out_ref[HALF:] = total.astype(out_ref.dtype)


def full(*shape):
    return pl.BlockSpec(shape, lambda i: (0,) * len(shape))


def cost(flops, size):
    return pl.CostEstimate(flops=flops, bytes_accessed=size, transcendentals=0)


def params(mib):
    return pltpu.CompilerParams(vmem_limit_bytes=mib << 20)


def per_device(images, projections, ctf_row, defocus_term, astig_term, astig_cross, phase_shift):
    ahead, back, unfold = tables()
    groups = math.prod(lax.axis_size(a) for a in DEF)
    places = math.prod(lax.axis_size(a) for a in LIB)
    deep, wide = lax.axis_size("z"), lax.axis_size("xhi")
    core = lax.axis_index("core").astype(jnp.int32).reshape(1, 1)
    swap = [(0, 1), (1, 0)]
    plane = (2, ROWS, N)
    work = 2 * ROWS * 768 * 256 * 2

    tile = images[0, 0]
    received = lax.ppermute(tile, "xhi", swap)
    mate = lax.ppermute(ctf_row, "xhi", swap)
    block = projections[0]
    copies = pl.pallas_call(
        copy_kernel,
        out_shape=pltpu.HBM((places,) + block.shape, BF16),
        grid=(1,),
        in_specs=[full(*block.shape)],
        out_specs=pl.BlockSpec(memory_space=pltpu.HBM),
        scratch_shapes=[
            pltpu.VMEM((groups,) + block.shape, BF16),
            pltpu.SemaphoreType.DMA((places // groups,)),
        ],
        cost_estimate=cost(0, 1 << 20),
        name="copies",
    )(block)
    images_all = lax.all_to_all(copies, LIB, 0, 0, tiled=False)

    tiles, keep, send = pl.pallas_call(
        tile_kernel,
        out_shape=[
            jax.ShapeDtypeStruct((2,) + plane, F32),
            jax.ShapeDtypeStruct((PART, N), BF16),
            jax.ShapeDtypeStruct((PART, N), BF16),
        ],
        grid=(1,),
        in_specs=[full(1, 1), full(1, 1), full(N, N), full(N, N), full(*ahead.shape)],
        out_specs=[full(2, *plane), full(PART, N), full(PART, N)],
        scratch_shapes=[pltpu.VMEM((ROWS, N), F32)],
        compiler_params=params(12),
        cost_estimate=cost(200 * work, 3 << 20),
        name="tile",
    )(core, mate, tile, received, ahead)

    pair = (keep.astype(F32) + lax.ppermute(send, "core", swap).astype(F32)).astype(BF16)
    moves = [
        lax.ppermute(pair, "z", [(z, (z + dz) % deep) for z in range(deep)])
        for dz in range(1, deep)
    ]

    table = jnp.stack([defocus_term, astig_term, astig_cross, phase_shift])
    table = jnp.pad(table, ((0, 4), (0, 128 - table.shape[1])))
    spec, weight = pl.pallas_call(
        gain_kernel,
        out_shape=[
            jax.ShapeDtypeStruct((2,) + plane, F32),
            jax.ShapeDtypeStruct((2, ROWS, N), F32),
        ],
        grid=(1,),
        in_specs=[full(1, 1), full(1, 1), full(*table.shape), full(2, *plane), full(*ahead.shape)],
        out_specs=[full(2, *plane), full(2, ROWS, N)],
        compiler_params=params(12),
        cost_estimate=cost(2 * ROWS * N * 60, 4 << 20),
        name="gain",
    )(ctf_row, mate, table, tiles, ahead)

    images_all, pair, spec = lax.optimization_barrier((images_all, pair, spec))

    near_all = pl.pallas_call(
        library_kernel,
        out_shape=jax.ShapeDtypeStruct((deep,) + plane, BF16),
        grid=(deep,),
        in_specs=[
            pl.BlockSpec((groups, None, N // groups, N), lambda i: (0, i, 0, 0)),
            full(*ahead.shape),
        ],
        out_specs=pl.BlockSpec((None,) + plane, lambda i: (i, 0, 0, 0)),
        compiler_params=params(12),
        cost_estimate=cost(deep * work, 4 << 20),
        name="library",
    )(images_all.reshape(groups, deep, N // groups, N), ahead)
    far_all = lax.ppermute(near_all, "core", swap)
    moves, near_all = lax.optimization_barrier((moves, near_all))
    mine = sum((m.astype(F32) for m in moves), pair.astype(F32)).astype(BF16)
    theirs = lax.ppermute(mine, "core", swap)
    white, white_weight = pl.pallas_call(
        whiten_kernel,
        out_shape=[
            jax.ShapeDtypeStruct((2,) + plane, F32),
            jax.ShapeDtypeStruct((2, ROWS, N), F32),
        ],
        grid=(1,),
        in_specs=[full(1, 1), full(2, *plane), full(2, ROWS, N), full(PART, N), full(PART, N)],
        out_specs=[full(2, *plane), full(2, ROWS, N)],
        compiler_params=params(12),
        cost_estimate=cost(60 * work, 4 << 20),
        name="whiten",
    )(core, spec, weight, mine, theirs)

    def match(t, dtype, name):
        lib_spec = pl.BlockSpec((None,) + plane, lambda i: (i, 0, 0, 0))
        return pl.pallas_call(
            match_kernel,
            out_shape=jax.ShapeDtypeStruct((N, N), dtype),
            grid=(deep,),
            in_specs=[
                lib_spec,
                lib_spec,
                pl.BlockSpec((None,) + plane, lambda i: (t, 0, 0, 0)),
                pl.BlockSpec((None, ROWS, N), lambda i: (t, 0, 0)),
                full(*back.shape),
                full(*unfold.shape),
            ],
            out_specs=full(N, N),
            scratch_shapes=[pltpu.VMEM(plane, F32)],
            compiler_params=params(12),
            cost_estimate=cost(2 * deep * 2 * work, 6 << 20),
            name=name,
        )(near_all, far_all, white, white_weight, back, unfold)

    got = lax.ppermute(match(1, BF16, "match_other"), "xhi", swap)
    best = match(0, F32, "match_own")
    return jnp.maximum(best, got.astype(F32))[None, None]


def solution(mesh):
    fine = Mesh(mesh.devices.reshape(2, 4, 4, 2, 2), DEF + BLK)
    in_specs = (P(DEF, BLK, None, None), P(BLK, DEF, None), P(DEF, BLK), P(), P(), P(), P())
    out_specs = P(DEF, BLK, None, None)
    return jax.shard_map(
        per_device, mesh=fine, in_specs=in_specs, out_specs=out_specs, check_vma=False
    )
```

```python
import math

import jax
import jax.numpy as jnp
import ml_dtypes
import numpy as np
from jax import lax
from jax.experimental import pallas as pl
from jax.experimental.pallas import tpu as pltpu
from jax.sharding import Mesh
from jax.sharding import PartitionSpec as P

DEF = ("xlo", "y")
BLK = ("z", "xhi", "core")
LIB = ("xlo", "y", "z")
N = 384
HALF = N // 2
THIRD = N // 3
BLOCKS = (64, 64, 72)
ROWS = sum(BLOCKS)
MARK = 16
SPLIT = 96
PART = ROWS - SPLIT
FOLD = 208
ROOT = math.sqrt(3.0) / 2.0
F32 = jnp.float32
BF16 = jnp.bfloat16


def tables():
    j = np.arange(N)
    phase = (j[:, None] * j[None, :]) % N
    cos = np.cos(2.0 * np.pi * phase / N)
    sin = np.sin(2.0 * np.pi * phase / N)
    bf = ml_dtypes.bfloat16
    u = np.concatenate([3 * np.arange(b) + c for c, b in zip((1, 2, 0), BLOCKS)])
    keep = (u <= HALF)[:, None]
    u = np.minimum(u, HALF)
    r = np.arange(THIRD)
    b1, b2 = BLOCKS[0], BLOCKS[0] + BLOCKS[1]
    real = np.concatenate([(keep * cos[u])[b2:, r], (keep * -sin[u])[b2:, r]])
    c1, s1 = cos[u[:b1]][:, r], sin[u[:b1]][:, r]
    c2, s2 = cos[u[b1:b2]][:, r], sin[u[b1:b2]][:, r]
    pair = np.block([[c1, s1], [c2, -s2], [-s1, c1], [-s2, -c2]])
    ahead, back = [], []
    for k in range(3):
        ck = cos[r][:, 3 * r + k]
        sk = sin[r][:, 3 * r + k]
        ahead.append(np.block([[ck, -sk], [sk, ck]]))
        back.append(np.block([[ck.T, sk.T], [-sk.T, ck.T]]))
    ahead, back = np.stack(ahead), np.stack(back)
    weight = np.where((u == 0) | (u == HALF), 1.0, 2.0) * keep[:, 0]
    fold = np.zeros((2, ROWS, ROWS))
    fold[0, : HALF + 1] = cos[: HALF + 1][:, u].astype(bf).astype(float) * weight
    fold[1, : HALF + 1] = sin[: HALF + 1][:, u].astype(bf).astype(float) * weight
    unfold = np.zeros((HALF, 2 * ROWS))
    unfold[0, HALF] = 1.0
    for i in range(1, HALF):
        unfold[i, ROWS + HALF - i] = 1.0
    ahead_all = np.concatenate([ahead.reshape(-1, 2 * THIRD), pair, np.pad(real, ((0, 0), (0, THIRD)))])
    pad = ((0, 0), (0, FOLD - ROWS), (0, 2 * THIRD - ROWS))
    back_all = np.concatenate([back.reshape(-1, 2 * THIRD), np.pad(fold, pad).reshape(-1, 2 * THIRD)])
    return [jnp.asarray(a.astype(bf)) for a in (ahead_all, back_all, unfold)]


def dot(a, b):
    return jnp.dot(a, b, preferred_element_type=F32)


def row_numbers():
    i = lax.broadcasted_iota(jnp.int32, (ROWS, N), 0)
    k = lax.broadcasted_iota(jnp.int32, (ROWS, N), 1)
    b1, b2 = BLOCKS[0], BLOCKS[0] + BLOCKS[1]
    u = jnp.where(i < b1, 3 * i + 1, jnp.where(i < b2, 3 * (i - b1) + 2, 3 * (i - b2)))
    v = jnp.where(
        k < THIRD, 3 * k, jnp.where(k < 2 * THIRD, 3 * (k - THIRD) + 1, 3 * (k - 2 * THIRD) + 2)
    )
    return u, v


def row_scale(u):
    return jnp.where((u > 0) & (u < HALF), 2.0, jnp.where(u <= HALF, 1.0, 0.0))


def copy_kernel(row_ref, tile_ref, block_ref, out_ref, sent_ref, wide_sc, sems):
    count = wide_sc.shape[0]
    wide_sc[...] = jnp.broadcast_to(block_ref[...][None], wide_sc.shape)
    moves = [
        pltpu.make_async_copy(wide_sc, out_ref.at[pl.ds(i * count, count)], sems.at[i])
        for i in range(out_ref.shape[0] // count)
    ]
    for move in moves:
        move.start()
    sent_ref[:N] = tile_ref[...]
    sent_ref[N:] = jnp.broadcast_to(row_ref[...].astype(F32), (MARK, N)).astype(BF16)
    for move in moves:
        move.wait()


def sine(x):
    x = x - jnp.round(x)
    a = jnp.abs(x)
    a = jnp.minimum(a, 0.5 - a)
    s = a * a
    p = jnp.full_like(x, -15.0946425768229800)
    for c in (
        42.0586939448600400,
        -76.7058597530613900,
        81.6052492760750400,
        -41.3417022403997600,
        6.28318530717958648,
    ):
        p = p * s + c
    p = p * a
    return jnp.where(x < 0.0, -p, p)


def half_spectrum(image, tab):
    wide = 2 * THIRD
    pair, real = tab[3 * wide : 4 * wide, :], tab[4 * wide :, :THIRD]
    image = image.astype(F32)
    x0, x1, x2 = image[:THIRD], image[THIRD : 2 * THIRD], image[2 * THIRD :]
    plus, minus = x1 + x2, x1 - x2
    f0 = (x0 + plus).astype(BF16)
    f1 = jnp.concatenate([(x0 - 0.5 * plus).astype(BF16), (-ROOT * minus).astype(BF16)], axis=0)
    low = dot(real, f0)
    high = dot(pair, f1)
    b, c = BLOCKS[0] + BLOCKS[1], BLOCKS[2]
    re = jnp.concatenate([high[:b], low[:c]], axis=0)
    im = jnp.concatenate([high[b:], low[c:]], axis=0)
    r0, r1, r2 = re[:, :THIRD], re[:, THIRD : 2 * THIRD], re[:, 2 * THIRD :]
    i0, i1, i2 = im[:, :THIRD], im[:, THIRD : 2 * THIRD], im[:, 2 * THIRD :]
    rp, rm = r1 + r2, ROOT * (r1 - r2)
    ip, im_ = i1 + i2, ROOT * (i1 - i2)
    rh, ih = r0 - 0.5 * rp, i0 - 0.5 * ip
    parts = ((r0 + rp, i0 + ip), (rh + im_, ih - rm), (rh - im_, ih + rm))
    result = []
    for k, (a, b) in enumerate(parts):
        lhs = jnp.concatenate([a.astype(BF16), b.astype(BF16)], axis=1)
        out = dot(lhs, tab[k * wide : (k + 1) * wide, :])
        result.append((out[:, :THIRD], out[:, THIRD:]))
    return result


def store_spectrum(ref, parts):
    for k, (re, im) in enumerate(parts):
        at = slice(k * THIRD, (k + 1) * THIRD)
        ref[0, :, at] = re.astype(ref.dtype)
        ref[1, :, at] = im.astype(ref.dtype)


def ctf_factors(row, table):
    lane = lax.broadcasted_iota(jnp.int32, table.shape, 1).astype(F32)
    chosen = jnp.sum(jnp.where(lane == row, table, 0.0), axis=1, keepdims=True)
    chosen = chosen * (1.0 / (2.0 * math.pi))
    u, v = row_numbers()
    row = jnp.where(u < HALF, u, u - N).astype(F32) * (1.0 / N)
    col = jnp.where(v < HALF, v, v - N).astype(F32) * (1.0 / N)
    r2, c2 = row * row, col * col
    base = chosen[0:1] * (r2 + c2) + chosen[1:2] * (r2 - c2) + chosen[3:4]
    cross = chosen[2:3] * (2.0 * row * col)
    plus = -sine(base + cross)
    at = slice(0, THIRD)
    inner = (u[:, at] > 0) & (u[:, at] < HALF) & (v[:, at] == HALF)
    mirror = jnp.where(inner, -sine(base[:, at] - cross[:, at]), plus[:, at])
    gain = jnp.concatenate([0.5 * (plus[:, at] + mirror), plus[:, THIRD:]], axis=1)
    square = plus * plus
    square = jnp.concatenate(
        [0.5 * (square[:, at] + mirror * mirror), square[:, THIRD:]], axis=1
    )
    return gain, row_scale(u) * square


def tile_kernel(core_ref, own_ref, other_ref, tab_ref, spec_ref, keep_ref, send_ref, power_sc):
    for t, ref in enumerate((own_ref, other_ref)):
        parts = half_spectrum(ref[:N], tab_ref)
        store_spectrum(spec_ref.at[t], parts)
        for k, (re, im) in enumerate(parts):
            at = slice(k * THIRD, (k + 1) * THIRD)
            square = re * re + im * im
            power_sc[:, at] = square if t == 0 else power_sc[:, at] + square
    low, high = power_sc[:PART], power_sc[SPLIT:]
    first = core_ref[...] == 0
    keep_ref[...] = jnp.where(first, low, high).astype(BF16)
    send_ref[...] = jnp.where(first, high, low).astype(BF16)


def gain_kernel(row_ref, mark_ref, table_ref, tile_ref, *refs):
    spec_ref, weight_ref = refs[-2:]
    for t, row in enumerate((row_ref[...], mark_ref[0:1, 0:1])):
        gain, weight_ref[t] = ctf_factors(row.astype(F32), table_ref[...])
        spec_ref[t, 0] = tile_ref[t, 0] * gain
        spec_ref[t, 1] = tile_ref[t, 1] * gain


def library_kernel(image_ref, tab_ref, out_ref):
    store_spectrum(out_ref, half_spectrum(image_ref[...].reshape(N, N), tab_ref))


def match_step(re, im, spec_ref, weight_ref, tab):
    wide = 2 * THIRD
    norm = jnp.sum((re * re + im * im) * weight_ref[...])
    scale = lax.rsqrt(jnp.full((1, THIRD), norm + 1e-06, F32))
    s_re, s_im = spec_ref[0], spec_ref[1]
    p_re = (s_re * re + s_im * im).astype(BF16)
    p_im = (s_im * re - s_re * im).astype(BF16)
    g = []
    for k in range(3):
        at = slice(k * THIRD, (k + 1) * THIRD)
        lhs = jnp.concatenate([p_re[:, at], p_im[:, at]], axis=1)
        g.append(dot(lhs, tab[k * wide : (k + 1) * wide, :]))
    (r0, i0), (r1, i1), (r2, i2) = ((x[:, :THIRD], x[:, THIRD:]) for x in g)
    slant = scale * ROOT
    rp, rm = r1 + r2, slant * (r1 - r2)
    ip, im_ = i1 + i2, slant * (i1 - i2)
    rh, ih = scale * (r0 - 0.5 * rp), scale * (i0 - 0.5 * ip)
    h_re = [scale * (r0 + rp), rh - im_, rh + im_]
    h_im = [scale * (i0 + ip), ih + rm, ih - rm]
    h_re = jnp.concatenate([h.astype(BF16) for h in h_re], axis=1)
    h_im = jnp.concatenate([h.astype(BF16) for h in h_im], axis=1)
    first = 3 * wide
    even = dot(tab[first : first + ROWS, :ROWS], h_re)
    odd = dot(tab[first + FOLD : first + FOLD + ROWS, :ROWS], h_im)
    return even - odd, even + odd


def whiten_kernel(core_ref, spec_ref, weight_ref, mine_ref, theirs_ref, *refs):
    spec_out, weight_out = refs[-2:]
    mine, theirs = mine_ref[...].astype(F32), theirs_ref[...].astype(F32)
    first = core_ref[...] == 0
    low, high = jnp.where(first, mine, theirs), jnp.where(first, theirs, mine)
    power = jnp.concatenate([low[:SPLIT], high], axis=0) * (1.0 / 16.0)
    u, _ = row_numbers()
    mean = jnp.sum(power * row_scale(u)) * (1.0 / (N * N))
    inverse_noise = 1.0 / (jnp.where(u <= HALF, power, 1.0) + 0.05 * mean)
    for t in range(2):
        spec_out[t, 0] = spec_ref[t, 0] * inverse_noise
        spec_out[t, 1] = spec_ref[t, 1] * inverse_noise
        weight_out[t] = weight_ref[t] * inverse_noise


def match_kernel(near_ref, far_ref, spec_ref, weight_ref, tab_ref, unfold_ref, out_ref, best_sc):
    step = pl.program_id(0)

    @pl.when(step == 0)
    def _():
        best_sc[...] = jnp.full_like(best_sc, -jnp.inf)

    for i in range(near_ref.shape[0]):
        pairs = [
            match_step(ref[i, 0].astype(F32), ref[i, 1].astype(F32), spec_ref, weight_ref, tab_ref)
            for ref in (near_ref, far_ref)
        ]
        for k in range(2):
            best_sc[k] = jnp.maximum(best_sc[k], jnp.maximum(pairs[0][k], pairs[1][k]))

    @pl.when(step == pl.num_programs(0) - 1)
    def _():
        out_ref[:HALF] = best_sc[0, :HALF].astype(out_ref.dtype)
        rest = best_sc[...].reshape(2 * ROWS, N)
        total = None
        for _ in range(3 if out_ref.dtype == F32 else 1):
            part = rest.astype(BF16)
            rest = rest - part.astype(F32)
            moved = dot(unfold_ref[...], part)
            total = moved if total is None else total + moved
        out_ref[HALF:] = total.astype(out_ref.dtype)


def full(*shape):
    return pl.BlockSpec(shape, lambda i: (0,) * len(shape))


def cost(flops, size):
    return pl.CostEstimate(flops=flops, bytes_accessed=size, transcendentals=0)


def params(mib):
    return pltpu.CompilerParams(vmem_limit_bytes=mib << 20)


def per_device(images, projections, ctf_row, defocus_term, astig_term, astig_cross, phase_shift):
    ahead, back, unfold = tables()
    groups = math.prod(lax.axis_size(a) for a in DEF)
    places = math.prod(lax.axis_size(a) for a in LIB)
    deep, wide = lax.axis_size("z"), lax.axis_size("xhi")
    core = lax.axis_index("core").astype(jnp.int32).reshape(1, 1)
    swap = [(0, 1), (1, 0)]
    kept = [pl.BlockSpec(memory_space=pltpu.VMEM)]
    plane = (2, ROWS, N)
    work = 2 * ROWS * 768 * 256 * 2

    tile = images[0, 0]
    block = projections[0]
    copies, sent = pl.pallas_call(
        copy_kernel,
        out_shape=[
            pltpu.HBM((places,) + block.shape, BF16),
            jax.ShapeDtypeStruct((N + MARK, N), BF16),
        ],
        grid=(1,),
        in_specs=[full(1, 1), full(N, N), full(*block.shape)],
        out_specs=[pl.BlockSpec(memory_space=pltpu.HBM), full(N + MARK, N)],
        scratch_shapes=[
            pltpu.VMEM((groups,) + block.shape, BF16),
            pltpu.SemaphoreType.DMA((places // groups,)),
        ],
        cost_estimate=cost(0, 1 << 20),
        name="copies",
    )(ctf_row, tile, block)
    received = lax.ppermute(sent, "xhi", swap)
    images_all = lax.all_to_all(copies, LIB, 0, 0, tiled=False)

    tiles, keep, send = pl.pallas_call(
        tile_kernel,
        out_shape=[
            jax.ShapeDtypeStruct((2,) + plane, F32),
            jax.ShapeDtypeStruct((PART, N), BF16),
            jax.ShapeDtypeStruct((PART, N), BF16),
        ],
        grid=(1,),
        in_specs=[full(1, 1), full(N, N), full(N + MARK, N), full(*ahead.shape)],
        out_specs=[full(2, *plane), full(PART, N), full(PART, N)],
        scratch_shapes=[pltpu.VMEM((ROWS, N), F32)],
        compiler_params=params(12),
        cost_estimate=cost(200 * work, 3 << 20),
        name="tile",
    )(core, tile, received, ahead)

    pair = (keep.astype(F32) + lax.ppermute(send, "core", swap).astype(F32)).astype(BF16)
    moves = [
        lax.ppermute(pair, "z", [(z, (z + dz) % deep) for z in range(deep)])
        for dz in range(1, deep)
    ]

    table = jnp.stack([defocus_term, astig_term, astig_cross, phase_shift])
    table = jnp.pad(table, ((0, 4), (0, 128 - table.shape[1])))
    spec, weight = pl.pallas_call(
        gain_kernel,
        out_shape=[
            jax.ShapeDtypeStruct((2,) + plane, F32),
            jax.ShapeDtypeStruct((2, ROWS, N), F32),
        ],
        grid=(1,),
        in_specs=[
            full(1, 1),
            pl.BlockSpec((MARK, N), lambda i: (N // MARK, 0)),
            full(*table.shape),
            full(2, *plane),
        ]
        + kept * 3,
        out_specs=[full(2, *plane), full(2, ROWS, N)],
        compiler_params=params(12),
        cost_estimate=cost(2 * ROWS * N * 60, 4 << 20),
        name="gain",
    )(ctf_row, received, table, tiles, ahead, back, unfold)

    images_all, pair, spec = lax.optimization_barrier((images_all, pair, spec))

    near_all = pl.pallas_call(
        library_kernel,
        out_shape=jax.ShapeDtypeStruct((deep,) + plane, BF16),
        grid=(deep,),
        in_specs=[
            pl.BlockSpec((groups, None, N // groups, N), lambda i: (0, i, 0, 0)),
            full(*ahead.shape),
        ],
        out_specs=pl.BlockSpec((None,) + plane, lambda i: (i, 0, 0, 0)),
        compiler_params=params(12),
        cost_estimate=cost(deep * work, 4 << 20),
        name="library",
    )(images_all.reshape(groups, deep, N // groups, N), ahead)
    far_all = lax.ppermute(near_all, "core", swap)
    moves, near_all = lax.optimization_barrier((moves, near_all))
    mine = sum((m.astype(F32) for m in moves), pair.astype(F32)).astype(BF16)
    theirs = lax.ppermute(mine, "core", swap)
    white, white_weight = pl.pallas_call(
        whiten_kernel,
        out_shape=[
            jax.ShapeDtypeStruct((2,) + plane, F32),
            jax.ShapeDtypeStruct((2, ROWS, N), F32),
        ],
        grid=(1,),
        in_specs=[full(1, 1), full(2, *plane), full(2, ROWS, N), full(PART, N), full(PART, N)]
        + kept * 2,
        out_specs=[full(2, *plane), full(2, ROWS, N)],
        compiler_params=params(12),
        cost_estimate=cost(60 * work, 4 << 20),
        name="whiten",
    )(core, spec, weight, mine, theirs, back, unfold)

    def match(t, dtype, name):
        lib_spec = pl.BlockSpec((2,) + plane, lambda i: (i, 0, 0, 0))
        return pl.pallas_call(
            match_kernel,
            out_shape=jax.ShapeDtypeStruct((N, N), dtype),
            grid=(deep // 2,),
            in_specs=[
                lib_spec,
                lib_spec,
                pl.BlockSpec((None,) + plane, lambda i: (t, 0, 0, 0)),
                pl.BlockSpec((None, ROWS, N), lambda i: (t, 0, 0)),
                full(*back.shape),
                full(*unfold.shape),
            ],
            out_specs=full(N, N),
            scratch_shapes=[pltpu.VMEM(plane, F32)],
            compiler_params=params(12),
            cost_estimate=cost(2 * deep * 2 * work, 6 << 20),
            name=name,
        )(near_all, far_all, white, white_weight, back, unfold)

    got = lax.ppermute(match(1, BF16, "match_other"), "xhi", swap)
    best = match(0, F32, "match_own")
    return jnp.maximum(best, got.astype(F32))[None, None]


def solution(mesh):
    fine = Mesh(mesh.devices.reshape(2, 4, 4, 2, 2), DEF + BLK)
    in_specs = (P(DEF, BLK, None, None), P(BLK, DEF, None), P(DEF, BLK), P(), P(), P(), P())
    out_specs = P(DEF, BLK, None, None)
    return jax.shard_map(
        per_device, mesh=fine, in_specs=in_specs, out_specs=out_specs, check_vma=False
    )
```

```python
import math

import jax
import jax.numpy as jnp
import ml_dtypes
import numpy as np
from jax import lax
from jax.experimental import pallas as pl
from jax.experimental.pallas import tpu as pltpu
from jax.sharding import Mesh
from jax.sharding import PartitionSpec as P

DEF = ("xlo", "y")
BLK = ("z", "xhi", "core")
LIB = ("xlo", "y", "z")
N = 384
HALF = N // 2
THIRD = N // 3
BLOCKS = (64, 64, 72)
ROWS = sum(BLOCKS)
SPLIT = 96
PART = ROWS - SPLIT
FOLD = 208
ROOT = math.sqrt(3.0) / 2.0
F32 = jnp.float32
BF16 = jnp.bfloat16


def tables():
    j = np.arange(N)
    phase = (j[:, None] * j[None, :]) % N
    cos = np.cos(2.0 * np.pi * phase / N)
    sin = np.sin(2.0 * np.pi * phase / N)
    bf = ml_dtypes.bfloat16
    u = np.concatenate([3 * np.arange(b) + c for c, b in zip((1, 2, 0), BLOCKS)])
    keep = (u <= HALF)[:, None]
    u = np.minimum(u, HALF)
    r = np.arange(THIRD)
    b1, b2 = BLOCKS[0], BLOCKS[0] + BLOCKS[1]
    real = np.concatenate([(keep * cos[u])[b2:, r], (keep * -sin[u])[b2:, r]])
    c1, s1 = cos[u[:b1]][:, r], sin[u[:b1]][:, r]
    c2, s2 = cos[u[b1:b2]][:, r], sin[u[b1:b2]][:, r]
    pair = np.block([[c1, s1], [c2, -s2], [-s1, c1], [-s2, -c2]])
    ahead, back = [], []
    for k in range(3):
        ck = cos[r][:, 3 * r + k]
        sk = sin[r][:, 3 * r + k]
        ahead.append(np.block([[ck, -sk], [sk, ck]]))
        back.append(np.block([[ck.T, sk.T], [-sk.T, ck.T]]))
    ahead, back = np.stack(ahead), np.stack(back)
    weight = np.where((u == 0) | (u == HALF), 1.0, 2.0) * keep[:, 0]
    fold = np.zeros((2, ROWS, ROWS))
    fold[0, : HALF + 1] = cos[: HALF + 1][:, u].astype(bf).astype(float) * weight
    fold[1, : HALF + 1] = sin[: HALF + 1][:, u].astype(bf).astype(float) * weight
    unfold = np.zeros((HALF, 2 * ROWS))
    unfold[0, HALF] = 1.0
    for i in range(1, HALF):
        unfold[i, ROWS + HALF - i] = 1.0
    ahead_all = np.concatenate([ahead.reshape(-1, 2 * THIRD), pair, np.pad(real, ((0, 0), (0, THIRD)))])
    pad = ((0, 0), (0, FOLD - ROWS), (0, 2 * THIRD - ROWS))
    back_all = np.concatenate([back.reshape(-1, 2 * THIRD), np.pad(fold, pad).reshape(-1, 2 * THIRD)])
    return [jnp.asarray(a.astype(bf)) for a in (ahead_all, back_all, unfold)]


def dot(a, b):
    return jnp.dot(a, b, preferred_element_type=F32)


def row_numbers():
    i = lax.broadcasted_iota(jnp.int32, (ROWS, N), 0)
    k = lax.broadcasted_iota(jnp.int32, (ROWS, N), 1)
    b1, b2 = BLOCKS[0], BLOCKS[0] + BLOCKS[1]
    u = jnp.where(i < b1, 3 * i + 1, jnp.where(i < b2, 3 * (i - b1) + 2, 3 * (i - b2)))
    v = jnp.where(
        k < THIRD, 3 * k, jnp.where(k < 2 * THIRD, 3 * (k - THIRD) + 1, 3 * (k - 2 * THIRD) + 2)
    )
    return u, v


def row_scale(u):
    return jnp.where((u > 0) & (u < HALF), 2.0, jnp.where(u <= HALF, 1.0, 0.0))


def copy_kernel(block_in, out_ref, block_ref, wide_sc, sem, sems):
    fetch = pltpu.make_async_copy(block_in, block_ref, sem)
    fetch.start()
    fetch.wait()
    count = wide_sc.shape[0]
    wide_sc[...] = jnp.broadcast_to(block_ref[...][None], wide_sc.shape)
    moves = [
        pltpu.make_async_copy(wide_sc, out_ref.at[pl.ds(i * count, count)], sems.at[i])
        for i in range(out_ref.shape[0] // count)
    ]
    for move in moves:
        move.start()
    for move in moves:
        move.wait()


def sine(x):
    x = x - jnp.round(x)
    a = jnp.abs(x)
    a = jnp.minimum(a, 0.5 - a)
    s = a * a
    p = jnp.full_like(x, -15.0946425768229800)
    for c in (
        42.0586939448600400,
        -76.7058597530613900,
        81.6052492760750400,
        -41.3417022403997600,
        6.28318530717958648,
    ):
        p = p * s + c
    p = p * a
    return jnp.where(x < 0.0, -p, p)


def half_spectrum(image, tab):
    wide = 2 * THIRD
    pair, real = tab[3 * wide : 4 * wide, :], tab[4 * wide :, :THIRD]
    image = image.astype(F32)
    x0, x1, x2 = image[:THIRD], image[THIRD : 2 * THIRD], image[2 * THIRD :]
    plus, minus = x1 + x2, x1 - x2
    f0 = (x0 + plus).astype(BF16)
    f1 = jnp.concatenate([(x0 - 0.5 * plus).astype(BF16), (-ROOT * minus).astype(BF16)], axis=0)
    low = dot(real, f0)
    high = dot(pair, f1)
    b, c = BLOCKS[0] + BLOCKS[1], BLOCKS[2]
    re = jnp.concatenate([high[:b], low[:c]], axis=0)
    im = jnp.concatenate([high[b:], low[c:]], axis=0)
    r0, r1, r2 = re[:, :THIRD], re[:, THIRD : 2 * THIRD], re[:, 2 * THIRD :]
    i0, i1, i2 = im[:, :THIRD], im[:, THIRD : 2 * THIRD], im[:, 2 * THIRD :]
    rp, rm = r1 + r2, ROOT * (r1 - r2)
    ip, im_ = i1 + i2, ROOT * (i1 - i2)
    rh, ih = r0 - 0.5 * rp, i0 - 0.5 * ip
    parts = ((r0 + rp, i0 + ip), (rh + im_, ih - rm), (rh - im_, ih + rm))
    result = []
    for k, (a, b) in enumerate(parts):
        lhs = jnp.concatenate([a.astype(BF16), b.astype(BF16)], axis=1)
        out = dot(lhs, tab[k * wide : (k + 1) * wide, :])
        result.append((out[:, :THIRD], out[:, THIRD:]))
    return result


def store_spectrum(ref, parts):
    for k, (re, im) in enumerate(parts):
        at = slice(k * THIRD, (k + 1) * THIRD)
        ref[0, :, at] = re.astype(ref.dtype)
        ref[1, :, at] = im.astype(ref.dtype)


def ctf_factors(row, table):
    lane = lax.broadcasted_iota(jnp.int32, table.shape, 1).astype(F32)
    chosen = jnp.sum(jnp.where(lane == row, table, 0.0), axis=1, keepdims=True)
    chosen = chosen * (1.0 / (2.0 * math.pi))
    u, v = row_numbers()
    row = jnp.where(u < HALF, u, u - N).astype(F32) * (1.0 / N)
    col = jnp.where(v < HALF, v, v - N).astype(F32) * (1.0 / N)
    r2, c2 = row * row, col * col
    base = chosen[0:1] * (r2 + c2) + chosen[1:2] * (r2 - c2) + chosen[3:4]
    cross = chosen[2:3] * (2.0 * row * col)
    plus = -sine(base + cross)
    at = slice(0, THIRD)
    inner = (u[:, at] > 0) & (u[:, at] < HALF) & (v[:, at] == HALF)
    mirror = jnp.where(inner, -sine(base[:, at] - cross[:, at]), plus[:, at])
    gain = jnp.concatenate([0.5 * (plus[:, at] + mirror), plus[:, THIRD:]], axis=1)
    square = plus * plus
    square = jnp.concatenate(
        [0.5 * (square[:, at] + mirror * mirror), square[:, THIRD:]], axis=1
    )
    return gain, row_scale(u) * square


def tile_kernel(core_ref, own_ref, other_ref, tab_ref, spec_ref, keep_ref, send_ref, power_sc):
    for t, ref in enumerate((own_ref, other_ref)):
        parts = half_spectrum(ref[...], tab_ref)
        store_spectrum(spec_ref.at[t], parts)
        for k, (re, im) in enumerate(parts):
            at = slice(k * THIRD, (k + 1) * THIRD)
            square = re * re + im * im
            power_sc[:, at] = square if t == 0 else power_sc[:, at] + square
    low, high = power_sc[:PART], power_sc[SPLIT:]
    first = core_ref[...] == 0
    keep_ref[...] = jnp.where(first, low, high).astype(BF16)
    send_ref[...] = jnp.where(first, high, low).astype(BF16)


def gain_kernel(row_ref, table_ref, tile_ref, *refs):
    spec_ref, weight_ref = refs[-2:]
    gain, weight_ref[...] = ctf_factors(row_ref[...].astype(F32), table_ref[...])
    spec_ref[0] = tile_ref[0] * gain
    spec_ref[1] = tile_ref[1] * gain


def library_kernel(image_ref, tab_ref, out_ref):
    store_spectrum(out_ref, half_spectrum(image_ref[...].reshape(N, N), tab_ref))


def match_step(re, im, spec_ref, weight_ref, tab):
    wide = 2 * THIRD
    norm = jnp.sum((re * re + im * im) * weight_ref[...])
    scale = lax.rsqrt(jnp.full((1, THIRD), norm + 1e-06, F32))
    s_re, s_im = spec_ref[0], spec_ref[1]
    p_re = (s_re * re + s_im * im).astype(BF16)
    p_im = (s_im * re - s_re * im).astype(BF16)
    g = []
    for k in range(3):
        at = slice(k * THIRD, (k + 1) * THIRD)
        lhs = jnp.concatenate([p_re[:, at], p_im[:, at]], axis=1)
        g.append(dot(lhs, tab[k * wide : (k + 1) * wide, :]))
    (r0, i0), (r1, i1), (r2, i2) = ((x[:, :THIRD], x[:, THIRD:]) for x in g)
    slant = scale * ROOT
    rp, rm = r1 + r2, slant * (r1 - r2)
    ip, im_ = i1 + i2, slant * (i1 - i2)
    rh, ih = scale * (r0 - 0.5 * rp), scale * (i0 - 0.5 * ip)
    h_re = [scale * (r0 + rp), rh - im_, rh + im_]
    h_im = [scale * (i0 + ip), ih + rm, ih - rm]
    h_re = jnp.concatenate([h.astype(BF16) for h in h_re], axis=1)
    h_im = jnp.concatenate([h.astype(BF16) for h in h_im], axis=1)
    first = 3 * wide
    even = dot(tab[first : first + ROWS, :ROWS], h_re)
    odd = dot(tab[first + FOLD : first + FOLD + ROWS, :ROWS], h_im)
    return even - odd, even + odd


def whiten_kernel(
    core_ref, own_ref, own_weight_ref, spec_ref, weight_ref, mine_ref, theirs_ref, *refs
):
    spec_out, weight_out = refs[-2:]
    mine, theirs = mine_ref[...].astype(F32), theirs_ref[...].astype(F32)
    first = core_ref[...] == 0
    low, high = jnp.where(first, mine, theirs), jnp.where(first, theirs, mine)
    power = jnp.concatenate([low[:SPLIT], high], axis=0) * (1.0 / 16.0)
    u, _ = row_numbers()
    mean = jnp.sum(power * row_scale(u)) * (1.0 / (N * N))
    inverse_noise = 1.0 / (jnp.where(u <= HALF, power, 1.0) + 0.05 * mean)
    for t, (spec, weight) in enumerate(((own_ref, own_weight_ref), (spec_ref, weight_ref))):
        spec_out[t, 0] = spec[0] * inverse_noise
        spec_out[t, 1] = spec[1] * inverse_noise
        weight_out[t] = weight[...] * inverse_noise


def match_kernel(near_ref, far_ref, spec_ref, weight_ref, tab_ref, unfold_ref, out_ref, best_sc):
    step = pl.program_id(0)

    @pl.when(step == 0)
    def _():
        best_sc[...] = jnp.full_like(best_sc, -jnp.inf)

    for i in range(near_ref.shape[0]):
        pairs = [
            match_step(ref[i, 0].astype(F32), ref[i, 1].astype(F32), spec_ref, weight_ref, tab_ref)
            for ref in (near_ref, far_ref)
        ]
        for k in range(2):
            best_sc[k] = jnp.maximum(best_sc[k], jnp.maximum(pairs[0][k], pairs[1][k]))

    @pl.when(step == pl.num_programs(0) - 1)
    def _():
        out_ref[:HALF] = best_sc[0, :HALF].astype(out_ref.dtype)
        rest = best_sc[...].reshape(2 * ROWS, N)
        total = None
        for _ in range(3 if out_ref.dtype == F32 else 1):
            part = rest.astype(BF16)
            rest = rest - part.astype(F32)
            moved = dot(unfold_ref[...], part)
            total = moved if total is None else total + moved
        out_ref[HALF:] = total.astype(out_ref.dtype)


def full(*shape):
    return pl.BlockSpec(shape, lambda i: (0,) * len(shape))


def cost(flops, size):
    return pl.CostEstimate(flops=flops, bytes_accessed=size, transcendentals=0)


def params(mib):
    return pltpu.CompilerParams(vmem_limit_bytes=mib << 20)


def per_device(images, projections, ctf_row, defocus_term, astig_term, astig_cross, phase_shift):
    ahead, back, unfold = tables()
    groups = math.prod(lax.axis_size(a) for a in DEF)
    places = math.prod(lax.axis_size(a) for a in LIB)
    deep, wide = lax.axis_size("z"), lax.axis_size("xhi")
    core = lax.axis_index("core").astype(jnp.int32).reshape(1, 1)
    swap = [(0, 1), (1, 0)]
    kept = [pl.BlockSpec(memory_space=pltpu.VMEM)]
    plane = (2, ROWS, N)
    work = 2 * ROWS * 768 * 256 * 2

    tile = images[0, 0]
    block = projections[0]
    received = lax.ppermute(tile, "xhi", swap)
    copies = pl.pallas_call(
        copy_kernel,
        out_shape=pltpu.HBM((places,) + block.shape, BF16),
        in_specs=[pl.BlockSpec(memory_space=pltpu.HBM)],
        out_specs=pl.BlockSpec(memory_space=pltpu.HBM),
        scratch_shapes=[
            pltpu.VMEM(block.shape, BF16),
            pltpu.VMEM((groups,) + block.shape, BF16),
            pltpu.SemaphoreType.DMA,
            pltpu.SemaphoreType.DMA((places // groups,)),
        ],
        cost_estimate=cost(0, 1 << 20),
        name="copies",
    )(block)
    images_all = lax.all_to_all(copies, LIB, 0, 0, tiled=False)

    tiles, keep, send = pl.pallas_call(
        tile_kernel,
        out_shape=[
            jax.ShapeDtypeStruct((2,) + plane, F32),
            jax.ShapeDtypeStruct((PART, N), BF16),
            jax.ShapeDtypeStruct((PART, N), BF16),
        ],
        grid=(1,),
        in_specs=[full(1, 1), full(N, N), full(N, N), full(*ahead.shape)],
        out_specs=[full(2, *plane), full(PART, N), full(PART, N)],
        scratch_shapes=[pltpu.VMEM((ROWS, N), F32)],
        compiler_params=params(12),
        cost_estimate=cost(200 * work, 3 << 20),
        name="tile",
    )(core, tile, received, ahead)

    pair = (keep.astype(F32) + lax.ppermute(send, "core", swap).astype(F32)).astype(BF16)
    moves = [
        lax.ppermute(pair, "z", [(z, (z + dz) % deep) for z in range(deep)])
        for dz in range(1, deep)
    ]

    table = jnp.stack([defocus_term, astig_term, astig_cross, phase_shift])
    table = jnp.pad(table, ((0, 4), (0, 128 - table.shape[1])))
    row, _ = lax.optimization_barrier((ctf_row, pair))
    mate = lax.ppermute(row, "xhi", swap)

    def gain(t, row, tables, name):
        return pl.pallas_call(
            gain_kernel,
            out_shape=[
                jax.ShapeDtypeStruct(plane, F32),
                jax.ShapeDtypeStruct((ROWS, N), F32),
            ],
            grid=(1,),
            in_specs=[
                full(1, 1),
                full(*table.shape),
                pl.BlockSpec((None,) + plane, lambda i: (t, 0, 0, 0)),
            ]
            + kept * len(tables),
            out_specs=[full(*plane), full(ROWS, N)],
            compiler_params=params(12),
            cost_estimate=cost(8 * work, 3 << 20),
            name=name,
        )(row, table, tiles, *tables)

    own = gain(0, ctf_row, (ahead, back, unfold), "gain_own")
    images_all, pair, own = lax.optimization_barrier((images_all, pair, own))

    near_all = pl.pallas_call(
        library_kernel,
        out_shape=jax.ShapeDtypeStruct((deep,) + plane, BF16),
        grid=(deep,),
        in_specs=[
            pl.BlockSpec((groups, None, N // groups, N), lambda i: (0, i, 0, 0)),
            full(*ahead.shape),
        ],
        out_specs=pl.BlockSpec((None,) + plane, lambda i: (i, 0, 0, 0)),
        compiler_params=params(12),
        cost_estimate=cost(deep * work, 4 << 20),
        name="library",
    )(images_all.reshape(groups, deep, N // groups, N), ahead)
    far_all = lax.ppermute(near_all, "core", swap)
    moves, near_all, mate = lax.optimization_barrier((moves, near_all, mate))
    other = gain(1, mate, (), "gain_other")
    mine = sum((m.astype(F32) for m in moves), pair.astype(F32)).astype(BF16)
    theirs = lax.ppermute(mine, "core", swap)
    white, white_weight = pl.pallas_call(
        whiten_kernel,
        out_shape=[
            jax.ShapeDtypeStruct((2,) + plane, F32),
            jax.ShapeDtypeStruct((2, ROWS, N), F32),
        ],
        grid=(1,),
        in_specs=[full(1, 1)]
        + [full(*plane), full(ROWS, N)] * 2
        + [full(PART, N)] * 2
        + kept * 2,
        out_specs=[full(2, *plane), full(2, ROWS, N)],
        compiler_params=params(12),
        cost_estimate=cost(60 * work, 4 << 20),
        name="whiten",
    )(core, *own, *other, mine, theirs, back, unfold)

    def match(t, dtype, name):
        lib_spec = pl.BlockSpec((2,) + plane, lambda i: (i, 0, 0, 0))
        return pl.pallas_call(
            match_kernel,
            out_shape=jax.ShapeDtypeStruct((N, N), dtype),
            grid=(deep // 2,),
            in_specs=[
                lib_spec,
                lib_spec,
                pl.BlockSpec((None,) + plane, lambda i: (t, 0, 0, 0)),
                pl.BlockSpec((None, ROWS, N), lambda i: (t, 0, 0)),
                full(*back.shape),
                full(*unfold.shape),
            ],
            out_specs=full(N, N),
            scratch_shapes=[pltpu.VMEM(plane, F32)],
            compiler_params=params(12),
            cost_estimate=cost(2 * deep * 2 * work, 6 << 20),
            name=name,
        )(near_all, far_all, white, white_weight, back, unfold)

    got = lax.ppermute(match(1, BF16, "match_other"), "xhi", swap)
    best = match(0, F32, "match_own")
    return jnp.maximum(best, got.astype(F32))[None, None]


def solution(mesh):
    fine = Mesh(mesh.devices.reshape(2, 4, 4, 2, 2), DEF + BLK)
    in_specs = (P(DEF, BLK, None, None), P(BLK, DEF, None), P(DEF, BLK), P(), P(), P(), P())
    out_specs = P(DEF, BLK, None, None)
    return jax.shard_map(
        per_device, mesh=fine, in_specs=in_specs, out_specs=out_specs, check_vma=False
    )
```

```python
import functools
import math

import jax
import jax.numpy as jnp
import ml_dtypes
import numpy as np
from jax import lax
from jax.experimental import pallas as pl
from jax.experimental.pallas import tpu as pltpu
from jax.sharding import Mesh
from jax.sharding import PartitionSpec as P

DEF = ("xlo", "y")
BLK = ("z", "xhi", "core")
LIB = ("xlo", "y", "z")
N = 384
HALF = N // 2
THIRD = N // 3
BLOCKS = (64, 64, 72)
ROWS = sum(BLOCKS)
SPLIT = 96
PART = ROWS - SPLIT
FOLD = 208
ROOT = math.sqrt(3.0) / 2.0
F32 = jnp.float32
BF16 = jnp.bfloat16


def tables():
    j = np.arange(N)
    phase = (j[:, None] * j[None, :]) % N
    cos = np.cos(2.0 * np.pi * phase / N)
    sin = np.sin(2.0 * np.pi * phase / N)
    bf = ml_dtypes.bfloat16
    u = np.concatenate([3 * np.arange(b) + c for c, b in zip((1, 2, 0), BLOCKS)])
    keep = (u <= HALF)[:, None]
    u = np.minimum(u, HALF)
    r = np.arange(THIRD)
    b1, b2 = BLOCKS[0], BLOCKS[0] + BLOCKS[1]
    real = np.concatenate([(keep * cos[u])[b2:, r], (keep * -sin[u])[b2:, r]])
    c1, s1 = cos[u[:b1]][:, r], sin[u[:b1]][:, r]
    c2, s2 = cos[u[b1:b2]][:, r], sin[u[b1:b2]][:, r]
    pair = np.block([[c1, s1], [c2, -s2], [-s1, c1], [-s2, -c2]])
    ahead, back = [], []
    for k in range(3):
        ck = cos[r][:, 3 * r + k]
        sk = sin[r][:, 3 * r + k]
        ahead.append(np.block([[ck, -sk], [sk, ck]]))
        back.append(np.block([[ck.T, sk.T], [-sk.T, ck.T]]))
    ahead, back = np.stack(ahead), np.stack(back)
    weight = np.where((u == 0) | (u == HALF), 1.0, 2.0) * keep[:, 0]
    fold = np.zeros((2, ROWS, ROWS))
    fold[0, : HALF + 1] = cos[: HALF + 1][:, u].astype(bf).astype(float) * weight
    fold[1, : HALF + 1] = sin[: HALF + 1][:, u].astype(bf).astype(float) * weight
    unfold = np.zeros((HALF, 2 * ROWS))
    unfold[0, HALF] = 1.0
    for i in range(1, HALF):
        unfold[i, ROWS + HALF - i] = 1.0
    ahead_all = np.concatenate([ahead.reshape(-1, 2 * THIRD), pair, np.pad(real, ((0, 0), (0, THIRD)))])
    pad = ((0, 0), (0, FOLD - ROWS), (0, 2 * THIRD - ROWS))
    back_all = np.concatenate([back.reshape(-1, 2 * THIRD), np.pad(fold, pad).reshape(-1, 2 * THIRD)])
    return [jnp.asarray(a.astype(bf)) for a in (ahead_all, back_all, unfold)]


def dot(a, b):
    return jnp.dot(a, b, preferred_element_type=F32)


def row_numbers():
    i = lax.broadcasted_iota(jnp.int32, (ROWS, N), 0)
    k = lax.broadcasted_iota(jnp.int32, (ROWS, N), 1)
    b1, b2 = BLOCKS[0], BLOCKS[0] + BLOCKS[1]
    u = jnp.where(i < b1, 3 * i + 1, jnp.where(i < b2, 3 * (i - b1) + 2, 3 * (i - b2)))
    v = jnp.where(
        k < THIRD, 3 * k, jnp.where(k < 2 * THIRD, 3 * (k - THIRD) + 1, 3 * (k - 2 * THIRD) + 2)
    )
    return u, v


def row_scale(u):
    return jnp.where((u > 0) & (u < HALF), 2.0, jnp.where(u <= HALF, 1.0, 0.0))


def copy_kernel(block_in, out_ref, block_ref, wide_sc, sem, sems):
    fetch = pltpu.make_async_copy(block_in, block_ref, sem)
    fetch.start()
    fetch.wait()
    count = wide_sc.shape[0]
    wide_sc[...] = jnp.broadcast_to(block_ref[...][None], wide_sc.shape)
    moves = [
        pltpu.make_async_copy(wide_sc, out_ref.at[pl.ds(i * count, count)], sems.at[i])
        for i in range(out_ref.shape[0] // count)
    ]
    for move in moves:
        move.start()
    for move in moves:
        move.wait()


def sine(x):
    x = x - jnp.round(x)
    a = jnp.abs(x)
    a = jnp.minimum(a, 0.5 - a)
    s = a * a
    p = jnp.full_like(x, -15.0946425768229800)
    for c in (
        42.0586939448600400,
        -76.7058597530613900,
        81.6052492760750400,
        -41.3417022403997600,
        6.28318530717958648,
    ):
        p = p * s + c
    p = p * a
    return jnp.where(x < 0.0, -p, p)


def half_spectrum(image, tab):
    wide = 2 * THIRD
    pair, real = tab[3 * wide : 4 * wide, :], tab[4 * wide :, :THIRD]
    image = image.astype(F32)
    x0, x1, x2 = image[:THIRD], image[THIRD : 2 * THIRD], image[2 * THIRD :]
    plus, minus = x1 + x2, x1 - x2
    f0 = (x0 + plus).astype(BF16)
    f1 = jnp.concatenate([(x0 - 0.5 * plus).astype(BF16), (-ROOT * minus).astype(BF16)], axis=0)
    low = dot(real, f0)
    high = dot(pair, f1)
    b, c = BLOCKS[0] + BLOCKS[1], BLOCKS[2]
    re = jnp.concatenate([high[:b], low[:c]], axis=0)
    im = jnp.concatenate([high[b:], low[c:]], axis=0)
    r0, r1, r2 = re[:, :THIRD], re[:, THIRD : 2 * THIRD], re[:, 2 * THIRD :]
    i0, i1, i2 = im[:, :THIRD], im[:, THIRD : 2 * THIRD], im[:, 2 * THIRD :]
    rp, rm = r1 + r2, ROOT * (r1 - r2)
    ip, im_ = i1 + i2, ROOT * (i1 - i2)
    rh, ih = r0 - 0.5 * rp, i0 - 0.5 * ip
    parts = ((r0 + rp, i0 + ip), (rh + im_, ih - rm), (rh - im_, ih + rm))
    result = []
    for k, (a, b) in enumerate(parts):
        lhs = jnp.concatenate([a.astype(BF16), b.astype(BF16)], axis=1)
        out = dot(lhs, tab[k * wide : (k + 1) * wide, :])
        result.append((out[:, :THIRD], out[:, THIRD:]))
    return result


def store_spectrum(ref, parts):
    for k, (re, im) in enumerate(parts):
        at = slice(k * THIRD, (k + 1) * THIRD)
        ref[0, :, at] = re.astype(ref.dtype)
        ref[1, :, at] = im.astype(ref.dtype)


def ctf_factors(row, table):
    lane = lax.broadcasted_iota(jnp.int32, table.shape, 1).astype(F32)
    chosen = jnp.sum(jnp.where(lane == row, table, 0.0), axis=1, keepdims=True)
    chosen = chosen * (1.0 / (2.0 * math.pi))
    u, v = row_numbers()
    row = jnp.where(u < HALF, u, u - N).astype(F32) * (1.0 / N)
    col = jnp.where(v < HALF, v, v - N).astype(F32) * (1.0 / N)
    r2, c2 = row * row, col * col
    base = chosen[0:1] * (r2 + c2) + chosen[1:2] * (r2 - c2) + chosen[3:4]
    cross = chosen[2:3] * (2.0 * row * col)
    plus = -sine(base + cross)
    at = slice(0, THIRD)
    inner = (u[:, at] > 0) & (u[:, at] < HALF) & (v[:, at] == HALF)
    mirror = jnp.where(inner, -sine(base[:, at] - cross[:, at]), plus[:, at])
    gain = jnp.concatenate([0.5 * (plus[:, at] + mirror), plus[:, THIRD:]], axis=1)
    square = plus * plus
    square = jnp.concatenate(
        [0.5 * (square[:, at] + mirror * mirror), square[:, THIRD:]], axis=1
    )
    return gain, row_scale(u) * square


def tile_kernel(core_ref, own_ref, other_ref, tab_ref, spec_ref, keep_ref, send_ref, power_sc):
    for t, ref in enumerate((own_ref, other_ref)):
        parts = half_spectrum(ref[...], tab_ref)
        store_spectrum(spec_ref.at[t], parts)
        for k, (re, im) in enumerate(parts):
            at = slice(k * THIRD, (k + 1) * THIRD)
            square = re * re + im * im
            power_sc[:, at] = square if t == 0 else power_sc[:, at] + square
    low, high = power_sc[:PART], power_sc[SPLIT:]
    first = core_ref[...] == 0
    keep_ref[...] = jnp.where(first, low, high).astype(BF16)
    send_ref[...] = jnp.where(first, high, low).astype(BF16)


def gain_kernel(row_ref, table_ref, tile_ref, *refs):
    spec_ref, weight_ref = refs[-2:]
    gain, weight_ref[...] = ctf_factors(row_ref[...].astype(F32), table_ref[...])
    spec_ref[0] = tile_ref[0] * gain
    spec_ref[1] = tile_ref[1] * gain


def library_kernel(image_ref, tab_ref, out_ref):
    step = pl.program_id(0)
    for i in range(2):
        image = image_ref[:, 2 * step + i].reshape(N, N)
        store_spectrum(out_ref.at[2 * step + i], half_spectrum(image, tab_ref))


def match_step(re, im, spec_ref, weight_ref, tab):
    wide = 2 * THIRD
    norm = jnp.sum((re * re + im * im) * weight_ref[...])
    scale = lax.rsqrt(jnp.full((1, THIRD), norm + 1e-06, F32))
    s_re, s_im = spec_ref[0], spec_ref[1]
    p_re = (s_re * re + s_im * im).astype(BF16)
    p_im = (s_im * re - s_re * im).astype(BF16)
    g = []
    for k in range(3):
        at = slice(k * THIRD, (k + 1) * THIRD)
        lhs = jnp.concatenate([p_re[:, at], p_im[:, at]], axis=1)
        g.append(dot(lhs, tab[k * wide : (k + 1) * wide, :]))
    (r0, i0), (r1, i1), (r2, i2) = ((x[:, :THIRD], x[:, THIRD:]) for x in g)
    slant = scale * ROOT
    rp, rm = r1 + r2, slant * (r1 - r2)
    ip, im_ = i1 + i2, slant * (i1 - i2)
    rh, ih = scale * (r0 - 0.5 * rp), scale * (i0 - 0.5 * ip)
    h_re = [scale * (r0 + rp), rh - im_, rh + im_]
    h_im = [scale * (i0 + ip), ih + rm, ih - rm]
    h_re = jnp.concatenate([h.astype(BF16) for h in h_re], axis=1)
    h_im = jnp.concatenate([h.astype(BF16) for h in h_im], axis=1)
    first = 3 * wide
    even = dot(tab[first : first + ROWS, :ROWS], h_re)
    odd = dot(tab[first + FOLD : first + FOLD + ROWS, :ROWS], h_im)
    return even - odd, even + odd


def whiten_kernel(
    core_ref, own_ref, own_weight_ref, spec_ref, weight_ref, mine_ref, theirs_ref, *refs
):
    spec_out, weight_out = refs[-2:]
    mine, theirs = mine_ref[...].astype(F32), theirs_ref[...].astype(F32)
    first = core_ref[...] == 0
    low, high = jnp.where(first, mine, theirs), jnp.where(first, theirs, mine)
    power = jnp.concatenate([low[:SPLIT], high], axis=0) * (1.0 / 16.0)
    u, _ = row_numbers()
    mean = jnp.sum(power * row_scale(u)) * (1.0 / (N * N))
    inverse_noise = 1.0 / (jnp.where(u <= HALF, power, 1.0) + 0.05 * mean)
    for t, (spec, weight) in enumerate(((own_ref, own_weight_ref), (spec_ref, weight_ref))):
        spec_out[t, 0] = spec[0] * inverse_noise
        spec_out[t, 1] = spec[1] * inverse_noise
        weight_out[t] = weight[...] * inverse_noise


def match_kernel(
    t, near_ref, far_ref, spec_ref, weight_ref, tab_ref, unfold_ref, out_ref, best_sc
):
    step = pl.program_id(0)

    @pl.when(step == 0)
    def _():
        best_sc[...] = jnp.full_like(best_sc, -jnp.inf)

    for i in range(2):
        pairs = [
            match_step(
                ref[2 * step + i, 0].astype(F32),
                ref[2 * step + i, 1].astype(F32),
                spec_ref.at[t],
                weight_ref.at[t],
                tab_ref,
            )
            for ref in (near_ref, far_ref)
        ]
        for k in range(2):
            best_sc[k] = jnp.maximum(best_sc[k], jnp.maximum(pairs[0][k], pairs[1][k]))

    @pl.when(step == pl.num_programs(0) - 1)
    def _():
        out_ref[:HALF] = best_sc[0, :HALF].astype(out_ref.dtype)
        rest = best_sc[...].reshape(2 * ROWS, N)
        total = None
        for _ in range(3 if out_ref.dtype == F32 else 1):
            part = rest.astype(BF16)
            rest = rest - part.astype(F32)
            moved = dot(unfold_ref[...], part)
            total = moved if total is None else total + moved
        out_ref[HALF:] = total.astype(out_ref.dtype)


def full(*shape):
    return pl.BlockSpec(shape, lambda i: (0,) * len(shape))


def cost(flops, size):
    return pl.CostEstimate(flops=flops, bytes_accessed=size, transcendentals=0)


def params(mib):
    return pltpu.CompilerParams(vmem_limit_bytes=mib << 20)


def per_device(images, projections, ctf_row, defocus_term, astig_term, astig_cross, phase_shift):
    ahead, back, unfold = tables()
    groups = math.prod(lax.axis_size(a) for a in DEF)
    places = math.prod(lax.axis_size(a) for a in LIB)
    deep, wide = lax.axis_size("z"), lax.axis_size("xhi")
    core = lax.axis_index("core").astype(jnp.int32).reshape(1, 1)
    swap = [(0, 1), (1, 0)]
    kept = [pl.BlockSpec(memory_space=pltpu.VMEM)]
    plane = (2, ROWS, N)
    work = 2 * ROWS * 768 * 256 * 2

    tile = images[0, 0]
    block = projections[0]
    received = lax.ppermute(tile, "xhi", swap)
    copies = pl.pallas_call(
        copy_kernel,
        out_shape=pltpu.HBM((places,) + block.shape, BF16),
        in_specs=[pl.BlockSpec(memory_space=pltpu.HBM)],
        out_specs=pl.BlockSpec(memory_space=pltpu.HBM),
        scratch_shapes=[
            pltpu.VMEM(block.shape, BF16),
            pltpu.VMEM((groups,) + block.shape, BF16),
            pltpu.SemaphoreType.DMA,
            pltpu.SemaphoreType.DMA((places // groups,)),
        ],
        cost_estimate=cost(0, 1 << 20),
        name="copies",
    )(block)
    images_all = lax.all_to_all(copies, LIB, 0, 0, tiled=False)

    tiles, keep, send = pl.pallas_call(
        tile_kernel,
        out_shape=[
            jax.ShapeDtypeStruct((2,) + plane, F32),
            jax.ShapeDtypeStruct((PART, N), BF16),
            jax.ShapeDtypeStruct((PART, N), BF16),
        ],
        grid=(1,),
        in_specs=[full(1, 1), full(N, N), full(N, N), full(*ahead.shape)],
        out_specs=[full(2, *plane), full(PART, N), full(PART, N)],
        scratch_shapes=[pltpu.VMEM((ROWS, N), F32)],
        compiler_params=params(12),
        cost_estimate=cost(200 * work, 3 << 20),
        name="tile",
    )(core, tile, received, ahead)

    pair = (keep.astype(F32) + lax.ppermute(send, "core", swap).astype(F32)).astype(BF16)
    moves = [
        lax.ppermute(pair, "z", [(z, (z + dz) % deep) for z in range(deep)])
        for dz in range(1, deep)
    ]

    table = jnp.stack([defocus_term, astig_term, astig_cross, phase_shift])
    table = jnp.pad(table, ((0, 4), (0, 128 - table.shape[1])))
    row, _ = lax.optimization_barrier((ctf_row, pair))
    mate = lax.ppermute(row, "xhi", swap)

    def gain(t, row, tables, name):
        return pl.pallas_call(
            gain_kernel,
            out_shape=[
                jax.ShapeDtypeStruct(plane, F32),
                jax.ShapeDtypeStruct((ROWS, N), F32),
            ],
            grid=(1,),
            in_specs=[
                full(1, 1),
                full(*table.shape),
                pl.BlockSpec((None,) + plane, lambda i: (t, 0, 0, 0)),
            ]
            + kept * len(tables),
            out_specs=[full(*plane), full(ROWS, N)],
            compiler_params=params(12),
            cost_estimate=cost(8 * work, 3 << 20),
            name=name,
        )(row, table, tiles, *tables)

    own = gain(0, ctf_row, (ahead, back, unfold), "gain_own")
    images_all, pair, own = lax.optimization_barrier((images_all, pair, own))

    near_all = pl.pallas_call(
        library_kernel,
        out_shape=pltpu.VMEM((deep,) + plane, BF16),
        grid=(deep // 2,),
        in_specs=kept * 2,
        out_specs=kept[0],
        compiler_params=params(12),
        cost_estimate=cost(deep * work, 4 << 20),
        name="library",
    )(images_all.reshape(groups, deep, N // groups, N), ahead)
    far_all = lax.ppermute(near_all, "core", swap)
    moves, near_all, mate = lax.optimization_barrier((moves, near_all, mate))
    other = gain(1, mate, (), "gain_other")
    mine = sum((m.astype(F32) for m in moves), pair.astype(F32)).astype(BF16)
    theirs = lax.ppermute(mine, "core", swap)
    white, white_weight = pl.pallas_call(
        whiten_kernel,
        out_shape=[
            pltpu.VMEM((2,) + plane, F32),
            pltpu.VMEM((2, ROWS, N), F32),
        ],
        in_specs=kept * 9,
        out_specs=kept * 2,
        compiler_params=params(12),
        cost_estimate=cost(60 * work, 4 << 20),
        name="whiten",
    )(core, *own, *other, mine, theirs, back, unfold)

    def match(t, dtype, name):
        return pl.pallas_call(
            functools.partial(match_kernel, t),
            out_shape=pltpu.VMEM((N, N), dtype),
            grid=(deep // 2,),
            in_specs=kept * 6,
            out_specs=kept[0],
            scratch_shapes=[pltpu.VMEM(plane, F32)],
            compiler_params=params(12),
            cost_estimate=cost(2 * deep * 2 * work, 6 << 20),
            name=name,
        )(near_all, far_all, white, white_weight, back, unfold)

    got = lax.ppermute(match(1, BF16, "match_other"), "xhi", swap)
    best = match(0, F32, "match_own")
    return jnp.maximum(best, got.astype(F32))[None, None]


def solution(mesh):
    fine = Mesh(mesh.devices.reshape(2, 4, 4, 2, 2), DEF + BLK)
    in_specs = (P(DEF, BLK, None, None), P(BLK, DEF, None), P(DEF, BLK), P(), P(), P(), P())
    out_specs = P(DEF, BLK, None, None)
    return jax.shard_map(
        per_device, mesh=fine, in_specs=in_specs, out_specs=out_specs, check_vma=False
    )
```

```python
import functools
import math

import jax
import jax.numpy as jnp
import ml_dtypes
import numpy as np
from jax import lax
from jax.experimental import pallas as pl
from jax.experimental.pallas import tpu as pltpu
from jax.sharding import Mesh
from jax.sharding import PartitionSpec as P

DEF = ("xlo", "y")
BLK = ("z", "xhi", "core")
LIB = ("xlo", "y", "z")
N = 384
HALF = N // 2
THIRD = N // 3
BLOCKS = (64, 64, 72)
ROWS = sum(BLOCKS)
SPLIT = 96
PART = ROWS - SPLIT
FOLD = 208
ROOT = math.sqrt(3.0) / 2.0
F32 = jnp.float32
BF16 = jnp.bfloat16


def tables():
    j = np.arange(N)
    phase = (j[:, None] * j[None, :]) % N
    cos = np.cos(2.0 * np.pi * phase / N)
    sin = np.sin(2.0 * np.pi * phase / N)
    bf = ml_dtypes.bfloat16
    u = np.concatenate([3 * np.arange(b) + c for c, b in zip((1, 2, 0), BLOCKS)])
    keep = (u <= HALF)[:, None]
    u = np.minimum(u, HALF)
    r = np.arange(THIRD)
    b1, b2 = BLOCKS[0], BLOCKS[0] + BLOCKS[1]
    real = np.concatenate([(keep * cos[u])[b2:, r], (keep * -sin[u])[b2:, r]])
    c1, s1 = cos[u[:b1]][:, r], sin[u[:b1]][:, r]
    c2, s2 = cos[u[b1:b2]][:, r], sin[u[b1:b2]][:, r]
    pair = np.block([[c1, s1], [c2, -s2], [-s1, c1], [-s2, -c2]])
    ahead, back = [], []
    for k in range(3):
        ck = cos[r][:, 3 * r + k]
        sk = sin[r][:, 3 * r + k]
        ahead.append(np.block([[ck, -sk], [sk, ck]]))
        back.append(np.block([[ck.T, sk.T], [-sk.T, ck.T]]))
    ahead, back = np.stack(ahead), np.stack(back)
    weight = np.where((u == 0) | (u == HALF), 1.0, 2.0) * keep[:, 0]
    fold = np.zeros((2, ROWS, ROWS))
    fold[0, : HALF + 1] = cos[: HALF + 1][:, u].astype(bf).astype(float) * weight
    fold[1, : HALF + 1] = sin[: HALF + 1][:, u].astype(bf).astype(float) * weight
    unfold = np.zeros((HALF, 2 * ROWS))
    unfold[0, HALF] = 1.0
    for i in range(1, HALF):
        unfold[i, ROWS + HALF - i] = 1.0
    ahead_all = np.concatenate([ahead.reshape(-1, 2 * THIRD), pair, np.pad(real, ((0, 0), (0, THIRD)))])
    pad = ((0, 0), (0, FOLD - ROWS), (0, 2 * THIRD - ROWS))
    back_all = np.concatenate([back.reshape(-1, 2 * THIRD), np.pad(fold, pad).reshape(-1, 2 * THIRD)])
    return [jnp.asarray(a.astype(bf)) for a in (ahead_all, back_all, unfold)]


def dot(a, b):
    return jnp.dot(a, b, preferred_element_type=F32)


def row_numbers():
    i = lax.broadcasted_iota(jnp.int32, (ROWS, N), 0)
    k = lax.broadcasted_iota(jnp.int32, (ROWS, N), 1)
    b1, b2 = BLOCKS[0], BLOCKS[0] + BLOCKS[1]
    u = jnp.where(i < b1, 3 * i + 1, jnp.where(i < b2, 3 * (i - b1) + 2, 3 * (i - b2)))
    v = jnp.where(
        k < THIRD, 3 * k, jnp.where(k < 2 * THIRD, 3 * (k - THIRD) + 1, 3 * (k - 2 * THIRD) + 2)
    )
    return u, v


def row_scale(u):
    return jnp.where((u > 0) & (u < HALF), 2.0, jnp.where(u <= HALF, 1.0, 0.0))


def copy_kernel(block_in, out_ref, block_ref, wide_sc, sem, sems):
    fetch = pltpu.make_async_copy(block_in, block_ref, sem)
    fetch.start()
    fetch.wait()
    count = wide_sc.shape[0]
    wide_sc[...] = jnp.broadcast_to(block_ref[...][None], wide_sc.shape)
    moves = [
        pltpu.make_async_copy(wide_sc, out_ref.at[pl.ds(i * count, count)], sems.at[i])
        for i in range(out_ref.shape[0] // count)
    ]
    for move in moves:
        move.start()
    for move in moves:
        move.wait()


def sine(x):
    x = x - jnp.round(x)
    a = jnp.abs(x)
    a = jnp.minimum(a, 0.5 - a)
    s = a * a
    p = jnp.full_like(x, -15.0946425768229800)
    for c in (
        42.0586939448600400,
        -76.7058597530613900,
        81.6052492760750400,
        -41.3417022403997600,
        6.28318530717958648,
    ):
        p = p * s + c
    p = p * a
    return jnp.where(x < 0.0, -p, p)


def half_spectrum(image, tab):
    wide = 2 * THIRD
    pair, real = tab[3 * wide : 4 * wide, :], tab[4 * wide :, :THIRD]
    image = image.astype(F32)
    x0, x1, x2 = image[:THIRD], image[THIRD : 2 * THIRD], image[2 * THIRD :]
    plus, minus = x1 + x2, x1 - x2
    f0 = (x0 + plus).astype(BF16)
    f1 = jnp.concatenate([(x0 - 0.5 * plus).astype(BF16), (-ROOT * minus).astype(BF16)], axis=0)
    low = dot(real, f0)
    high = dot(pair, f1)
    b, c = BLOCKS[0] + BLOCKS[1], BLOCKS[2]
    re = jnp.concatenate([high[:b], low[:c]], axis=0)
    im = jnp.concatenate([high[b:], low[c:]], axis=0)
    r0, r1, r2 = re[:, :THIRD], re[:, THIRD : 2 * THIRD], re[:, 2 * THIRD :]
    i0, i1, i2 = im[:, :THIRD], im[:, THIRD : 2 * THIRD], im[:, 2 * THIRD :]
    rp, rm = r1 + r2, ROOT * (r1 - r2)
    ip, im_ = i1 + i2, ROOT * (i1 - i2)
    rh, ih = r0 - 0.5 * rp, i0 - 0.5 * ip
    parts = ((r0 + rp, i0 + ip), (rh + im_, ih - rm), (rh - im_, ih + rm))
    result = []
    for k, (a, b) in enumerate(parts):
        lhs = jnp.concatenate([a.astype(BF16), b.astype(BF16)], axis=1)
        out = dot(lhs, tab[k * wide : (k + 1) * wide, :])
        result.append((out[:, :THIRD], out[:, THIRD:]))
    return result


def store_spectrum(ref, parts):
    for k, (re, im) in enumerate(parts):
        at = slice(k * THIRD, (k + 1) * THIRD)
        ref[0, :, at] = re.astype(ref.dtype)
        ref[1, :, at] = im.astype(ref.dtype)


def ctf_factors(row, table):
    lane = lax.broadcasted_iota(jnp.int32, table.shape, 1).astype(F32)
    chosen = jnp.sum(jnp.where(lane == row, table, 0.0), axis=1, keepdims=True)
    chosen = chosen * (1.0 / (2.0 * math.pi))
    u, v = row_numbers()
    row = jnp.where(u < HALF, u, u - N).astype(F32) * (1.0 / N)
    col = jnp.where(v < HALF, v, v - N).astype(F32) * (1.0 / N)
    r2, c2 = row * row, col * col
    base = chosen[0:1] * (r2 + c2) + chosen[1:2] * (r2 - c2) + chosen[3:4]
    cross = chosen[2:3] * (2.0 * row * col)
    plus = -sine(base + cross)
    at = slice(0, THIRD)
    inner = (u[:, at] > 0) & (u[:, at] < HALF) & (v[:, at] == HALF)
    mirror = jnp.where(inner, -sine(base[:, at] - cross[:, at]), plus[:, at])
    gain = jnp.concatenate([0.5 * (plus[:, at] + mirror), plus[:, THIRD:]], axis=1)
    square = plus * plus
    square = jnp.concatenate(
        [0.5 * (square[:, at] + mirror * mirror), square[:, THIRD:]], axis=1
    )
    return gain, row_scale(u) * square


def tile_kernel(core_ref, own_ref, other_ref, tab_ref, spec_ref, keep_ref, send_ref, power_sc):
    for t, ref in enumerate((own_ref, other_ref)):
        parts = half_spectrum(ref[...], tab_ref)
        store_spectrum(spec_ref.at[t], parts)
        for k, (re, im) in enumerate(parts):
            at = slice(k * THIRD, (k + 1) * THIRD)
            square = re * re + im * im
            power_sc[:, at] = square if t == 0 else power_sc[:, at] + square
    low, high = power_sc[:PART], power_sc[SPLIT:]
    first = core_ref[...] == 0
    keep_ref[...] = jnp.where(first, low, high).astype(BF16)
    send_ref[...] = jnp.where(first, high, low).astype(BF16)


def gain_kernel(t, row_ref, table_ref, tile_ref, *refs):
    spec_ref, weight_ref = refs[-2:]
    gain, weight_ref[...] = ctf_factors(row_ref[...].astype(F32), table_ref[...])
    spec_ref[0] = tile_ref[t, 0] * gain
    spec_ref[1] = tile_ref[t, 1] * gain


def library_kernel(image_ref, tab_ref, out_ref):
    step = pl.program_id(0)
    for i in range(2):
        image = image_ref[:, 2 * step + i].reshape(N, N)
        store_spectrum(out_ref.at[2 * step + i], half_spectrum(image, tab_ref))


def whiten_kernel(
    core_ref, own_ref, own_weight_ref, spec_ref, weight_ref, mine_ref, theirs_ref, *refs
):
    spec_out, weight_out = refs[-2:]
    mine, theirs = mine_ref[...].astype(F32), theirs_ref[...].astype(F32)
    first = core_ref[...] == 0
    low, high = jnp.where(first, mine, theirs), jnp.where(first, theirs, mine)
    power = jnp.concatenate([low[:SPLIT], high], axis=0) * (1.0 / 16.0)
    u, _ = row_numbers()
    mean = jnp.sum(power * row_scale(u)) * (1.0 / (N * N))
    inverse_noise = 1.0 / (jnp.where(u <= HALF, power, 1.0) + 0.05 * mean)
    for t, (spec, weight) in enumerate(((own_ref, own_weight_ref), (spec_ref, weight_ref))):
        spec_out[t, 0] = spec[0] * inverse_noise
        spec_out[t, 1] = spec[1] * inverse_noise
        weight_out[t] = weight[...] * inverse_noise


def match_kernel(
    t, near_ref, far_ref, spec_ref, weight_ref, tab_ref, unfold_ref, out_ref, p_sc, h_sc, best_sc
):
    wide = 2 * THIRD
    count = 2 * near_ref.shape[0]
    s_re, s_im = spec_ref[t, 0], spec_ref[t, 1]
    scales = []
    for j in range(count):
        ref = (near_ref, far_ref)[j % 2]
        re, im = ref[j // 2, 0].astype(F32), ref[j // 2, 1].astype(F32)
        norm = jnp.sum((re * re + im * im) * weight_ref[t])
        scales.append(lax.rsqrt(jnp.full((1, THIRD), norm + 1e-06, F32)))
        p_re = (s_re * re + s_im * im).astype(BF16)
        p_im = (s_im * re - s_re * im).astype(BF16)
        rows = slice(j * FOLD, j * FOLD + ROWS)
        for k in range(3):
            at = slice(k * THIRD, (k + 1) * THIRD)
            p_sc[k, rows, :THIRD] = p_re[:, at]
            p_sc[k, rows, THIRD:] = p_im[:, at]
    g = [dot(p_sc[k], tab_ref[k * wide : (k + 1) * wide, :]) for k in range(3)]
    for j, scale in enumerate(scales):
        rows = slice(j * FOLD, j * FOLD + ROWS)
        (r0, i0), (r1, i1), (r2, i2) = ((x[rows, :THIRD], x[rows, THIRD:]) for x in g)
        slant = scale * ROOT
        rp, rm = r1 + r2, slant * (r1 - r2)
        ip, im_ = i1 + i2, slant * (i1 - i2)
        rh, ih = scale * (r0 - 0.5 * rp), scale * (i0 - 0.5 * ip)
        h_re = (scale * (r0 + rp), rh - im_, rh + im_)
        h_im = (scale * (i0 + ip), ih + rm, ih - rm)
        for k in range(3):
            at = slice(j * N + k * THIRD, j * N + (k + 1) * THIRD)
            h_sc[0, :, at] = h_re[k].astype(BF16)
            h_sc[1, :, at] = h_im[k].astype(BF16)
    first = 3 * wide
    even = dot(tab_ref[first : first + ROWS, :ROWS], h_sc[0])
    odd = dot(tab_ref[first + FOLD : first + FOLD + ROWS, :ROWS], h_sc[1])
    minus, plus = even[:, :N] - odd[:, :N], even[:, :N] + odd[:, :N]
    for j in range(1, count):
        at = slice(j * N, (j + 1) * N)
        minus = jnp.maximum(minus, even[:, at] - odd[:, at])
        plus = jnp.maximum(plus, even[:, at] + odd[:, at])
    best_sc[0] = minus
    best_sc[1] = plus
    out_ref[:HALF] = best_sc[0, :HALF].astype(out_ref.dtype)
    rest = best_sc[...].reshape(2 * ROWS, N)
    total = None
    for _ in range(3 if out_ref.dtype == F32 else 1):
        part = rest.astype(BF16)
        rest = rest - part.astype(F32)
        moved = dot(unfold_ref[...], part)
        total = moved if total is None else total + moved
    out_ref[HALF:] = total.astype(out_ref.dtype)


def full(*shape):
    return pl.BlockSpec(shape, lambda i: (0,) * len(shape))


def cost(flops, size):
    return pl.CostEstimate(flops=flops, bytes_accessed=size, transcendentals=0)


def params(mib):
    return pltpu.CompilerParams(vmem_limit_bytes=mib << 20)


def per_device(images, projections, ctf_row, defocus_term, astig_term, astig_cross, phase_shift):
    ahead, back, unfold = tables()
    groups = math.prod(lax.axis_size(a) for a in DEF)
    places = math.prod(lax.axis_size(a) for a in LIB)
    deep, wide = lax.axis_size("z"), lax.axis_size("xhi")
    core = lax.axis_index("core").astype(jnp.int32).reshape(1, 1)
    swap = [(0, 1), (1, 0)]
    kept = [pl.BlockSpec(memory_space=pltpu.VMEM)]
    plane = (2, ROWS, N)
    work = 2 * ROWS * 768 * 256 * 2

    tile = images[0, 0]
    block = projections[0]
    received = lax.ppermute(tile, "xhi", swap)
    copies = pl.pallas_call(
        copy_kernel,
        out_shape=pltpu.HBM((places,) + block.shape, BF16),
        in_specs=[pl.BlockSpec(memory_space=pltpu.HBM)],
        out_specs=pl.BlockSpec(memory_space=pltpu.HBM),
        scratch_shapes=[
            pltpu.VMEM(block.shape, BF16),
            pltpu.VMEM((groups,) + block.shape, BF16),
            pltpu.SemaphoreType.DMA,
            pltpu.SemaphoreType.DMA((places // groups,)),
        ],
        cost_estimate=cost(0, 1 << 20),
        name="copies",
    )(block)
    images_all = lax.all_to_all(copies, LIB, 0, 0, tiled=False)

    tiles, keep, send = pl.pallas_call(
        tile_kernel,
        out_shape=[
            jax.ShapeDtypeStruct((2,) + plane, F32),
            jax.ShapeDtypeStruct((PART, N), BF16),
            jax.ShapeDtypeStruct((PART, N), BF16),
        ],
        grid=(1,),
        in_specs=[full(1, 1), full(N, N), full(N, N), full(*ahead.shape)],
        out_specs=[full(2, *plane), full(PART, N), full(PART, N)],
        scratch_shapes=[pltpu.VMEM((ROWS, N), F32)],
        compiler_params=params(12),
        cost_estimate=cost(200 * work, 3 << 20),
        name="tile",
    )(core, tile, received, ahead)

    pair = (keep.astype(F32) + lax.ppermute(send, "core", swap).astype(F32)).astype(BF16)
    moves = [
        lax.ppermute(pair, "z", [(z, (z + dz) % deep) for z in range(deep)])
        for dz in range(1, deep)
    ]

    table = jnp.stack([defocus_term, astig_term, astig_cross, phase_shift])
    table = jnp.pad(table, ((0, 4), (0, 128 - table.shape[1])))
    row, _ = lax.optimization_barrier((ctf_row, pair))
    mate = lax.ppermute(row, "xhi", swap)

    def gain(t, row, tables, name):
        return pl.pallas_call(
            functools.partial(gain_kernel, t),
            out_shape=[
                pltpu.VMEM(plane, F32),
                pltpu.VMEM((ROWS, N), F32),
            ],
            in_specs=[full(1, 1)] + kept * (2 + len(tables)),
            out_specs=kept * 2,
            grid=(1,),
            compiler_params=params(12),
            cost_estimate=cost(8 * work, 3 << 20),
            name=name,
        )(row, table, tiles, *tables)

    own = gain(0, ctf_row, (ahead, back, unfold), "gain_own")
    images_all, pair, own = lax.optimization_barrier((images_all, pair, own))

    near_all = pl.pallas_call(
        library_kernel,
        out_shape=pltpu.VMEM((deep,) + plane, BF16),
        grid=(deep // 2,),
        in_specs=kept * 2,
        out_specs=kept[0],
        compiler_params=params(12),
        cost_estimate=cost(deep * work, 4 << 20),
        name="library",
    )(images_all.reshape(groups, deep, N // groups, N), ahead)
    far_all = lax.ppermute(near_all, "core", swap)
    moves, near_all, mate = lax.optimization_barrier((moves, near_all, mate))
    other = gain(1, mate, (), "gain_other")
    mine = sum((m.astype(F32) for m in moves), pair.astype(F32)).astype(BF16)
    theirs = lax.ppermute(mine, "core", swap)
    white, white_weight = pl.pallas_call(
        whiten_kernel,
        out_shape=[
            pltpu.VMEM((2,) + plane, F32),
            pltpu.VMEM((2, ROWS, N), F32),
        ],
        in_specs=kept * 9,
        out_specs=kept * 2,
        compiler_params=params(12),
        cost_estimate=cost(60 * work, 4 << 20),
        name="whiten",
    )(core, *own, *other, mine, theirs, back, unfold)

    def match(t, dtype, name):
        return pl.pallas_call(
            functools.partial(match_kernel, t),
            out_shape=pltpu.VMEM((N, N), dtype),
            in_specs=kept * 6,
            out_specs=kept[0],
            scratch_shapes=[
                pltpu.VMEM((3, 2 * deep * FOLD, 2 * THIRD), BF16),
                pltpu.VMEM((2, ROWS, 2 * deep * N), BF16),
                pltpu.VMEM(plane, F32),
            ],
            compiler_params=params(24),
            cost_estimate=cost(2 * deep * 2 * work, 6 << 20),
            name=name,
        )(near_all, far_all, white, white_weight, back, unfold)

    got = lax.ppermute(match(1, BF16, "match_other"), "xhi", swap)
    best = match(0, F32, "match_own")
    return jnp.maximum(best, got.astype(F32))[None, None]


def solution(mesh):
    fine = Mesh(mesh.devices.reshape(2, 4, 4, 2, 2), DEF + BLK)
    in_specs = (P(DEF, BLK, None, None), P(BLK, DEF, None), P(DEF, BLK), P(), P(), P(), P())
    out_specs = P(DEF, BLK, None, None)
    return jax.shard_map(
        per_device, mesh=fine, in_specs=in_specs, out_specs=out_specs, check_vma=False
    )
```

```python
import functools
import math

import jax
import jax.numpy as jnp
import ml_dtypes
import numpy as np
from jax import lax
from jax.experimental import pallas as pl
from jax.experimental.pallas import tpu as pltpu
from jax.sharding import Mesh
from jax.sharding import PartitionSpec as P

DEF = ("xlo", "y")
BLK = ("z", "xhi", "core")
LIB = ("xlo", "y", "z")
N = 384
HALF = N // 2
THIRD = N // 3
BLOCKS = (64, 64, 72)
ROWS = sum(BLOCKS)
SPLIT = 96
PART = ROWS - SPLIT
FOLD = 208
ROOT = math.sqrt(3.0) / 2.0
F32 = jnp.float32
BF16 = jnp.bfloat16


def tables():
    j = np.arange(N)
    phase = (j[:, None] * j[None, :]) % N
    cos = np.cos(2.0 * np.pi * phase / N)
    sin = np.sin(2.0 * np.pi * phase / N)
    bf = ml_dtypes.bfloat16
    u = np.concatenate([3 * np.arange(b) + c for c, b in zip((1, 2, 0), BLOCKS)])
    keep = (u <= HALF)[:, None]
    u = np.minimum(u, HALF)
    r = np.arange(THIRD)
    b1, b2 = BLOCKS[0], BLOCKS[0] + BLOCKS[1]
    real = np.concatenate([(keep * cos[u])[b2:, r], (keep * -sin[u])[b2:, r]])
    c1, s1 = cos[u[:b1]][:, r], sin[u[:b1]][:, r]
    c2, s2 = cos[u[b1:b2]][:, r], sin[u[b1:b2]][:, r]
    pair = np.block([[c1, s1], [c2, -s2], [-s1, c1], [-s2, -c2]])
    ahead, back = [], []
    for k in range(3):
        ck = cos[r][:, 3 * r + k]
        sk = sin[r][:, 3 * r + k]
        ahead.append(np.block([[ck, -sk], [sk, ck]]))
        back.append(np.block([[ck.T, sk.T], [-sk.T, ck.T]]))
    ahead, back = np.stack(ahead), np.stack(back)
    weight = np.where((u == 0) | (u == HALF), 1.0, 2.0) * keep[:, 0]
    fold = np.zeros((2, ROWS, ROWS))
    fold[0, : HALF + 1] = cos[: HALF + 1][:, u].astype(bf).astype(float) * weight
    fold[1, : HALF + 1] = sin[: HALF + 1][:, u].astype(bf).astype(float) * weight
    unfold = np.zeros((HALF, 2 * ROWS))
    unfold[0, HALF] = 1.0
    for i in range(1, HALF):
        unfold[i, ROWS + HALF - i] = 1.0
    ahead_all = np.concatenate([ahead.reshape(-1, 2 * THIRD), pair, np.pad(real, ((0, 0), (0, THIRD)))])
    pad = ((0, 0), (0, FOLD - ROWS), (0, 2 * THIRD - ROWS))
    back_all = np.concatenate([back.reshape(-1, 2 * THIRD), np.pad(fold, pad).reshape(-1, 2 * THIRD)])
    return [jnp.asarray(a.astype(bf)) for a in (ahead_all, back_all, unfold)]


def dot(a, b):
    return jnp.dot(a, b, preferred_element_type=F32)


def row_numbers():
    i = lax.broadcasted_iota(jnp.int32, (ROWS, N), 0)
    k = lax.broadcasted_iota(jnp.int32, (ROWS, N), 1)
    b1, b2 = BLOCKS[0], BLOCKS[0] + BLOCKS[1]
    u = jnp.where(i < b1, 3 * i + 1, jnp.where(i < b2, 3 * (i - b1) + 2, 3 * (i - b2)))
    v = jnp.where(
        k < THIRD, 3 * k, jnp.where(k < 2 * THIRD, 3 * (k - THIRD) + 1, 3 * (k - 2 * THIRD) + 2)
    )
    return u, v


def row_scale(u):
    return jnp.where((u > 0) & (u < HALF), 2.0, jnp.where(u <= HALF, 1.0, 0.0))


def copy_kernel(block_in, out_ref, block_ref, wide_sc, sem, sems):
    fetch = pltpu.make_async_copy(block_in, block_ref, sem)
    fetch.start()
    fetch.wait()
    count = wide_sc.shape[0]
    wide_sc[...] = jnp.broadcast_to(block_ref[...][None], wide_sc.shape)
    moves = [
        pltpu.make_async_copy(wide_sc, out_ref.at[pl.ds(i * count, count)], sems.at[i])
        for i in range(out_ref.shape[0] // count)
    ]
    for move in moves:
        move.start()
    for move in moves:
        move.wait()


def sine(x):
    x = x - jnp.round(x)
    a = jnp.abs(x)
    a = jnp.minimum(a, 0.5 - a)
    s = a * a
    p = jnp.full_like(x, -15.0946425768229800)
    for c in (
        42.0586939448600400,
        -76.7058597530613900,
        81.6052492760750400,
        -41.3417022403997600,
        6.28318530717958648,
    ):
        p = p * s + c
    p = p * a
    return jnp.where(x < 0.0, -p, p)


def half_spectrum(image, tab):
    wide = 2 * THIRD
    pair, real = tab[3 * wide : 4 * wide, :], tab[4 * wide :, :THIRD]
    image = image.astype(F32)
    x0, x1, x2 = image[:THIRD], image[THIRD : 2 * THIRD], image[2 * THIRD :]
    plus, minus = x1 + x2, x1 - x2
    f0 = (x0 + plus).astype(BF16)
    f1 = jnp.concatenate([(x0 - 0.5 * plus).astype(BF16), (-ROOT * minus).astype(BF16)], axis=0)
    low = dot(real, f0)
    high = dot(pair, f1)
    b, c = BLOCKS[0] + BLOCKS[1], BLOCKS[2]
    re = jnp.concatenate([high[:b], low[:c]], axis=0)
    im = jnp.concatenate([high[b:], low[c:]], axis=0)
    r0, r1, r2 = re[:, :THIRD], re[:, THIRD : 2 * THIRD], re[:, 2 * THIRD :]
    i0, i1, i2 = im[:, :THIRD], im[:, THIRD : 2 * THIRD], im[:, 2 * THIRD :]
    rp, rm = r1 + r2, ROOT * (r1 - r2)
    ip, im_ = i1 + i2, ROOT * (i1 - i2)
    rh, ih = r0 - 0.5 * rp, i0 - 0.5 * ip
    parts = ((r0 + rp, i0 + ip), (rh + im_, ih - rm), (rh - im_, ih + rm))
    result = []
    for k, (a, b) in enumerate(parts):
        lhs = jnp.concatenate([a.astype(BF16), b.astype(BF16)], axis=1)
        out = dot(lhs, tab[k * wide : (k + 1) * wide, :])
        result.append((out[:, :THIRD], out[:, THIRD:]))
    return result


def store_spectrum(ref, parts):
    for k, (re, im) in enumerate(parts):
        at = slice(k * THIRD, (k + 1) * THIRD)
        ref[0, :, at] = re.astype(ref.dtype)
        ref[1, :, at] = im.astype(ref.dtype)


def ctf_factors(row, table):
    lane = lax.broadcasted_iota(jnp.int32, table.shape, 1).astype(F32)
    chosen = jnp.sum(jnp.where(lane == row, table, 0.0), axis=1, keepdims=True)
    chosen = chosen * (1.0 / (2.0 * math.pi))
    u, v = row_numbers()
    row = jnp.where(u < HALF, u, u - N).astype(F32) * (1.0 / N)
    col = jnp.where(v < HALF, v, v - N).astype(F32) * (1.0 / N)
    r2, c2 = row * row, col * col
    base = chosen[0:1] * (r2 + c2) + chosen[1:2] * (r2 - c2) + chosen[3:4]
    cross = chosen[2:3] * (2.0 * row * col)
    plus = -sine(base + cross)
    at = slice(0, THIRD)
    inner = (u[:, at] > 0) & (u[:, at] < HALF) & (v[:, at] == HALF)
    mirror = jnp.where(inner, -sine(base[:, at] - cross[:, at]), plus[:, at])
    gain = jnp.concatenate([0.5 * (plus[:, at] + mirror), plus[:, THIRD:]], axis=1)
    square = plus * plus
    square = jnp.concatenate(
        [0.5 * (square[:, at] + mirror * mirror), square[:, THIRD:]], axis=1
    )
    return gain, row_scale(u) * square


def tile_kernel(core_ref, own_ref, other_ref, tab_ref, spec_ref, keep_ref, send_ref, power_sc):
    for t, ref in enumerate((own_ref, other_ref)):
        parts = half_spectrum(ref[...], tab_ref)
        store_spectrum(spec_ref.at[t], parts)
        for k, (re, im) in enumerate(parts):
            at = slice(k * THIRD, (k + 1) * THIRD)
            square = re * re + im * im
            power_sc[:, at] = square if t == 0 else power_sc[:, at] + square
    low, high = power_sc[:PART], power_sc[SPLIT:]
    first = core_ref[...] == 0
    keep_ref[...] = jnp.where(first, low, high).astype(BF16)
    send_ref[...] = jnp.where(first, high, low).astype(BF16)


def gain_kernel(t, row_ref, table_ref, tile_ref, *refs):
    spec_ref, weight_ref = refs[-2:]
    gain, weight_ref[...] = ctf_factors(row_ref[...].astype(F32), table_ref[...])
    spec_ref[0] = tile_ref[t, 0] * gain
    spec_ref[1] = tile_ref[t, 1] * gain


def library_kernel(first, image_ref, tab_ref, out_ref):
    for i in range(out_ref.shape[0]):
        image = image_ref[:, first + i].reshape(N, N)
        store_spectrum(out_ref.at[i], half_spectrum(image, tab_ref))


def whiten_kernel(
    core_ref, own_ref, own_weight_ref, spec_ref, weight_ref, mine_ref, theirs_ref, *refs
):
    spec_out, weight_out = refs[-2:]
    mine, theirs = mine_ref[...].astype(F32), theirs_ref[...].astype(F32)
    first = core_ref[...] == 0
    low, high = jnp.where(first, mine, theirs), jnp.where(first, theirs, mine)
    power = jnp.concatenate([low[:SPLIT], high], axis=0) * (1.0 / 16.0)
    u, _ = row_numbers()
    mean = jnp.sum(power * row_scale(u)) * (1.0 / (N * N))
    inverse_noise = 1.0 / (jnp.where(u <= HALF, power, 1.0) + 0.05 * mean)
    for t, (spec, weight) in enumerate(((own_ref, own_weight_ref), (spec_ref, weight_ref))):
        spec_out[t, 0] = spec[0] * inverse_noise
        spec_out[t, 1] = spec[1] * inverse_noise
        weight_out[t] = weight[...] * inverse_noise


def match_kernel(t, *refs):
    libs, refs = refs[:4], refs[4:]
    spec_ref, weight_ref, tab_ref, unfold_ref, out_ref, p_sc, h_sc, best_sc = refs
    wide = 2 * THIRD
    count = 4 * libs[0].shape[0]
    s_re, s_im = spec_ref[t, 0], spec_ref[t, 1]
    scales = []
    for j in range(count):
        ref = libs[j % 4]
        re, im = ref[j // 4, 0].astype(F32), ref[j // 4, 1].astype(F32)
        norm = jnp.sum((re * re + im * im) * weight_ref[t])
        scales.append(lax.rsqrt(jnp.full((1, THIRD), norm + 1e-06, F32)))
        p_re = (s_re * re + s_im * im).astype(BF16)
        p_im = (s_im * re - s_re * im).astype(BF16)
        rows = slice(j * FOLD, j * FOLD + ROWS)
        for k in range(3):
            at = slice(k * THIRD, (k + 1) * THIRD)
            p_sc[k, rows, :THIRD] = p_re[:, at]
            p_sc[k, rows, THIRD:] = p_im[:, at]
    g = [dot(p_sc[k], tab_ref[k * wide : (k + 1) * wide, :]) for k in range(3)]
    for j, scale in enumerate(scales):
        rows = slice(j * FOLD, j * FOLD + ROWS)
        (r0, i0), (r1, i1), (r2, i2) = ((x[rows, :THIRD], x[rows, THIRD:]) for x in g)
        slant = scale * ROOT
        rp, rm = r1 + r2, slant * (r1 - r2)
        ip, im_ = i1 + i2, slant * (i1 - i2)
        rh, ih = scale * (r0 - 0.5 * rp), scale * (i0 - 0.5 * ip)
        h_re = (scale * (r0 + rp), rh - im_, rh + im_)
        h_im = (scale * (i0 + ip), ih + rm, ih - rm)
        for k in range(3):
            at = slice(j * N + k * THIRD, j * N + (k + 1) * THIRD)
            h_sc[0, :, at] = h_re[k].astype(BF16)
            h_sc[1, :, at] = h_im[k].astype(BF16)
    first = 3 * wide
    even = dot(tab_ref[first : first + ROWS, :ROWS], h_sc[0])
    odd = dot(tab_ref[first + FOLD : first + FOLD + ROWS, :ROWS], h_sc[1])
    minus, plus = even[:, :N] - odd[:, :N], even[:, :N] + odd[:, :N]
    for j in range(1, count):
        at = slice(j * N, (j + 1) * N)
        minus = jnp.maximum(minus, even[:, at] - odd[:, at])
        plus = jnp.maximum(plus, even[:, at] + odd[:, at])
    best_sc[0] = minus
    best_sc[1] = plus
    out_ref[:HALF] = best_sc[0, :HALF].astype(out_ref.dtype)
    rest = best_sc[...].reshape(2 * ROWS, N)
    total = None
    for _ in range(3 if out_ref.dtype == F32 else 1):
        part = rest.astype(BF16)
        rest = rest - part.astype(F32)
        moved = dot(unfold_ref[...], part)
        total = moved if total is None else total + moved
    out_ref[HALF:] = total.astype(out_ref.dtype)


def full(*shape):
    return pl.BlockSpec(shape, lambda i: (0,) * len(shape))


def cost(flops, size):
    return pl.CostEstimate(flops=flops, bytes_accessed=size, transcendentals=0)


def params(mib):
    return pltpu.CompilerParams(vmem_limit_bytes=mib << 20)


def per_device(images, projections, ctf_row, defocus_term, astig_term, astig_cross, phase_shift):
    ahead, back, unfold = tables()
    groups = math.prod(lax.axis_size(a) for a in DEF)
    places = math.prod(lax.axis_size(a) for a in LIB)
    deep, wide = lax.axis_size("z"), lax.axis_size("xhi")
    core = lax.axis_index("core").astype(jnp.int32).reshape(1, 1)
    swap = [(0, 1), (1, 0)]
    kept = [pl.BlockSpec(memory_space=pltpu.VMEM)]
    plane = (2, ROWS, N)
    work = 2 * ROWS * 768 * 256 * 2

    tile = images[0, 0]
    block = projections[0]
    received = lax.ppermute(tile, "xhi", swap)
    copies = pl.pallas_call(
        copy_kernel,
        out_shape=pltpu.HBM((places,) + block.shape, BF16),
        in_specs=[pl.BlockSpec(memory_space=pltpu.HBM)],
        out_specs=pl.BlockSpec(memory_space=pltpu.HBM),
        scratch_shapes=[
            pltpu.VMEM(block.shape, BF16),
            pltpu.VMEM((groups,) + block.shape, BF16),
            pltpu.SemaphoreType.DMA,
            pltpu.SemaphoreType.DMA((places // groups,)),
        ],
        cost_estimate=cost(0, 1 << 20),
        name="copies",
    )(block)
    images_all = lax.all_to_all(copies, LIB, 0, 0, tiled=False)

    tiles, keep, send = pl.pallas_call(
        tile_kernel,
        out_shape=[
            jax.ShapeDtypeStruct((2,) + plane, F32),
            jax.ShapeDtypeStruct((PART, N), BF16),
            jax.ShapeDtypeStruct((PART, N), BF16),
        ],
        grid=(1,),
        in_specs=[full(1, 1), full(N, N), full(N, N), full(*ahead.shape)],
        out_specs=[full(2, *plane), full(PART, N), full(PART, N)],
        scratch_shapes=[pltpu.VMEM((ROWS, N), F32)],
        compiler_params=params(12),
        cost_estimate=cost(200 * work, 3 << 20),
        name="tile",
    )(core, tile, received, ahead)

    pair = (keep.astype(F32) + lax.ppermute(send, "core", swap).astype(F32)).astype(BF16)
    moves = [
        lax.ppermute(pair, "z", [(z, (z + dz) % deep) for z in range(deep)])
        for dz in range(1, deep)
    ]

    table = jnp.stack([defocus_term, astig_term, astig_cross, phase_shift])
    table = jnp.pad(table, ((0, 4), (0, 128 - table.shape[1])))
    row, _ = lax.optimization_barrier((ctf_row, pair))
    mate = lax.ppermute(row, "xhi", swap)

    def gain(t, row, tables, name):
        return pl.pallas_call(
            functools.partial(gain_kernel, t),
            out_shape=[
                pltpu.VMEM(plane, F32),
                pltpu.VMEM((ROWS, N), F32),
            ],
            in_specs=[full(1, 1)] + kept * (2 + len(tables)),
            out_specs=kept * 2,
            grid=(1,),
            compiler_params=params(12),
            cost_estimate=cost(8 * work, 3 << 20),
            name=name,
        )(row, table, tiles, *tables)

    own = gain(0, ctf_row, (ahead, back, unfold), "gain_own")
    images_all, pair, own = lax.optimization_barrier((images_all, pair, own))

    images_all = images_all.reshape(groups, deep, N // groups, N)
    near = [
        pl.pallas_call(
            functools.partial(library_kernel, first),
            out_shape=pltpu.VMEM((deep // 2,) + plane, BF16),
            in_specs=kept * 2,
            out_specs=kept[0],
            compiler_params=params(12),
            cost_estimate=cost(deep // 2 * work, 3 << 20),
            name="library",
        )(images_all, ahead)
        for first in (0, deep // 2)
    ]
    far = [lax.ppermute(part, "core", swap) for part in near]

    moves, near, mate = lax.optimization_barrier((moves, near, mate))
    other = gain(1, mate, (), "gain_other")
    mine = sum((m.astype(F32) for m in moves), pair.astype(F32)).astype(BF16)
    theirs = lax.ppermute(mine, "core", swap)
    white, white_weight = pl.pallas_call(
        whiten_kernel,
        out_shape=[
            pltpu.VMEM((2,) + plane, F32),
            pltpu.VMEM((2, ROWS, N), F32),
        ],
        in_specs=kept * 9,
        out_specs=kept * 2,
        compiler_params=params(12),
        cost_estimate=cost(60 * work, 4 << 20),
        name="whiten",
    )(core, *own, *other, mine, theirs, back, unfold)

    def match(t, dtype, name):
        return pl.pallas_call(
            functools.partial(match_kernel, t),
            out_shape=pltpu.VMEM((N, N), dtype),
            in_specs=kept * 8,
            out_specs=kept[0],
            scratch_shapes=[
                pltpu.VMEM((3, 2 * deep * FOLD, 2 * THIRD), BF16),
                pltpu.VMEM((2, ROWS, 2 * deep * N), BF16),
                pltpu.VMEM(plane, F32),
            ],
            compiler_params=params(24),
            cost_estimate=cost(2 * deep * 2 * work, 6 << 20),
            name=name,
        )(*near, *far, white, white_weight, back, unfold)

    got = lax.ppermute(match(1, BF16, "match_other"), "xhi", swap)
    best = match(0, F32, "match_own")
    return jnp.maximum(best, got.astype(F32))[None, None]


def solution(mesh):
    fine = Mesh(mesh.devices.reshape(2, 4, 4, 2, 2), DEF + BLK)
    in_specs = (P(DEF, BLK, None, None), P(BLK, DEF, None), P(DEF, BLK), P(), P(), P(), P())
    out_specs = P(DEF, BLK, None, None)
    return jax.shard_map(
        per_device, mesh=fine, in_specs=in_specs, out_specs=out_specs, check_vma=False
    )
```

```python
import functools
import math

import jax
import jax.numpy as jnp
import ml_dtypes
import numpy as np
from jax import lax
from jax.experimental import pallas as pl
from jax.experimental.pallas import tpu as pltpu
from jax.sharding import Mesh
from jax.sharding import PartitionSpec as P

DEF = ("xlo", "y")
BLK = ("z", "xhi", "core")
LIB = ("xlo", "y", "z")
N = 384
HALF = N // 2
THIRD = N // 3
BLOCKS = (64, 64, 72)
ROWS = sum(BLOCKS)
SPLIT = 96
PART = ROWS - SPLIT
FOLD = 208
ROOT = math.sqrt(3.0) / 2.0
F32 = jnp.float32
BF16 = jnp.bfloat16


def tables():
    j = np.arange(N)
    phase = (j[:, None] * j[None, :]) % N
    cos = np.cos(2.0 * np.pi * phase / N)
    sin = np.sin(2.0 * np.pi * phase / N)
    bf = ml_dtypes.bfloat16
    u = np.concatenate([3 * np.arange(b) + c for c, b in zip((1, 2, 0), BLOCKS)])
    keep = (u <= HALF)[:, None]
    u = np.minimum(u, HALF)
    r = np.arange(THIRD)
    b1, b2 = BLOCKS[0], BLOCKS[0] + BLOCKS[1]
    real = np.concatenate([(keep * cos[u])[b2:, r], (keep * -sin[u])[b2:, r]])
    c1, s1 = cos[u[:b1]][:, r], sin[u[:b1]][:, r]
    c2, s2 = cos[u[b1:b2]][:, r], sin[u[b1:b2]][:, r]
    pair = np.block([[c1, s1], [c2, -s2], [-s1, c1], [-s2, -c2]])
    ahead, back = [], []
    for k in range(3):
        ck = cos[r][:, 3 * r + k]
        sk = sin[r][:, 3 * r + k]
        ahead.append(np.block([[ck, -sk], [sk, ck]]))
        back.append(np.block([[ck.T, sk.T], [-sk.T, ck.T]]))
    ahead, back = np.stack(ahead), np.stack(back)
    weight = np.where((u == 0) | (u == HALF), 1.0, 2.0) * keep[:, 0]
    fold = np.zeros((2, ROWS, ROWS))
    fold[0, : HALF + 1] = cos[: HALF + 1][:, u].astype(bf).astype(float) * weight
    fold[1, : HALF + 1] = sin[: HALF + 1][:, u].astype(bf).astype(float) * weight
    unfold = np.zeros((HALF, 2 * ROWS))
    unfold[0, HALF] = 1.0
    for i in range(1, HALF):
        unfold[i, ROWS + HALF - i] = 1.0
    ahead_all = np.concatenate([ahead.reshape(-1, 2 * THIRD), pair, np.pad(real, ((0, 0), (0, THIRD)))])
    pad = ((0, 0), (0, FOLD - ROWS), (0, 2 * THIRD - ROWS))
    back_all = np.concatenate([back.reshape(-1, 2 * THIRD), np.pad(fold, pad).reshape(-1, 2 * THIRD)])
    return [jnp.asarray(a.astype(bf)) for a in (ahead_all, back_all, unfold)]


def dot(a, b):
    return jnp.dot(a, b, preferred_element_type=F32)


def row_numbers():
    i = lax.broadcasted_iota(jnp.int32, (ROWS, N), 0)
    k = lax.broadcasted_iota(jnp.int32, (ROWS, N), 1)
    b1, b2 = BLOCKS[0], BLOCKS[0] + BLOCKS[1]
    u = jnp.where(i < b1, 3 * i + 1, jnp.where(i < b2, 3 * (i - b1) + 2, 3 * (i - b2)))
    v = jnp.where(
        k < THIRD, 3 * k, jnp.where(k < 2 * THIRD, 3 * (k - THIRD) + 1, 3 * (k - 2 * THIRD) + 2)
    )
    return u, v


def row_scale(u):
    return jnp.where((u > 0) & (u < HALF), 2.0, jnp.where(u <= HALF, 1.0, 0.0))


def copy_kernel(block_in, out_ref, block_ref, wide_sc, sem, sems):
    fetch = pltpu.make_async_copy(block_in, block_ref, sem)
    fetch.start()
    fetch.wait()
    count = wide_sc.shape[0]
    wide_sc[...] = jnp.broadcast_to(block_ref[...][None], wide_sc.shape)
    moves = [
        pltpu.make_async_copy(wide_sc, out_ref.at[pl.ds(i * count, count)], sems.at[i])
        for i in range(out_ref.shape[0] // count)
    ]
    for move in moves:
        move.start()
    for move in moves:
        move.wait()


def sine(x):
    x = x - jnp.round(x)
    a = jnp.abs(x)
    a = jnp.minimum(a, 0.5 - a)
    s = a * a
    p = jnp.full_like(x, -15.0946425768229800)
    for c in (
        42.0586939448600400,
        -76.7058597530613900,
        81.6052492760750400,
        -41.3417022403997600,
        6.28318530717958648,
    ):
        p = p * s + c
    p = p * a
    return jnp.where(x < 0.0, -p, p)


def half_spectrum(image, tab):
    wide = 2 * THIRD
    pair, real = tab[3 * wide : 4 * wide, :], tab[4 * wide :, :THIRD]
    image = image.astype(F32)
    x0, x1, x2 = image[:THIRD], image[THIRD : 2 * THIRD], image[2 * THIRD :]
    plus, minus = x1 + x2, x1 - x2
    f0 = (x0 + plus).astype(BF16)
    f1 = jnp.concatenate([(x0 - 0.5 * plus).astype(BF16), (-ROOT * minus).astype(BF16)], axis=0)
    low = dot(real, f0)
    high = dot(pair, f1)
    b, c = BLOCKS[0] + BLOCKS[1], BLOCKS[2]
    re = jnp.concatenate([high[:b], low[:c]], axis=0)
    im = jnp.concatenate([high[b:], low[c:]], axis=0)
    r0, r1, r2 = re[:, :THIRD], re[:, THIRD : 2 * THIRD], re[:, 2 * THIRD :]
    i0, i1, i2 = im[:, :THIRD], im[:, THIRD : 2 * THIRD], im[:, 2 * THIRD :]
    rp, rm = r1 + r2, ROOT * (r1 - r2)
    ip, im_ = i1 + i2, ROOT * (i1 - i2)
    rh, ih = r0 - 0.5 * rp, i0 - 0.5 * ip
    parts = ((r0 + rp, i0 + ip), (rh + im_, ih - rm), (rh - im_, ih + rm))
    result = []
    for k, (a, b) in enumerate(parts):
        lhs = jnp.concatenate([a.astype(BF16), b.astype(BF16)], axis=1)
        out = dot(lhs, tab[k * wide : (k + 1) * wide, :])
        result.append((out[:, :THIRD], out[:, THIRD:]))
    return result


def store_spectrum(ref, parts):
    for k, (re, im) in enumerate(parts):
        at = slice(k * THIRD, (k + 1) * THIRD)
        ref[0, :, at] = re.astype(ref.dtype)
        ref[1, :, at] = im.astype(ref.dtype)


def ctf_factors(row, table):
    lane = lax.broadcasted_iota(jnp.int32, table.shape, 1).astype(F32)
    chosen = jnp.sum(jnp.where(lane == row, table, 0.0), axis=1, keepdims=True)
    chosen = chosen * (1.0 / (2.0 * math.pi))
    u, v = row_numbers()
    row = jnp.where(u < HALF, u, u - N).astype(F32) * (1.0 / N)
    col = jnp.where(v < HALF, v, v - N).astype(F32) * (1.0 / N)
    r2, c2 = row * row, col * col
    base = chosen[0:1] * (r2 + c2) + chosen[1:2] * (r2 - c2) + chosen[3:4]
    cross = chosen[2:3] * (2.0 * row * col)
    plus = -sine(base + cross)
    at = slice(0, THIRD)
    inner = (u[:, at] > 0) & (u[:, at] < HALF) & (v[:, at] == HALF)
    mirror = jnp.where(inner, -sine(base[:, at] - cross[:, at]), plus[:, at])
    gain = jnp.concatenate([0.5 * (plus[:, at] + mirror), plus[:, THIRD:]], axis=1)
    square = plus * plus
    square = jnp.concatenate(
        [0.5 * (square[:, at] + mirror * mirror), square[:, THIRD:]], axis=1
    )
    return gain, row_scale(u) * square


def tile_kernel(core_ref, own_ref, other_ref, tab_ref, spec_ref, keep_ref, send_ref, power_sc):
    for t, ref in enumerate((own_ref, other_ref)):
        parts = half_spectrum(ref[...], tab_ref)
        store_spectrum(spec_ref.at[t], parts)
        for k, (re, im) in enumerate(parts):
            at = slice(k * THIRD, (k + 1) * THIRD)
            square = re * re + im * im
            power_sc[:, at] = square if t == 0 else power_sc[:, at] + square
    low, high = power_sc[:PART], power_sc[SPLIT:]
    first = core_ref[...] == 0
    keep_ref[...] = jnp.where(first, low, high).astype(BF16)
    send_ref[...] = jnp.where(first, high, low).astype(BF16)


def gain_kernel(t, row_ref, table_ref, tile_ref, *refs):
    spec_ref, weight_ref, sent_ref = refs[-3:]
    row = row_ref[0:1, 0:1].astype(F32)
    sent_ref[...] = jnp.broadcast_to(row, sent_ref.shape)
    gain, weight_ref[...] = ctf_factors(row, table_ref[...])
    spec_ref[0] = tile_ref[t, 0] * gain
    spec_ref[1] = tile_ref[t, 1] * gain


def library_kernel(first, image_ref, tab_ref, out_ref):
    for i in range(out_ref.shape[0]):
        image = image_ref[:, first + i].reshape(N, N)
        store_spectrum(out_ref.at[i], half_spectrum(image, tab_ref))


def whiten_kernel(
    core_ref, own_ref, own_weight_ref, spec_ref, weight_ref, mine_ref, theirs_ref, *refs
):
    spec_out, weight_out = refs[-2:]
    mine, theirs = mine_ref[...].astype(F32), theirs_ref[...].astype(F32)
    first = core_ref[...] == 0
    low, high = jnp.where(first, mine, theirs), jnp.where(first, theirs, mine)
    power = jnp.concatenate([low[:SPLIT], high], axis=0) * (1.0 / 16.0)
    u, _ = row_numbers()
    mean = jnp.sum(power * row_scale(u)) * (1.0 / (N * N))
    inverse_noise = 1.0 / (jnp.where(u <= HALF, power, 1.0) + 0.05 * mean)
    for t, (spec, weight) in enumerate(((own_ref, own_weight_ref), (spec_ref, weight_ref))):
        spec_out[t, 0] = spec[0] * inverse_noise
        spec_out[t, 1] = spec[1] * inverse_noise
        weight_out[t] = weight[...] * inverse_noise


def match_kernel(t, *refs):
    libs, refs = refs[:4], refs[4:]
    spec_ref, weight_ref, tab_ref, unfold_ref, out_ref, p_sc, h_sc, best_sc = refs
    wide = 2 * THIRD
    count = 4 * libs[0].shape[0]
    s_re, s_im = spec_ref[t, 0], spec_ref[t, 1]
    scales = []
    for j in range(count):
        ref = libs[j % 4]
        re, im = ref[j // 4, 0].astype(F32), ref[j // 4, 1].astype(F32)
        norm = jnp.sum((re * re + im * im) * weight_ref[t])
        scales.append(lax.rsqrt(jnp.full((1, THIRD), norm + 1e-06, F32)))
        p_re = (s_re * re + s_im * im).astype(BF16)
        p_im = (s_im * re - s_re * im).astype(BF16)
        rows = slice(j * FOLD, j * FOLD + ROWS)
        for k in range(3):
            at = slice(k * THIRD, (k + 1) * THIRD)
            p_sc[k, rows, :THIRD] = p_re[:, at]
            p_sc[k, rows, THIRD:] = p_im[:, at]
    g = [dot(p_sc[k], tab_ref[k * wide : (k + 1) * wide, :]) for k in range(3)]
    for j, scale in enumerate(scales):
        rows = slice(j * FOLD, j * FOLD + ROWS)
        (r0, i0), (r1, i1), (r2, i2) = ((x[rows, :THIRD], x[rows, THIRD:]) for x in g)
        slant = scale * ROOT
        rp, rm = r1 + r2, slant * (r1 - r2)
        ip, im_ = i1 + i2, slant * (i1 - i2)
        rh, ih = scale * (r0 - 0.5 * rp), scale * (i0 - 0.5 * ip)
        h_re = (scale * (r0 + rp), rh - im_, rh + im_)
        h_im = (scale * (i0 + ip), ih + rm, ih - rm)
        for k in range(3):
            at = slice(j * N + k * THIRD, j * N + (k + 1) * THIRD)
            h_sc[0, :, at] = h_re[k].astype(BF16)
            h_sc[1, :, at] = h_im[k].astype(BF16)
    first = 3 * wide
    even = dot(tab_ref[first : first + ROWS, :ROWS], h_sc[0])
    odd = dot(tab_ref[first + FOLD : first + FOLD + ROWS, :ROWS], h_sc[1])
    minus, plus = even[:, :N] - odd[:, :N], even[:, :N] + odd[:, :N]
    for j in range(1, count):
        at = slice(j * N, (j + 1) * N)
        minus = jnp.maximum(minus, even[:, at] - odd[:, at])
        plus = jnp.maximum(plus, even[:, at] + odd[:, at])
    best_sc[0] = minus
    best_sc[1] = plus
    out_ref[:HALF] = best_sc[0, :HALF].astype(out_ref.dtype)
    rest = best_sc[...].reshape(2 * ROWS, N)
    total = None
    for _ in range(3 if out_ref.dtype == F32 else 1):
        part = rest.astype(BF16)
        rest = rest - part.astype(F32)
        moved = dot(unfold_ref[...], part)
        total = moved if total is None else total + moved
    out_ref[HALF:] = total.astype(out_ref.dtype)


def full(*shape):
    return pl.BlockSpec(shape, lambda i: (0,) * len(shape))


def cost(flops, size):
    return pl.CostEstimate(flops=flops, bytes_accessed=size, transcendentals=0)


def params(mib):
    return pltpu.CompilerParams(vmem_limit_bytes=mib << 20)


def per_device(images, projections, ctf_row, defocus_term, astig_term, astig_cross, phase_shift):
    ahead, back, unfold = tables()
    groups = math.prod(lax.axis_size(a) for a in DEF)
    places = math.prod(lax.axis_size(a) for a in LIB)
    deep, wide = lax.axis_size("z"), lax.axis_size("xhi")
    core = lax.axis_index("core").astype(jnp.int32).reshape(1, 1)
    swap = [(0, 1), (1, 0)]
    kept = [pl.BlockSpec(memory_space=pltpu.VMEM)]
    plane = (2, ROWS, N)
    work = 2 * ROWS * 768 * 256 * 2

    tile = images[0, 0]
    block = projections[0]
    received = lax.ppermute(tile, "xhi", swap)
    copies = pl.pallas_call(
        copy_kernel,
        out_shape=pltpu.HBM((places,) + block.shape, BF16),
        in_specs=[pl.BlockSpec(memory_space=pltpu.HBM)],
        out_specs=pl.BlockSpec(memory_space=pltpu.HBM),
        scratch_shapes=[
            pltpu.VMEM(block.shape, BF16),
            pltpu.VMEM((groups,) + block.shape, BF16),
            pltpu.SemaphoreType.DMA,
            pltpu.SemaphoreType.DMA((places // groups,)),
        ],
        cost_estimate=cost(0, 1 << 20),
        name="copies",
    )(block)
    images_all = lax.all_to_all(copies, LIB, 0, 0, tiled=False)

    tiles, keep, send = pl.pallas_call(
        tile_kernel,
        out_shape=[
            jax.ShapeDtypeStruct((2,) + plane, F32),
            jax.ShapeDtypeStruct((PART, N), BF16),
            jax.ShapeDtypeStruct((PART, N), BF16),
        ],
        grid=(1,),
        in_specs=[full(1, 1), full(N, N), full(N, N), full(*ahead.shape)],
        out_specs=[full(2, *plane), full(PART, N), full(PART, N)],
        scratch_shapes=[pltpu.VMEM((ROWS, N), F32)],
        compiler_params=params(12),
        cost_estimate=cost(200 * work, 3 << 20),
        name="tile",
    )(core, tile, received, ahead)

    pair = (keep.astype(F32) + lax.ppermute(send, "core", swap).astype(F32)).astype(BF16)
    moves = [
        lax.ppermute(pair, "z", [(z, (z + dz) % deep) for z in range(deep)])
        for dz in range(1, deep)
    ]

    table = jnp.stack([defocus_term, astig_term, astig_cross, phase_shift])
    table = jnp.pad(table, ((0, 4), (0, 128 - table.shape[1])))
    def gain(t, row, tables, name):
        return pl.pallas_call(
            functools.partial(gain_kernel, t),
            out_shape=[
                pltpu.VMEM(plane, F32),
                pltpu.VMEM((ROWS, N), F32),
                pltpu.VMEM((8, 128), F32),
            ],
            in_specs=([full(1, 1)] if t == 0 else kept) + kept * (2 + len(tables)),
            out_specs=kept * 3,
            grid=(1,),
            compiler_params=params(12),
            cost_estimate=cost(8 * work, 3 << 20),
            name=name,
        )(row, table, tiles, *tables)

    *own, sent = gain(0, ctf_row, (ahead, back, unfold), "gain_own")
    mate = lax.ppermute(sent, "xhi", swap)
    images_all, pair, own = lax.optimization_barrier((images_all, pair, own))

    images_all = images_all.reshape(groups, deep, N // groups, N)
    near = [
        pl.pallas_call(
            functools.partial(library_kernel, first),
            out_shape=pltpu.VMEM((deep // 2,) + plane, BF16),
            in_specs=kept * 2,
            out_specs=kept[0],
            compiler_params=params(12),
            cost_estimate=cost(deep // 2 * work * (1 + 5 * first), 3 << 20),
            name="library",
        )(images_all, ahead)
        for first in (0, deep // 2)
    ]
    far = [lax.ppermute(part, "core", swap) for part in near]

    moves, near, mate = lax.optimization_barrier((moves, near, mate))
    *other, _ = gain(1, mate, (), "gain_other")
    mine = sum((m.astype(F32) for m in moves), pair.astype(F32)).astype(BF16)
    theirs = lax.ppermute(mine, "core", swap)
    white, white_weight = pl.pallas_call(
        whiten_kernel,
        out_shape=[
            pltpu.VMEM((2,) + plane, F32),
            pltpu.VMEM((2, ROWS, N), F32),
        ],
        in_specs=kept * 9,
        out_specs=kept * 2,
        compiler_params=params(12),
        cost_estimate=cost(60 * work, 4 << 20),
        name="whiten",
    )(core, *own, *other, mine, theirs, back, unfold)

    def match(t, dtype, name):
        return pl.pallas_call(
            functools.partial(match_kernel, t),
            out_shape=pltpu.VMEM((N, N), dtype),
            in_specs=kept * 8,
            out_specs=kept[0],
            scratch_shapes=[
                pltpu.VMEM((3, 2 * deep * FOLD, 2 * THIRD), BF16),
                pltpu.VMEM((2, ROWS, 2 * deep * N), BF16),
                pltpu.VMEM(plane, F32),
            ],
            compiler_params=params(24),
            cost_estimate=cost(2 * deep * 2 * work, 6 << 20),
            name=name,
        )(*near, *far, white, white_weight, back, unfold)

    got = lax.ppermute(match(1, BF16, "match_other"), "xhi", swap)
    best = match(0, F32, "match_own")
    return jnp.maximum(best, got.astype(F32))[None, None]


def solution(mesh):
    fine = Mesh(mesh.devices.reshape(2, 4, 4, 2, 2), DEF + BLK)
    in_specs = (P(DEF, BLK, None, None), P(BLK, DEF, None), P(DEF, BLK), P(), P(), P(), P())
    out_specs = P(DEF, BLK, None, None)
    return jax.shard_map(
        per_device, mesh=fine, in_specs=in_specs, out_specs=out_specs, check_vma=False
    )
```

```python
import functools
import math

import jax
import jax.numpy as jnp
import ml_dtypes
import numpy as np
from jax import lax
from jax.experimental import pallas as pl
from jax.experimental.pallas import tpu as pltpu
from jax.sharding import Mesh
from jax.sharding import PartitionSpec as P

DEF = ("xlo", "y")
BLK = ("z", "xhi", "core")
LIB = ("xlo", "y", "z")
N = 384
HALF = N // 2
THIRD = N // 3
BLOCKS = (64, 64, 72)
ROWS = sum(BLOCKS)
SPLIT = 96
PART = ROWS - SPLIT
FOLD = 208
ROOT = math.sqrt(3.0) / 2.0
F32 = jnp.float32
BF16 = jnp.bfloat16


def tables():
    j = np.arange(N)
    phase = (j[:, None] * j[None, :]) % N
    cos = np.cos(2.0 * np.pi * phase / N)
    sin = np.sin(2.0 * np.pi * phase / N)
    bf = ml_dtypes.bfloat16
    u = np.concatenate([3 * np.arange(b) + c for c, b in zip((1, 2, 0), BLOCKS)])
    keep = (u <= HALF)[:, None]
    u = np.minimum(u, HALF)
    r = np.arange(THIRD)
    b1, b2 = BLOCKS[0], BLOCKS[0] + BLOCKS[1]
    real = np.concatenate([(keep * cos[u])[b2:, r], (keep * -sin[u])[b2:, r]])
    c1, s1 = cos[u[:b1]][:, r], sin[u[:b1]][:, r]
    c2, s2 = cos[u[b1:b2]][:, r], sin[u[b1:b2]][:, r]
    pair = np.block([[c1, s1], [c2, -s2], [-s1, c1], [-s2, -c2]])
    ahead, back = [], []
    for k in range(3):
        ck = cos[r][:, 3 * r + k]
        sk = sin[r][:, 3 * r + k]
        ahead.append(np.block([[ck, -sk], [sk, ck]]))
        back.append(np.block([[ck.T, sk.T], [-sk.T, ck.T]]))
    ahead, back = np.stack(ahead), np.stack(back)
    weight = np.where((u == 0) | (u == HALF), 1.0, 2.0) * keep[:, 0]
    fold = np.zeros((2, ROWS, ROWS))
    fold[0, : HALF + 1] = cos[: HALF + 1][:, u].astype(bf).astype(float) * weight
    fold[1, : HALF + 1] = sin[: HALF + 1][:, u].astype(bf).astype(float) * weight
    unfold = np.zeros((HALF, 2 * ROWS))
    unfold[0, HALF] = 1.0
    for i in range(1, HALF):
        unfold[i, ROWS + HALF - i] = 1.0
    ahead_all = np.concatenate([ahead.reshape(-1, 2 * THIRD), pair, np.pad(real, ((0, 0), (0, THIRD)))])
    pad = ((0, 0), (0, FOLD - ROWS), (0, 2 * THIRD - ROWS))
    back_all = np.concatenate([back.reshape(-1, 2 * THIRD), np.pad(fold, pad).reshape(-1, 2 * THIRD)])
    return [jnp.asarray(a.astype(bf)) for a in (ahead_all, back_all, unfold)]


def dot(a, b):
    return jnp.dot(a, b, preferred_element_type=F32)


def row_numbers():
    i = lax.broadcasted_iota(jnp.int32, (ROWS, N), 0)
    k = lax.broadcasted_iota(jnp.int32, (ROWS, N), 1)
    b1, b2 = BLOCKS[0], BLOCKS[0] + BLOCKS[1]
    u = jnp.where(i < b1, 3 * i + 1, jnp.where(i < b2, 3 * (i - b1) + 2, 3 * (i - b2)))
    v = jnp.where(
        k < THIRD, 3 * k, jnp.where(k < 2 * THIRD, 3 * (k - THIRD) + 1, 3 * (k - 2 * THIRD) + 2)
    )
    return u, v


def row_scale(u):
    return jnp.where((u > 0) & (u < HALF), 2.0, jnp.where(u <= HALF, 1.0, 0.0))


def copy_kernel(block_in, out_ref, block_ref, wide_sc, sem, sems):
    fetch = pltpu.make_async_copy(block_in, block_ref, sem)
    fetch.start()
    fetch.wait()
    count = wide_sc.shape[0]
    wide_sc[...] = jnp.broadcast_to(block_ref[...][None], wide_sc.shape)
    moves = [
        pltpu.make_async_copy(wide_sc, out_ref.at[pl.ds(i * count, count)], sems.at[i])
        for i in range(out_ref.shape[0] // count)
    ]
    for move in moves:
        move.start()
    for move in moves:
        move.wait()


def sine(x):
    x = x - jnp.round(x)
    a = jnp.abs(x)
    a = jnp.minimum(a, 0.5 - a)
    s = a * a
    p = jnp.full_like(x, -15.0946425768229800)
    for c in (
        42.0586939448600400,
        -76.7058597530613900,
        81.6052492760750400,
        -41.3417022403997600,
        6.28318530717958648,
    ):
        p = p * s + c
    p = p * a
    return jnp.where(x < 0.0, -p, p)


def half_spectrum(image, tab):
    wide = 2 * THIRD
    pair, real = tab[3 * wide : 4 * wide, :], tab[4 * wide :, :THIRD]
    image = image.astype(F32)
    x0, x1, x2 = image[:THIRD], image[THIRD : 2 * THIRD], image[2 * THIRD :]
    plus, minus = x1 + x2, x1 - x2
    f0 = (x0 + plus).astype(BF16)
    f1 = jnp.concatenate([(x0 - 0.5 * plus).astype(BF16), (-ROOT * minus).astype(BF16)], axis=0)
    low = dot(real, f0)
    high = dot(pair, f1)
    b, c = BLOCKS[0] + BLOCKS[1], BLOCKS[2]
    re = jnp.concatenate([high[:b], low[:c]], axis=0)
    im = jnp.concatenate([high[b:], low[c:]], axis=0)
    r0, r1, r2 = re[:, :THIRD], re[:, THIRD : 2 * THIRD], re[:, 2 * THIRD :]
    i0, i1, i2 = im[:, :THIRD], im[:, THIRD : 2 * THIRD], im[:, 2 * THIRD :]
    rp, rm = r1 + r2, ROOT * (r1 - r2)
    ip, im_ = i1 + i2, ROOT * (i1 - i2)
    rh, ih = r0 - 0.5 * rp, i0 - 0.5 * ip
    parts = ((r0 + rp, i0 + ip), (rh + im_, ih - rm), (rh - im_, ih + rm))
    result = []
    for k, (a, b) in enumerate(parts):
        lhs = jnp.concatenate([a.astype(BF16), b.astype(BF16)], axis=1)
        out = dot(lhs, tab[k * wide : (k + 1) * wide, :])
        result.append((out[:, :THIRD], out[:, THIRD:]))
    return result


def store_spectrum(ref, parts):
    for k, (re, im) in enumerate(parts):
        at = slice(k * THIRD, (k + 1) * THIRD)
        ref[0, :, at] = re.astype(ref.dtype)
        ref[1, :, at] = im.astype(ref.dtype)


def ctf_factors(row, table):
    lane = lax.broadcasted_iota(jnp.int32, table.shape, 1).astype(F32)
    chosen = jnp.sum(jnp.where(lane == row, table, 0.0), axis=1, keepdims=True)
    chosen = chosen * (1.0 / (2.0 * math.pi))
    u, v = row_numbers()
    row = jnp.where(u < HALF, u, u - N).astype(F32) * (1.0 / N)
    col = jnp.where(v < HALF, v, v - N).astype(F32) * (1.0 / N)
    r2, c2 = row * row, col * col
    base = chosen[0:1] * (r2 + c2) + chosen[1:2] * (r2 - c2) + chosen[3:4]
    cross = chosen[2:3] * (2.0 * row * col)
    plus = -sine(base + cross)
    at = slice(0, THIRD)
    inner = (u[:, at] > 0) & (u[:, at] < HALF) & (v[:, at] == HALF)
    mirror = jnp.where(inner, -sine(base[:, at] - cross[:, at]), plus[:, at])
    gain = jnp.concatenate([0.5 * (plus[:, at] + mirror), plus[:, THIRD:]], axis=1)
    square = plus * plus
    square = jnp.concatenate(
        [0.5 * (square[:, at] + mirror * mirror), square[:, THIRD:]], axis=1
    )
    return gain, row_scale(u) * square


def tile_kernel(core_ref, own_ref, other_ref, tab_ref, spec_ref, keep_ref, send_ref, power_sc):
    for t, ref in enumerate((own_ref, other_ref)):
        parts = half_spectrum(ref[...], tab_ref)
        store_spectrum(spec_ref.at[t], parts)
        for k, (re, im) in enumerate(parts):
            at = slice(k * THIRD, (k + 1) * THIRD)
            square = re * re + im * im
            power_sc[:, at] = square if t == 0 else power_sc[:, at] + square
    low, high = power_sc[:PART], power_sc[SPLIT:]
    first = core_ref[...] == 0
    keep_ref[...] = jnp.where(first, low, high).astype(BF16)
    send_ref[...] = jnp.where(first, high, low).astype(BF16)


def gain_kernel(t, row_ref, table_ref, tile_ref, *refs):
    spec_ref, weight_ref, sent_ref = refs[-3:]
    row = row_ref[0:1, 0:1].astype(F32)
    sent_ref[...] = jnp.broadcast_to(row, sent_ref.shape)
    gain, weight_ref[...] = ctf_factors(row, table_ref[...])
    spec_ref[0] = tile_ref[t, 0] * gain
    spec_ref[1] = tile_ref[t, 1] * gain


def library_kernel(first, image_ref, tab_ref, out_ref):
    for i in range(out_ref.shape[0]):
        image = image_ref[:, first + i].reshape(N, N)
        store_spectrum(out_ref.at[i], half_spectrum(image, tab_ref))


def whiten_kernel(
    core_ref, own_ref, own_weight_ref, spec_ref, weight_ref, mine_ref, theirs_ref, *refs
):
    spec_out, weight_out = refs[-2:]
    mine, theirs = mine_ref[...].astype(F32), theirs_ref[...].astype(F32)
    first = core_ref[...] == 0
    low, high = jnp.where(first, mine, theirs), jnp.where(first, theirs, mine)
    power = jnp.concatenate([low[:SPLIT], high], axis=0) * (1.0 / 16.0)
    u, _ = row_numbers()
    mean = jnp.sum(power * row_scale(u)) * (1.0 / (N * N))
    inverse_noise = 1.0 / (jnp.where(u <= HALF, power, 1.0) + 0.05 * mean)
    for t, (spec, weight) in enumerate(((own_ref, own_weight_ref), (spec_ref, weight_ref))):
        spec_out[t, 0] = spec[0] * inverse_noise
        spec_out[t, 1] = spec[1] * inverse_noise
        weight_out[t] = weight[...] * inverse_noise


def match_kernel(t, *refs):
    libs, refs = refs[:4], refs[4:]
    spec_ref, weight_ref, tab_ref, unfold_ref, out_ref, p_sc, h_sc, best_sc = refs
    wide = 2 * THIRD
    count = 4 * libs[0].shape[0]
    s_re, s_im = spec_ref[t, 0], spec_ref[t, 1]
    scales = []
    for j in range(count):
        ref = libs[j % 4]
        re, im = ref[j // 4, 0].astype(F32), ref[j // 4, 1].astype(F32)
        norm = jnp.sum((re * re + im * im) * weight_ref[t])
        scales.append(lax.rsqrt(jnp.full((1, THIRD), norm + 1e-06, F32)))
        p_re = (s_re * re + s_im * im).astype(BF16)
        p_im = (s_im * re - s_re * im).astype(BF16)
        rows = slice(j * FOLD, j * FOLD + ROWS)
        for k in range(3):
            at = slice(k * THIRD, (k + 1) * THIRD)
            p_sc[k, rows, :THIRD] = p_re[:, at]
            p_sc[k, rows, THIRD:] = p_im[:, at]
    g = [dot(p_sc[k], tab_ref[k * wide : (k + 1) * wide, :]) for k in range(3)]
    for j, scale in enumerate(scales):
        rows = slice(j * FOLD, j * FOLD + ROWS)
        (r0, i0), (r1, i1), (r2, i2) = ((x[rows, :THIRD], x[rows, THIRD:]) for x in g)
        slant = scale * ROOT
        rp, rm = r1 + r2, slant * (r1 - r2)
        ip, im_ = i1 + i2, slant * (i1 - i2)
        rh, ih = scale * (r0 - 0.5 * rp), scale * (i0 - 0.5 * ip)
        h_re = (scale * (r0 + rp), rh - im_, rh + im_)
        h_im = (scale * (i0 + ip), ih + rm, ih - rm)
        for k in range(3):
            at = slice(j * N + k * THIRD, j * N + (k + 1) * THIRD)
            h_sc[0, :, at] = h_re[k].astype(BF16)
            h_sc[1, :, at] = h_im[k].astype(BF16)
    first = 3 * wide
    even = dot(tab_ref[first : first + ROWS, :ROWS], h_sc[0])
    odd = dot(tab_ref[first + FOLD : first + FOLD + ROWS, :ROWS], h_sc[1])
    minus, plus = even[:, :N] - odd[:, :N], even[:, :N] + odd[:, :N]
    for j in range(1, count):
        at = slice(j * N, (j + 1) * N)
        minus = jnp.maximum(minus, even[:, at] - odd[:, at])
        plus = jnp.maximum(plus, even[:, at] + odd[:, at])
    best_sc[0] = minus
    best_sc[1] = plus
    out_ref[:HALF] = best_sc[0, :HALF].astype(out_ref.dtype)
    rest = best_sc[...].reshape(2 * ROWS, N)
    total = None
    for _ in range(3 if out_ref.dtype == F32 else 1):
        part = rest.astype(BF16)
        rest = rest - part.astype(F32)
        moved = dot(unfold_ref[...], part)
        total = moved if total is None else total + moved
    out_ref[HALF:] = total.astype(out_ref.dtype)


def full(*shape):
    return pl.BlockSpec(shape, lambda i: (0,) * len(shape))


def cost(flops, size):
    return pl.CostEstimate(flops=flops, bytes_accessed=size, transcendentals=0)


def params(mib):
    return pltpu.CompilerParams(vmem_limit_bytes=mib << 20)


def per_device(images, projections, ctf_row, defocus_term, astig_term, astig_cross, phase_shift):
    ahead, back, unfold = tables()
    groups = math.prod(lax.axis_size(a) for a in DEF)
    places = math.prod(lax.axis_size(a) for a in LIB)
    deep, wide = lax.axis_size("z"), lax.axis_size("xhi")
    core = lax.axis_index("core").astype(jnp.int32).reshape(1, 1)
    swap = [(0, 1), (1, 0)]
    kept = [pl.BlockSpec(memory_space=pltpu.VMEM)]
    plane = (2, ROWS, N)
    work = 2 * ROWS * 768 * 256 * 2

    tile = images[0, 0]
    block = projections[0]
    received = lax.ppermute(tile, "xhi", swap)
    copies = pl.pallas_call(
        copy_kernel,
        out_shape=pltpu.HBM((places,) + block.shape, BF16),
        in_specs=[pl.BlockSpec(memory_space=pltpu.HBM)],
        out_specs=pl.BlockSpec(memory_space=pltpu.HBM),
        scratch_shapes=[
            pltpu.VMEM(block.shape, BF16),
            pltpu.VMEM((groups,) + block.shape, BF16),
            pltpu.SemaphoreType.DMA,
            pltpu.SemaphoreType.DMA((places // groups,)),
        ],
        cost_estimate=cost(0, 1 << 20),
        name="copies",
    )(block)
    images_all = lax.all_to_all(copies, LIB, 0, 0, tiled=False)

    tiles, keep, send = pl.pallas_call(
        tile_kernel,
        out_shape=[
            jax.ShapeDtypeStruct((2,) + plane, F32),
            jax.ShapeDtypeStruct((PART, N), BF16),
            jax.ShapeDtypeStruct((PART, N), BF16),
        ],
        grid=(1,),
        in_specs=[full(1, 1), full(N, N), full(N, N), full(*ahead.shape)],
        out_specs=[full(2, *plane), full(PART, N), full(PART, N)],
        scratch_shapes=[pltpu.VMEM((ROWS, N), F32)],
        compiler_params=params(12),
        cost_estimate=cost(200 * work, 3 << 20),
        name="tile",
    )(core, tile, received, ahead)

    pair = (keep.astype(F32) + lax.ppermute(send, "core", swap).astype(F32)).astype(BF16)
    moves = [
        lax.ppermute(pair, "z", [(z, (z + dz) % deep) for z in range(deep)])
        for dz in range(1, deep)
    ]

    table = jnp.stack([defocus_term, astig_term, astig_cross, phase_shift])
    table = jnp.pad(table, ((0, 4), (0, 128 - table.shape[1])))
    def gain(t, row, tables, name):
        return pl.pallas_call(
            functools.partial(gain_kernel, t),
            out_shape=[
                pltpu.VMEM(plane, F32),
                pltpu.VMEM((ROWS, N), F32),
                pltpu.VMEM((8, 128), F32),
            ],
            in_specs=([full(1, 1)] if t == 0 else kept) + kept * (2 + len(tables)),
            out_specs=kept * 3,
            grid=(1,),
            compiler_params=params(12),
            cost_estimate=cost(8 * work, 3 << 20),
            name=name,
        )(row, table, tiles, *tables)

    *own, sent = gain(0, ctf_row, (ahead, back, unfold), "gain_own")
    mate = lax.ppermute(sent, "xhi", swap)
    images_all, pair, own = lax.optimization_barrier((images_all, pair, own))

    images_all = images_all.reshape(groups, deep, N // groups, N)
    held, mate = lax.optimization_barrier((images_all, mate))
    near = [
        pl.pallas_call(
            functools.partial(library_kernel, first),
            out_shape=pltpu.VMEM((deep // 2,) + plane, BF16),
            in_specs=kept * 2,
            out_specs=kept[0],
            compiler_params=params(12),
            cost_estimate=cost(deep // 2 * work, 3 << 20),
            name="library",
        )(held if first else images_all, ahead)
        for first in (0, deep // 2)
    ]
    far = [lax.ppermute(part, "core", swap) for part in near]

    moves, near, mate = lax.optimization_barrier((moves, near, mate))
    *other, _ = gain(1, mate, (), "gain_other")
    mine = sum((m.astype(F32) for m in moves), pair.astype(F32)).astype(BF16)
    theirs = lax.ppermute(mine, "core", swap)
    white, white_weight = pl.pallas_call(
        whiten_kernel,
        out_shape=[
            pltpu.VMEM((2,) + plane, F32),
            pltpu.VMEM((2, ROWS, N), F32),
        ],
        in_specs=kept * 9,
        out_specs=kept * 2,
        compiler_params=params(12),
        cost_estimate=cost(60 * work, 4 << 20),
        name="whiten",
    )(core, *own, *other, mine, theirs, back, unfold)

    def match(t, dtype, name):
        return pl.pallas_call(
            functools.partial(match_kernel, t),
            out_shape=pltpu.VMEM((N, N), dtype),
            in_specs=kept * 8,
            out_specs=kept[0],
            scratch_shapes=[
                pltpu.VMEM((3, 2 * deep * FOLD, 2 * THIRD), BF16),
                pltpu.VMEM((2, ROWS, 2 * deep * N), BF16),
                pltpu.VMEM(plane, F32),
            ],
            compiler_params=params(24),
            cost_estimate=cost(2 * deep * 2 * work, 6 << 20),
            name=name,
        )(*near, *far, white, white_weight, back, unfold)

    got = lax.ppermute(match(1, BF16, "match_other"), "xhi", swap)
    best = match(0, F32, "match_own")
    return jnp.maximum(best, got.astype(F32))[None, None]


def solution(mesh):
    fine = Mesh(mesh.devices.reshape(2, 4, 4, 2, 2), DEF + BLK)
    in_specs = (P(DEF, BLK, None, None), P(BLK, DEF, None), P(DEF, BLK), P(), P(), P(), P())
    out_specs = P(DEF, BLK, None, None)
    return jax.shard_map(
        per_device, mesh=fine, in_specs=in_specs, out_specs=out_specs, check_vma=False
    )
```

```python
import functools
import math

import jax
import jax.numpy as jnp
import ml_dtypes
import numpy as np
from jax import lax
from jax.experimental import pallas as pl
from jax.experimental.pallas import tpu as pltpu
from jax.sharding import Mesh
from jax.sharding import PartitionSpec as P

DEF = ("xlo", "y")
BLK = ("z", "xhi", "core")
LIB = ("xlo", "y", "z")
N = 384
HALF = N // 2
THIRD = N // 3
BLOCKS = (64, 64, 72)
ROWS = sum(BLOCKS)
SPLIT = 96
PART = ROWS - SPLIT
FOLD = 208
ROOT = math.sqrt(3.0) / 2.0
F32 = jnp.float32
BF16 = jnp.bfloat16


def tables():
    j = np.arange(N)
    phase = (j[:, None] * j[None, :]) % N
    cos = np.cos(2.0 * np.pi * phase / N)
    sin = np.sin(2.0 * np.pi * phase / N)
    bf = ml_dtypes.bfloat16
    u = np.concatenate([3 * np.arange(b) + c for c, b in zip((1, 2, 0), BLOCKS)])
    keep = (u <= HALF)[:, None]
    u = np.minimum(u, HALF)
    r = np.arange(THIRD)
    b1, b2 = BLOCKS[0], BLOCKS[0] + BLOCKS[1]
    real = np.concatenate([(keep * cos[u])[b2:, r], (keep * -sin[u])[b2:, r]])
    c1, s1 = cos[u[:b1]][:, r], sin[u[:b1]][:, r]
    c2, s2 = cos[u[b1:b2]][:, r], sin[u[b1:b2]][:, r]
    pair = np.block([[c1, s1], [c2, -s2], [-s1, c1], [-s2, -c2]])
    ahead, back = [], []
    for k in range(3):
        ck = cos[r][:, 3 * r + k]
        sk = sin[r][:, 3 * r + k]
        ahead.append(np.block([[ck, -sk], [sk, ck]]))
        back.append(np.block([[ck.T, sk.T], [-sk.T, ck.T]]))
    ahead, back = np.stack(ahead), np.stack(back)
    weight = np.where((u == 0) | (u == HALF), 1.0, 2.0) * keep[:, 0]
    fold = np.zeros((2, ROWS, ROWS))
    fold[0, : HALF + 1] = cos[: HALF + 1][:, u].astype(bf).astype(float) * weight
    fold[1, : HALF + 1] = sin[: HALF + 1][:, u].astype(bf).astype(float) * weight
    unfold = np.zeros((HALF, 2 * ROWS))
    unfold[0, HALF] = 1.0
    for i in range(1, HALF):
        unfold[i, ROWS + HALF - i] = 1.0
    ahead_all = np.concatenate([ahead.reshape(-1, 2 * THIRD), pair, np.pad(real, ((0, 0), (0, THIRD)))])
    pad = ((0, 0), (0, FOLD - ROWS), (0, 2 * THIRD - ROWS))
    back_all = np.concatenate([back.reshape(-1, 2 * THIRD), np.pad(fold, pad).reshape(-1, 2 * THIRD)])
    return [jnp.asarray(a.astype(bf)) for a in (ahead_all, back_all, unfold)]


def dot(a, b):
    return jnp.dot(a, b, preferred_element_type=F32)


def row_numbers():
    i = lax.broadcasted_iota(jnp.int32, (ROWS, N), 0)
    k = lax.broadcasted_iota(jnp.int32, (ROWS, N), 1)
    b1, b2 = BLOCKS[0], BLOCKS[0] + BLOCKS[1]
    u = jnp.where(i < b1, 3 * i + 1, jnp.where(i < b2, 3 * (i - b1) + 2, 3 * (i - b2)))
    v = jnp.where(
        k < THIRD, 3 * k, jnp.where(k < 2 * THIRD, 3 * (k - THIRD) + 1, 3 * (k - 2 * THIRD) + 2)
    )
    return u, v


def row_scale(u):
    return jnp.where((u > 0) & (u < HALF), 2.0, jnp.where(u <= HALF, 1.0, 0.0))


def copy_kernel(block_in, out_ref, block_ref, wide_sc, sem, sems):
    fetch = pltpu.make_async_copy(block_in, block_ref, sem)
    fetch.start()
    fetch.wait()
    count = wide_sc.shape[0]
    wide_sc[...] = jnp.broadcast_to(block_ref[...][None], wide_sc.shape)
    moves = [
        pltpu.make_async_copy(wide_sc, out_ref.at[pl.ds(i * count, count)], sems.at[i])
        for i in range(out_ref.shape[0] // count)
    ]
    for move in moves:
        move.start()
    for move in moves:
        move.wait()


def sine(x):
    x = x - jnp.round(x)
    a = jnp.abs(x)
    a = jnp.minimum(a, 0.5 - a)
    s = a * a
    p = jnp.full_like(x, -15.0946425768229800)
    for c in (
        42.0586939448600400,
        -76.7058597530613900,
        81.6052492760750400,
        -41.3417022403997600,
        6.28318530717958648,
    ):
        p = p * s + c
    p = p * a
    return jnp.where(x < 0.0, -p, p)


def half_spectrum(image, tab):
    wide = 2 * THIRD
    pair, real = tab[3 * wide : 4 * wide, :], tab[4 * wide :, :THIRD]
    image = image.astype(F32)
    x0, x1, x2 = image[:THIRD], image[THIRD : 2 * THIRD], image[2 * THIRD :]
    plus, minus = x1 + x2, x1 - x2
    f0 = (x0 + plus).astype(BF16)
    f1 = jnp.concatenate([(x0 - 0.5 * plus).astype(BF16), (-ROOT * minus).astype(BF16)], axis=0)
    low = dot(real, f0)
    high = dot(pair, f1)
    b, c = BLOCKS[0] + BLOCKS[1], BLOCKS[2]
    re = jnp.concatenate([high[:b], low[:c]], axis=0)
    im = jnp.concatenate([high[b:], low[c:]], axis=0)
    r0, r1, r2 = re[:, :THIRD], re[:, THIRD : 2 * THIRD], re[:, 2 * THIRD :]
    i0, i1, i2 = im[:, :THIRD], im[:, THIRD : 2 * THIRD], im[:, 2 * THIRD :]
    rp, rm = r1 + r2, ROOT * (r1 - r2)
    ip, im_ = i1 + i2, ROOT * (i1 - i2)
    rh, ih = r0 - 0.5 * rp, i0 - 0.5 * ip
    parts = ((r0 + rp, i0 + ip), (rh + im_, ih - rm), (rh - im_, ih + rm))
    result = []
    for k, (a, b) in enumerate(parts):
        lhs = jnp.concatenate([a.astype(BF16), b.astype(BF16)], axis=1)
        out = dot(lhs, tab[k * wide : (k + 1) * wide, :])
        result.append((out[:, :THIRD], out[:, THIRD:]))
    return result


def store_spectrum(ref, parts):
    for k, (re, im) in enumerate(parts):
        at = slice(k * THIRD, (k + 1) * THIRD)
        ref[0, :, at] = re.astype(ref.dtype)
        ref[1, :, at] = im.astype(ref.dtype)


def ctf_factors(row, table):
    lane = lax.broadcasted_iota(jnp.int32, table.shape, 1).astype(F32)
    chosen = jnp.sum(jnp.where(lane == row, table, 0.0), axis=1, keepdims=True)
    chosen = chosen * (1.0 / (2.0 * math.pi))
    u, v = row_numbers()
    row = jnp.where(u < HALF, u, u - N).astype(F32) * (1.0 / N)
    col = jnp.where(v < HALF, v, v - N).astype(F32) * (1.0 / N)
    r2, c2 = row * row, col * col
    base = chosen[0:1] * (r2 + c2) + chosen[1:2] * (r2 - c2) + chosen[3:4]
    cross = chosen[2:3] * (2.0 * row * col)
    plus = -sine(base + cross)
    at = slice(0, THIRD)
    inner = (u[:, at] > 0) & (u[:, at] < HALF) & (v[:, at] == HALF)
    mirror = jnp.where(inner, -sine(base[:, at] - cross[:, at]), plus[:, at])
    gain = jnp.concatenate([0.5 * (plus[:, at] + mirror), plus[:, THIRD:]], axis=1)
    square = plus * plus
    square = jnp.concatenate(
        [0.5 * (square[:, at] + mirror * mirror), square[:, THIRD:]], axis=1
    )
    return gain, row_scale(u) * square


def tile_kernel(core_ref, own_ref, other_ref, tab_ref, spec_ref, keep_ref, send_ref, power_sc):
    for t, ref in enumerate((own_ref, other_ref)):
        parts = half_spectrum(ref[...], tab_ref)
        store_spectrum(spec_ref.at[t], parts)
        for k, (re, im) in enumerate(parts):
            at = slice(k * THIRD, (k + 1) * THIRD)
            square = re * re + im * im
            power_sc[:, at] = square if t == 0 else power_sc[:, at] + square
    low, high = power_sc[:PART], power_sc[SPLIT:]
    first = core_ref[...] == 0
    keep_ref[...] = jnp.where(first, low, high).astype(BF16)
    send_ref[...] = jnp.where(first, high, low).astype(BF16)


def gain_kernel(t, row_ref, table_ref, tile_ref, *refs):
    spec_ref, weight_ref, sent_ref = refs[-3:]
    row = row_ref[0:1, 0:1].astype(F32)
    sent_ref[...] = jnp.broadcast_to(row, sent_ref.shape)
    gain, weight_ref[...] = ctf_factors(row, table_ref[...])
    spec_ref[0] = tile_ref[t, 0] * gain
    spec_ref[1] = tile_ref[t, 1] * gain


def library_kernel(first, image_ref, tab_ref, out_ref):
    for i in range(out_ref.shape[0]):
        image = image_ref[:, first + i].reshape(N, N)
        store_spectrum(out_ref.at[i], half_spectrum(image, tab_ref))


def whiten_kernel(
    core_ref, own_ref, own_weight_ref, spec_ref, weight_ref, mine_ref, theirs_ref, *refs
):
    spec_out, weight_out = refs[-2:]
    mine, theirs = mine_ref[...].astype(F32), theirs_ref[...].astype(F32)
    first = core_ref[...] == 0
    low, high = jnp.where(first, mine, theirs), jnp.where(first, theirs, mine)
    power = jnp.concatenate([low[:SPLIT], high], axis=0) * (1.0 / 16.0)
    u, _ = row_numbers()
    mean = jnp.sum(power * row_scale(u)) * (1.0 / (N * N))
    inverse_noise = 1.0 / (jnp.where(u <= HALF, power, 1.0) + 0.05 * mean)
    for t, (spec, weight) in enumerate(((own_ref, own_weight_ref), (spec_ref, weight_ref))):
        spec_out[t, 0] = spec[0] * inverse_noise
        spec_out[t, 1] = spec[1] * inverse_noise
        weight_out[t] = weight[...] * inverse_noise


def match_kernel(t, *refs):
    libs, refs = refs[:4], refs[4:]
    spec_ref, weight_ref, tab_ref, unfold_ref, out_ref, p_sc, h_sc, best_sc = refs
    wide = 2 * THIRD
    count = 4 * libs[0].shape[0]
    s_re, s_im = spec_ref[t, 0], spec_ref[t, 1]
    scales = []
    for j in range(count):
        ref = libs[j % 4]
        re, im = ref[j // 4, 0].astype(F32), ref[j // 4, 1].astype(F32)
        norm = jnp.sum((re * re + im * im) * weight_ref[t])
        scales.append(lax.rsqrt(jnp.full((1, THIRD), norm + 1e-06, F32)))
        p_re = (s_re * re + s_im * im).astype(BF16)
        p_im = (s_im * re - s_re * im).astype(BF16)
        rows = slice(j * FOLD, j * FOLD + ROWS)
        for k in range(3):
            at = slice(k * THIRD, (k + 1) * THIRD)
            p_sc[k, rows, :THIRD] = p_re[:, at]
            p_sc[k, rows, THIRD:] = p_im[:, at]
    g = [dot(p_sc[k], tab_ref[k * wide : (k + 1) * wide, :]) for k in range(3)]
    for j, scale in enumerate(scales):
        rows = slice(j * FOLD, j * FOLD + ROWS)
        (r0, i0), (r1, i1), (r2, i2) = ((x[rows, :THIRD], x[rows, THIRD:]) for x in g)
        slant = scale * ROOT
        rp, rm = r1 + r2, slant * (r1 - r2)
        ip, im_ = i1 + i2, slant * (i1 - i2)
        rh, ih = scale * (r0 - 0.5 * rp), scale * (i0 - 0.5 * ip)
        h_re = (scale * (r0 + rp), rh - im_, rh + im_)
        h_im = (scale * (i0 + ip), ih + rm, ih - rm)
        for k in range(3):
            at = slice(j * N + k * THIRD, j * N + (k + 1) * THIRD)
            h_sc[0, :, at] = h_re[k].astype(BF16)
            h_sc[1, :, at] = h_im[k].astype(BF16)
    first = 3 * wide
    even = dot(tab_ref[first : first + ROWS, :ROWS], h_sc[0])
    odd = dot(tab_ref[first + FOLD : first + FOLD + ROWS, :ROWS], h_sc[1])
    minus, plus = even[:, :N] - odd[:, :N], even[:, :N] + odd[:, :N]
    for j in range(1, count):
        at = slice(j * N, (j + 1) * N)
        minus = jnp.maximum(minus, even[:, at] - odd[:, at])
        plus = jnp.maximum(plus, even[:, at] + odd[:, at])
    best_sc[0] = minus
    best_sc[1] = plus
    out_ref[:HALF] = best_sc[0, :HALF].astype(out_ref.dtype)
    rest = best_sc[...].reshape(2 * ROWS, N)
    total = None
    for _ in range(3 if out_ref.dtype == F32 else 1):
        part = rest.astype(BF16)
        rest = rest - part.astype(F32)
        moved = dot(unfold_ref[...], part)
        total = moved if total is None else total + moved
    out_ref[HALF:] = total.astype(out_ref.dtype)


def full(*shape):
    return pl.BlockSpec(shape, lambda i: (0,) * len(shape))


def cost(flops, size):
    return pl.CostEstimate(flops=flops, bytes_accessed=size, transcendentals=0)


def params(mib):
    return pltpu.CompilerParams(vmem_limit_bytes=mib << 20)


def per_device(images, projections, ctf_row, defocus_term, astig_term, astig_cross, phase_shift):
    ahead, back, unfold = tables()
    groups = math.prod(lax.axis_size(a) for a in DEF)
    places = math.prod(lax.axis_size(a) for a in LIB)
    deep, wide = lax.axis_size("z"), lax.axis_size("xhi")
    core = lax.axis_index("core").astype(jnp.int32).reshape(1, 1)
    swap = [(0, 1), (1, 0)]
    kept = [pl.BlockSpec(memory_space=pltpu.VMEM)]
    plane = (2, ROWS, N)
    work = 2 * ROWS * 768 * 256 * 2

    tile = images[0, 0]
    block = projections[0]
    received = lax.ppermute(tile, "xhi", swap)
    copies = pl.pallas_call(
        copy_kernel,
        out_shape=pltpu.HBM((places,) + block.shape, BF16),
        in_specs=[pl.BlockSpec(memory_space=pltpu.HBM)],
        out_specs=pl.BlockSpec(memory_space=pltpu.HBM),
        scratch_shapes=[
            pltpu.VMEM(block.shape, BF16),
            pltpu.VMEM((groups,) + block.shape, BF16),
            pltpu.SemaphoreType.DMA,
            pltpu.SemaphoreType.DMA((places // groups,)),
        ],
        cost_estimate=cost(0, 1 << 20),
        name="copies",
    )(block)
    images_all = lax.all_to_all(copies, LIB, 0, 0, tiled=False)

    tiles, keep, send = pl.pallas_call(
        tile_kernel,
        out_shape=[
            jax.ShapeDtypeStruct((2,) + plane, F32),
            jax.ShapeDtypeStruct((PART, N), BF16),
            jax.ShapeDtypeStruct((PART, N), BF16),
        ],
        grid=(1,),
        in_specs=[full(1, 1), full(N, N), full(N, N), full(*ahead.shape)],
        out_specs=[full(2, *plane), full(PART, N), full(PART, N)],
        scratch_shapes=[pltpu.VMEM((ROWS, N), F32)],
        compiler_params=params(12),
        cost_estimate=cost(200 * work, 3 << 20),
        name="tile",
    )(core, tile, received, ahead)

    pair = (keep.astype(F32) + lax.ppermute(send, "core", swap).astype(F32)).astype(BF16)
    moves = [
        lax.ppermute(pair, "z", [(z, (z + dz) % deep) for z in range(deep)])
        for dz in range(1, deep)
    ]

    table = jnp.stack([defocus_term, astig_term, astig_cross, phase_shift])
    table = jnp.pad(table, ((0, 4), (0, 128 - table.shape[1])))
    def gain(t, row, tables, name):
        return pl.pallas_call(
            functools.partial(gain_kernel, t),
            out_shape=[
                pltpu.VMEM(plane, F32),
                pltpu.VMEM((ROWS, N), F32),
                pltpu.VMEM((8, 128), F32),
            ],
            in_specs=([full(1, 1)] if t == 0 else kept) + kept * (2 + len(tables)),
            out_specs=kept * 3,
            grid=(1,),
            compiler_params=params(12),
            cost_estimate=cost(8 * work, 3 << 20),
            name=name,
        )(row, table, tiles, *tables)

    *own, sent = gain(0, ctf_row, (ahead, back, unfold), "gain_own")
    mate = lax.ppermute(sent, "xhi", swap)
    images_all, pair, own = lax.optimization_barrier((images_all, pair, own))

    images_all = images_all.reshape(groups, deep, N // groups, N)
    near = [
        pl.pallas_call(
            functools.partial(library_kernel, first),
            out_shape=pltpu.VMEM((deep // 2,) + plane, BF16),
            in_specs=kept * 2,
            out_specs=kept[0],
            compiler_params=params(12),
            cost_estimate=cost(deep // 2 * work, 3 << 20),
            name="library",
        )(images_all, ahead)
        for first in (0, deep // 2)
    ]
    far = [lax.ppermute(part, "core", swap) for part in near]

    moves, near, mate = lax.optimization_barrier((moves, near, mate))
    *other, _ = gain(1, mate, (), "gain_other")
    mine = sum((m.astype(F32) for m in moves), pair.astype(F32)).astype(BF16)
    theirs = lax.ppermute(mine, "core", swap)
    white, white_weight = pl.pallas_call(
        whiten_kernel,
        out_shape=[
            pltpu.VMEM((2,) + plane, F32),
            pltpu.VMEM((2, ROWS, N), F32),
        ],
        in_specs=kept * 9,
        out_specs=kept * 2,
        compiler_params=params(12),
        cost_estimate=cost(60 * work, 4 << 20),
        name="whiten",
    )(core, *own, *other, mine, theirs, back, unfold)

    def match(t, dtype, name):
        return pl.pallas_call(
            functools.partial(match_kernel, t),
            out_shape=pltpu.VMEM((N, N), dtype),
            in_specs=kept * 8,
            out_specs=kept[0],
            scratch_shapes=[
                pltpu.VMEM((3, 2 * deep * FOLD, 2 * THIRD), BF16),
                pltpu.VMEM((2, ROWS, 2 * deep * N), BF16),
                pltpu.VMEM(plane, F32),
            ],
            compiler_params=params(24),
            cost_estimate=cost(2 * deep * 2 * work, 6 << 20),
            name=name,
        )(*near, *far, white, white_weight, back, unfold)

    got = lax.ppermute(match(1, BF16, "match_other"), "xhi", swap)
    best = match(0, F32, "match_own")
    return jnp.maximum(best, got.astype(F32))[None, None]


def solution(mesh):
    fine = Mesh(mesh.devices.reshape(2, 4, 4, 2, 2), DEF + BLK)
    in_specs = (P(DEF, BLK, None, None), P(BLK, DEF, None), P(DEF, BLK), P(), P(), P(), P())
    out_specs = P(DEF, BLK, None, None)
    return jax.shard_map(
        per_device, mesh=fine, in_specs=in_specs, out_specs=out_specs, check_vma=False
    )
```
